32 devices in a mesh: dp: 4 (over x, core), fsdp: 8 (over z, y).
Axes of the slice: x: 2, y: 2, z: 4, core: 2. Of those that a mesh axis runs over, the one named last changes fastest.
Arguments:
- tokens: bfloat16 [2, 4, 2048, 1152], P(None, 'dp', 'fsdp'), may hold values from -6 to 6
- cotangent: bfloat16 [2, 4, 2048, 1152], P(None, 'dp', 'fsdp'), may hold values from -6 to 6
- lengths: int32 [2, 4, 8], P(None, 'dp'), may hold values from 1 to 128, 768 in all within a row
- master: float32 [1152, 23296], P('fsdp'), may hold values from -0.1875 to 0.1875
- gains: float32 [5120], replicated, may hold values from 0.5 to 1.5
- gain_stats: float32 [5120], replicated, may hold values from 1024 to 65536
- owner: int32 [1456, 1], P('fsdp'), may hold values from 0 to 3; in each aligned block of 182 rows (0 to 181, 182 to 363, ...) at most 57 rows name the same one
- stat_left: float32 [8, 228, 144, 144], P('fsdp', 'dp'), may hold values from -3145728 to 3145728
- stat_right: float32 [8, 228, 128, 128], P('fsdp', 'dp'), may hold values from -3670016 to 3670016
- root_left: bfloat16 [8, 228, 144, 144], P('fsdp', 'dp')
- root_right: bfloat16 [8, 228, 128, 128], P('fsdp', 'dp')
Outputs:
- output: bfloat16 [2, 4, 2048, 1152], P(None, 'dp', 'fsdp')
- input_grad: bfloat16 [2, 4, 2048, 1152], P(None, 'dp', 'fsdp')
- weight_grad: float32 [8, 228, 144, 128], P('fsdp', 'dp')
- gain_grad: float32 [5120], replicated
- new_left: float32 [8, 228, 144, 144], P('fsdp', 'dp')
- new_right: float32 [8, 228, 128, 128], P('fsdp', 'dp')
- new_master: float32 [1152, 23296], P('fsdp')
- new_weights: bfloat16 [1152, 23296], P('fsdp')
- new_gain_stats: float32 [5120], replicated
- gain_change: float32 [5120], replicated
The draws below stay inside these ranges and needn't reach their ends.
Inputs may be any that keep to these rules, and one draw needn't show every extreme that they name: `lengths`: each row lists the used slots of the 8 continuations of one group; a row sums to 768 and holds at least one 128. `owner`: entry j * 182 + b names the dp index that owns block b of row band j; among one band's 182 entries no index appears more than 57 times.
All inputs are finite; a program needn't handle non-finite values.
Results may differ from the reference program's by a relative error of at most 0.02.
The reference program's roundings to bfloat16 on the way count: a program that leaves them out, or rounds other values in their place, can miss the bound.
Values may be sent and summed in bfloat16 or wider, within the bound.
No kernel may reach another device: no remote copies, remote signals or barrier semaphores. Data moves between devices by JAX's collectives and lax.ppermute only.
A program may use at most 448 MiB of HBM per device.

```python
import math
import jax
import jax.numpy as jnp
import numpy as np
from jax import lax

D = 1152
HEADS = 4
HD = 256
FF = 6912
WIN = 512
PROMPT = 1024
CONT = 8
CLEN = 128
MB = 2
GROUPS = 1
BC = 128
GLEN = 2048
RS = 144
QKVW = 1536
NCOL = 23296
NBLK = 182
CAP = 57
NGAIN = 5120
TOKENS = 16384
N_DP = 4
N_FSDP = 8


def near_identity(key, lead, order):
    noise = jax.random.uniform(key, lead + (order, order), jnp.float32, -1.0, 1.0)
    return jnp.eye(order, dtype=jnp.float32) + noise * (0.8 / math.sqrt(order))


def draw_root_left(key, part):
    return near_identity(jax.random.fold_in(key, 11), (N_FSDP, N_DP * CAP), RS).astype(jnp.bfloat16)


def draw_root_right(key, part):
    return near_identity(jax.random.fold_in(key, 23), (N_FSDP, N_DP * CAP), BC).astype(jnp.bfloat16)


def level_of(own_key, shape, shards, low, high):
    level = 1.0
    for dim, blocks in shards:
        steps = jax.random.uniform(jax.random.fold_in(jax.random.fold_in(own_key, 6), dim), (blocks,), jnp.float32, low / len(shards), high / len(shards))
        level = level * jnp.repeat(jnp.exp(steps), shape[dim] // blocks).reshape((-1,) + (1,) * (len(shape) - 1 - dim))
    return level


def split_up(number_of, total, limit, skew):
    portions = [(1 << 20) // math.isqrt(rank ** skew) + 1 for rank in range(2, number_of + 1)]
    spare, given = total - limit - (number_of - 1), [1] * (number_of - 1)
    while spare > 0:
        movable = [i for i in range(number_of - 1) if given[i] < limit]
        pool, budget = sum([portions[i] for i in movable]), spare
        for i in movable:
            addition = min(limit - given[i], max(1, budget * portions[i] // pool), spare)
            given[i] = given[i] + addition
            spare = spare - addition
    return np.array([limit] + given)


def ragged_sizes(key, count, total, bound, lean):
    if count == 2:
        one = jax.random.randint(key, (), max(1, total - bound), min(bound, total - 1) + 1)
        return jnp.stack([one, total - one])
    sizes = jnp.asarray(split_up(count, total, bound, lean), jnp.int32)
    twos = (count - 1) // 2
    giver, taker = sizes[1:1 + 2 * twos:2], sizes[2:2 + 2 * twos:2]
    room = jnp.minimum(giver - 1, bound - taker)
    shifted = jax.random.randint(jax.random.fold_in(key, 1), (twos,), 0, 1 << 20) % (room + 1)
    sizes = sizes.at[1:1 + 2 * twos:2].set(giver - shifted).at[2:2 + 2 * twos:2].set(taker + shifted)
    return sizes[jax.random.permutation(jax.random.fold_in(key, 2), count)]


def routed_block(stream_key, own, number, rows, amount, top, reach, lean):
    order = jax.random.permutation(stream_key, amount)
    heavy_load, usual = load_shares(amount, rows * top, reach, lean, True), load_shares(amount, rows * top, reach, lean, False)
    places = jnp.arange(amount)

    def named(sizes, rotation):
        used = int((sizes > 0).sum())
        fixed = max(1, used // 4)
        shifted = fixed + (places - fixed + rotation * (used - fixed)) % max(1, amount - fixed)
        return jnp.zeros((amount,), jnp.int32).at[order[jnp.where(places < fixed, places, shifted)]].set(jnp.asarray(sizes, jnp.int32))

    sizes = jnp.where(number % 4 == 0, named(heavy_load, number // 4), named(usual, number - number // 4 - 1))
    mixed = jax.random.permutation(jax.random.fold_in(own, 3), amount)
    donor, taker = mixed[0:amount // 2 * 2:2], mixed[1:amount // 2 * 2:2]
    margin = jnp.minimum(sizes[donor] - 1, reach - sizes[taker]) // 2
    margin = jnp.where((donor == order[0]) | (taker == order[0]) | (sizes[taker] == 0), 0, jnp.maximum(margin, 0))
    shifted = jax.random.randint(jax.random.fold_in(own, 4), (amount // 2,), 0, 1 << 20) % (margin + 1)
    sizes = sizes.at[donor].add(-shifted).at[taker].add(shifted)
    labels = jnp.searchsorted(jnp.cumsum(sizes), jnp.arange(rows * top), side="right").astype(jnp.int32)
    listing = labels.reshape(top, rows).T
    listing = listing[jax.random.permutation(jax.random.fold_in(own, 1), rows)]
    rotation = jax.random.randint(jax.random.fold_in(own, 2), (rows, 1), 0, top)
    return jnp.take_along_axis(listing, (jnp.arange(top)[None, :] + rotation) % top, axis=1)


def load_shares(number_of, total, reach, slope, full):
    loads = [(1 << 20) // math.isqrt(standing ** slope) + 1 for standing in range(1, number_of + 1)]
    largest = reach if full else min(reach, max(-(-total // number_of), total * loads[0] // sum(loads)))
    least = 1 if total - largest >= number_of - 1 else 0
    holding, spare = [largest] + [least] * (number_of - 1), total - largest - least * (number_of - 1)
    while spare > 0:
        candidates = [i for i in range(1, number_of) if holding[i] < largest] or [i for i in range(1, number_of) if holding[i] < reach]
        whole, budget = sum([loads[i] for i in candidates]), spare
        for i in candidates:
            addition = min(reach - holding[i], max(1, budget * loads[i] // whole), spare)
            holding[i] = holding[i] + addition
            spare = spare - addition
    return np.array(holding)


def scatter_about(key, extent, spread, most, pieces=(), held_as=jnp.bfloat16):
    factor_of = level_of(key, extent, pieces, -0.22, 0.18) if pieces else 1.0
    array = jax.random.normal(key, extent, jnp.float32) * spread * factor_of
    return jnp.minimum(jnp.maximum(array, -most), most).astype(held_as)


def setup_inputs(seed: int = 0) -> dict:
    key_list = jax.random.split(jax.random.key(seed), 12)
    tokens = scatter_about(key_list[0], (MB, N_DP * GROUPS, GLEN, D), 1.0, 6.0, ((1, 4), (2, 8)))
    cotangent = scatter_about(key_list[1], (MB, N_DP * GROUPS, GLEN, D), 1.0, 6.0, ((1, 4), (2, 8)))
    lengths = jax.vmap(lambda own: ragged_sizes(own, CONT, 3 * CONT * CLEN // 4, CLEN, 1))(jax.random.split(key_list[2], MB * (N_DP * GROUPS))).reshape((MB, N_DP * GROUPS, CONT)).astype(jnp.int32)
    master = scatter_about(key_list[3], (D, NCOL), D ** -0.5, 0.1875, ((0, 8),), jnp.float32)
    gains = jnp.clip(1.0 + 0.1 * jax.random.normal(key_list[4], (NGAIN,), jnp.float32), 0.5, 1.5)
    gain_stats = jnp.clip(jnp.exp(jax.random.uniform(key_list[5], (NGAIN,), jnp.float32, math.log(1024.0), math.log(65536.0))), 1024.0, 65536.0)
    owner_keys = jax.random.split(jax.random.fold_in(key_list[6], 1), (N_FSDP * NBLK) // NBLK)
    owner_turns = jax.random.permutation(jax.random.fold_in(key_list[6], 3), (N_FSDP * NBLK) // NBLK)
    owner = jax.vmap(lambda own, number: routed_block(jax.random.fold_in(key_list[6], 2), own, number, NBLK, N_DP, 1, CAP, 1))(owner_keys, owner_turns).reshape((N_FSDP * NBLK, 1))
    stat_left = scatter_about(key_list[7], (N_FSDP, N_DP * CAP, RS, RS), (BC * TOKENS // 4), 3145728, ((0, 8), (1, 4)), jnp.float32)
    stat_right = scatter_about(key_list[8], (N_FSDP, N_DP * CAP, BC, BC), (RS * TOKENS // 4), 3670016, ((0, 8), (1, 4)), jnp.float32)
    root_left = draw_root_left(jax.random.fold_in(key_list[11], 71), 0)
    root_right = draw_root_right(jax.random.fold_in(key_list[11], 71), 0)
    return {"tokens": tokens, "cotangent": cotangent, "lengths": lengths, "master": master, "gains": gains, "gain_stats": gain_stats, "owner": owner, "stat_left": stat_left, "stat_right": stat_right, "root_left": root_left, "root_right": root_right}


EPSILON = 1e-06
HIGHEST = lax.Precision.HIGHEST
MASKED = -1e+30
RATE = 0.02
GAIN_RATE = 0.05
DECAY = 0.5

@jax.custom_vjp
def low(v):
    return lax.optimization_barrier(v.astype(jnp.bfloat16)).astype(jnp.float32)

@jax.custom_vjp
def low_back(v):
    return v

def low_keep(v):
    return (low(v), None)

def low_pass(kept, grad):
    return (grad,)

def back_keep(v):
    return (v, None)

def back_low(kept, grad):
    return (low(grad),)
low.defvjp(low_keep, low_pass)
low_back.defvjp(back_keep, back_low)

def rms_gain(values, gain):
    return values * lax.rsqrt(lax.optimization_barrier(jnp.mean(values * values, axis=-1, keepdims=True)) + EPSILON) * gain

def rope_tables(positions):
    half_width = HD // 2
    freqs = 10000.0 ** (-2.0 * jnp.arange(half_width, dtype=jnp.float32) / HD)
    angles = positions.astype(jnp.float32)[:, None] * freqs[None, :]
    return (jnp.cos(angles), jnp.sin(angles))

def rotate(values, cosine, sine):
    half_width = values.shape[-1] // 2
    first_half = values[..., :half_width]
    second_half = values[..., half_width:]
    return jnp.concatenate([first_half * cosine - second_half * sine, second_half * cosine + first_half * sine], axis=-1)

def slot_layout(slots):
    in_prompt = slots < PROMPT
    offset = slots - PROMPT
    segment = jnp.where(in_prompt, -1, offset // CLEN)
    position = jnp.where(in_prompt, slots, PROMPT + offset % CLEN)
    return (segment.astype(jnp.int32), position.astype(jnp.int32))

def visibility(query_slots, key_slots, lens):
    query_seg, query_pos = slot_layout(query_slots)
    key_seg, key_pos = slot_layout(key_slots)
    picks = key_seg[:, None] == jnp.arange(CONT, dtype=jnp.int32)[None, :]
    key_len = lax.optimization_barrier(jnp.sum(jnp.where(picks, lens[None, :], 0), axis=1))
    key_used = (key_seg < 0) | (key_pos - PROMPT < key_len)
    distance = query_pos[:, None] - key_pos[None, :]
    same_part = (key_seg[None, :] < 0) | (key_seg[None, :] == query_seg[:, None])
    return (distance >= 0) & (distance < WIN) & same_part & key_used[None, :]

def group_forward(group_in, weights, gains, lens):
    pre_attn = gains[:D]
    post_attn = gains[D:2 * D]
    pre_ffw = gains[2 * D:3 * D]
    post_ffw = gains[3 * D:4 * D]
    query_gain = gains[4 * D:4 * D + HD]
    key_gain = gains[4 * D + HD:]
    gate_start = QKVW + HEADS * HD
    normed = low(rms_gain(group_in, pre_attn))
    projected = low_back(jnp.dot(normed, weights[:, :QKVW], precision=HIGHEST))
    queries = projected[:, :HEADS * HD].reshape(GLEN, HEADS, HD)
    keys = projected[:, HEADS * HD:(HEADS + 1) * HD]
    values = projected[:, (HEADS + 1) * HD:]
    slots = jnp.arange(GLEN, dtype=jnp.int32)
    segment, positions = slot_layout(slots)
    cosine, sine = rope_tables(positions)
    rot_queries = low(rotate(rms_gain(queries, query_gain), cosine[:, None, :], sine[:, None, :]))
    rot_keys = low(rotate(rms_gain(keys, key_gain), cosine, sine))
    low_values = low(values)
    visible = visibility(slots, slots, lens)
    scores = low_back(jnp.einsum('qhd,kd->hqk', rot_queries, rot_keys, precision=HIGHEST) * HD ** (-0.5))
    scores = jnp.where(visible[None], scores, MASKED)
    probs = jax.nn.softmax(scores, axis=-1)
    mixed = jnp.einsum('hqk,kd->qhd', low(probs), low_values, precision=HIGHEST).reshape(GLEN, HEADS * HD)
    attended = low(low_back(mixed))
    branch_one = low_back(jnp.dot(attended, weights[:, QKVW:gate_start].T, precision=HIGHEST))
    resid = group_in + rms_gain(branch_one, post_attn)
    ffw_in = low(rms_gain(resid, pre_ffw))
    gate = low_back(jnp.dot(ffw_in, weights[:, gate_start:gate_start + FF], precision=HIGHEST))
    up_proj = low_back(jnp.dot(ffw_in, weights[:, gate_start + FF:gate_start + 2 * FF], precision=HIGHEST))
    hidden = low(jax.nn.gelu(gate, approximate=True) * up_proj)
    branch_two = low_back(jnp.dot(hidden, weights[:, gate_start + 2 * FF:].T, precision=HIGHEST))
    return resid + rms_gain(branch_two, post_ffw)

def full_forward(master, gains, group_tokens, group_lens):
    weights = low(master)

    def one_group(pair):
        return group_forward(pair[0], weights, gains, pair[1])
    return lax.map(jax.checkpoint(one_group), (group_tokens, group_lens))

def reference(tokens, cotangent, lengths, master, gains, gain_stats, owner, stat_left, stat_right, root_left, root_right):
    groups_all = tokens.shape[0] * tokens.shape[1]
    flat_tokens = tokens.astype(jnp.float32).reshape(groups_all, GLEN, D)
    flat_lens = lengths.reshape(groups_all, CONT).astype(jnp.int32)

    def forward(master_in, gains_in, tokens_in):
        return full_forward(master_in, gains_in, tokens_in, flat_lens)
    result, pullback = jax.vjp(forward, master, gains, flat_tokens)
    full_grad, gain_grad, token_grad = pullback(cotangent.astype(jnp.float32).reshape(groups_all, GLEN, D))
    output = result.astype(jnp.bfloat16).reshape(tokens.shape)
    input_grad = token_grad.astype(jnp.bfloat16).reshape(tokens.shape)
    bands = full_grad.reshape(N_FSDP, RS, NBLK, BC).transpose(0, 2, 1, 3)
    owners = owner.reshape(N_FSDP, NBLK).astype(jnp.int32)
    member = (owners[:, :, None] == jnp.arange(N_DP, dtype=jnp.int32)[None, None, :]).astype(jnp.int32)
    ranks = lax.optimization_barrier(jnp.sum((jnp.cumsum(member, axis=1) - 1) * member, axis=2)).astype(jnp.int32)
    slot = (owners * CAP + ranks).astype(jnp.int32)
    pick = (slot[:, None, :] == jnp.arange(N_DP * CAP, dtype=jnp.int32)[None, :, None]).astype(jnp.float32)
    slot_grads = jnp.einsum('jsb,jbrc->jsrc', pick, bands, precision=HIGHEST)
    new_left = DECAY * stat_left + (1.0 - DECAY) * jnp.einsum('jsrc,jstc->jsrt', slot_grads, slot_grads, precision=HIGHEST)
    new_right = DECAY * stat_right + (1.0 - DECAY) * jnp.einsum('jsrc,jsrd->jscd', slot_grads, slot_grads, precision=HIGHEST)
    shaped = jnp.einsum('jsrt,jstc->jsrc', root_left.astype(jnp.float32), slot_grads, precision=HIGHEST)
    shaped = jnp.einsum('jsrc,jscd->jsrd', shaped, root_right.astype(jnp.float32), precision=HIGHEST)
    factor = lax.rsqrt(lax.optimization_barrier(jnp.mean(shaped * shaped, axis=(2, 3), keepdims=True)) + EPSILON)
    changes = -RATE * shaped * factor
    placed = jnp.take_along_axis(changes, slot[:, :, None, None], axis=1)
    new_master = master + placed.transpose(0, 2, 1, 3).reshape(D, NCOL)
    new_weights = new_master.astype(jnp.bfloat16)
    new_gain_stats = DECAY * gain_stats + (1.0 - DECAY) * gain_grad * gain_grad
    gain_change = -GAIN_RATE * gain_grad * lax.rsqrt(new_gain_stats)
    return (output, input_grad, slot_grads, gain_grad, new_left, new_right, new_master, new_weights, new_gain_stats, gain_change)
```

```python
import jax
import jax.numpy as jnp
import numpy as np
from jax import lax
from jax.sharding import PartitionSpec as P

D = 1152
HEADS = 4
HD = 256
FF = 6912
WIN = 512
PROMPT = 1024
CONT = 8
CLEN = 128
BC = 128
GLEN = 2048
QKVW = 1536
OUTW = HEADS * HD
NBLK = 182
ATTN_BLOCKS = (QKVW + OUTW) // BC
FF_BLOCKS = FF // BC

EPSILON = 1e-06
MASKED = -1e30
RATE = 0.02
GAIN_RATE = 0.05
DECAY = 0.5
SCALE = HD ** (-0.5)
MAX_ROUNDS = 16
BF = jnp.bfloat16
F32 = jnp.float32


def rms_gain(values, gain):
    return values * lax.rsqrt(jnp.mean(values * values, axis=-1, keepdims=True) + EPSILON) * gain


def rope_tables(positions):
    half_width = HD // 2
    freqs = 10000.0 ** (-2.0 * jnp.arange(half_width, dtype=F32) / HD)
    angles = positions.astype(F32)[:, None] * freqs[None, :]
    return (jnp.cos(angles), jnp.sin(angles))


def rotate(values, cosine, sine):
    half_width = values.shape[-1] // 2
    first_half = values[..., :half_width]
    second_half = values[..., half_width:]
    return jnp.concatenate(
        [first_half * cosine - second_half * sine, second_half * cosine + first_half * sine],
        axis=-1,
    )


def slot_layout(slots):
    in_prompt = slots < PROMPT
    offset = slots - PROMPT
    segment = jnp.where(in_prompt, -1, offset // CLEN)
    position = jnp.where(in_prompt, slots, PROMPT + offset % CLEN)
    return (segment, position)


def visibility(query_slots, key_slots, lens):
    query_seg, query_pos = slot_layout(query_slots)
    key_seg, key_pos = slot_layout(key_slots)
    picks = key_seg[:, None] == jnp.arange(CONT, dtype=jnp.int32)[None, :]
    key_len = jnp.sum(jnp.where(picks, lens[None, :], 0), axis=1)
    key_used = (key_seg < 0) | (key_pos - PROMPT < key_len)
    distance = query_pos[:, None] - key_pos[None, :]
    same_part = (key_seg[None, :] < 0) | (key_seg[None, :] == query_seg[:, None])
    present = key_slots >= 0
    return (distance >= 0) & (distance < WIN) & same_part & (key_used & present)[None, :]


def split_gains(gains):
    return (
        gains[:D],
        gains[D : 2 * D],
        gains[2 * D : 3 * D],
        gains[3 * D : 4 * D],
        gains[4 * D : 4 * D + HD],
        gains[4 * D + HD :],
    )


def prepare_heads(queries, keys, query_gain, key_gain, cosine, sine):
    rot_queries = rotate(rms_gain(queries, query_gain), cosine[:, None, :], sine[:, None, :])
    rot_keys = rotate(rms_gain(keys, key_gain), cosine, sine)
    return (rot_queries, rot_keys)


def dot_nn(left, right):
    return jnp.dot(left, right, preferred_element_type=F32)


def dot_nt(left, right):
    return lax.dot_general(left, right, (((1,), (1,)), ((), ())), preferred_element_type=F32)


def dot_tn(left, right):
    return lax.dot_general(left, right, (((0,), (0,)), ((), ())), preferred_element_type=F32)


def swap_core(value, nd):
    return lax.ppermute(value, "dp", [(e, e ^ 1) for e in range(nd)])


def shift_x(value, nd, step):
    nx = nd // 2
    pairs = [(e, ((e // 2 + step) % nx) * 2 + e % 2) for e in range(nd)]
    return lax.ppermute(value, "dp", pairs)


def gather_parts(value, nd):
    mine = [value] + [shift_x(value, nd, k) for k in range(1, nd // 2)]
    return mine + [swap_core(part, nd) for part in mine]


def gather_dp(value, nd):
    return jnp.concatenate(gather_parts(value, nd), axis=0)


def part_owners(nd):
    nx = nd // 2
    me = lax.axis_index("dp")
    x, core = me // 2, me % 2
    out = []
    for flip in range(2):
        for k in range(nx):
            out.append(((x + nx - k) % nx) * 2 + (core if flip == 0 else 1 - core))
    return out


def scatter_sum_dp(own_half, other_half, nd):
    nx = nd // 2
    received = swap_core(other_half.astype(BF), nd)
    total = own_half + received.astype(F32)
    rows = total.shape[0] // nx
    result = total[:rows]
    for k in range(1, nx):
        sent = total[k * rows : (k + 1) * rows].astype(BF)
        result = result + shift_x(sent, nd, nx - k).astype(F32)
    return result


def sum_everywhere(value, nd, nf):
    for axis, count in (("dp", nd), ("fsdp", nf)):
        step = 1
        while step < count:
            value = value + lax.ppermute(value, axis, [(e, e ^ step) for e in range(count)])
            step *= 2
    return value


def key_plan(nf):
    rows = GLEN // nf
    slots = np.arange(GLEN)
    seg = np.where(slots < PROMPT, -1, (slots - PROMPT) // CLEN)
    pos = np.where(slots < PROMPT, slots, PROMPT + (slots - PROMPT) % CLEN)
    dist = pos[:, None] - pos[None, :]
    vis = (dist >= 0) & (dist < WIN) & ((seg[None, :] < 0) | (seg[None, :] == seg[:, None]))
    need = vis.reshape(nf, rows, nf, rows).any(axis=(1, 3))
    sources = [[u for u in reversed(range(nf)) if need[t, u] and u != t] for t in range(nf)]
    count = max(len(s) for s in sources)
    plan, tables = [], []
    for k in range(count):
        edges = [(s[k], t) for t, s in enumerate(sources) if len(s) > k]
        rounds = []
        while edges:
            used, now, later = set(), [], []
            for src, dst in edges:
                if src in used:
                    later.append((src, dst))
                else:
                    used.add(src)
                    now.append((src, dst))
            rounds.append(now)
            edges = later
        plan.append(rounds)
        tables.append([s[k] if len(s) > k else -1 for s in sources])
    return (plan, tables)


def pick_static(table, index):
    values = jnp.asarray(table, jnp.int32)
    hit = jnp.arange(len(table), dtype=jnp.int32) == index
    return jnp.sum(jnp.where(hit, values, 0))


def spread_keys(own, nf):
    rows = own.shape[1]
    me = lax.axis_index("fsdp")
    step = jnp.arange(rows, dtype=jnp.int32)
    plan, tables = key_plan(nf)
    if sum(len(r) for r in plan) > MAX_ROUNDS:
        return (
            lax.all_gather(own, "fsdp", axis=1, tiled=True),
            jnp.arange(rows * nf, dtype=jnp.int32),
        )
    parts, ids = [own], [me * rows + step]
    for rounds, table in zip(plan, tables):
        got = [lax.ppermute(own, "fsdp", pairs) for pairs in rounds]
        total = got[0]
        for more in got[1:]:
            total = total + more
        source = pick_static(table, me)
        parts.append(total)
        ids.append(jnp.where(source >= 0, source * rows + step, -1))
    return (jnp.concatenate(parts, axis=1), jnp.concatenate(ids))


def return_key_grads(terms, rows, nf):
    plan, _ = key_plan(nf)
    if sum(len(r) for r in plan) > MAX_ROUNDS:
        return lax.psum_scatter(
            terms.astype(BF), "fsdp", scatter_dimension=1, tiled=True
        ).astype(F32)
    total = terms[:, :rows]
    for k, rounds in enumerate(plan):
        sent = terms[:, (k + 1) * rows : (k + 2) * rows].astype(BF)
        for pairs in rounds:
            back = lax.ppermute(sent, "fsdp", [(dst, src) for src, dst in pairs])
            total = total + back.astype(F32)
    return total


def attend(query_low, keys, values, visible):
    scores = jnp.einsum("thd,kd->thk", query_low, keys, preferred_element_type=F32) * SCALE
    scores = jnp.where(visible[:, None, :], scores, MASKED)
    highest = jnp.max(scores, axis=-1, keepdims=True)
    expo = jnp.exp(scores - highest)
    probs = expo / jnp.sum(expo, axis=-1, keepdims=True)
    mixed = jnp.einsum("thk,kd->thd", probs.astype(BF), values, preferred_element_type=F32)
    return (mixed, probs)


def attend_back(query_low, keys, values, probs, low_mixed):
    grad_probs = jnp.einsum("thd,kd->thk", low_mixed, values, preferred_element_type=F32)
    row_dot = jnp.sum(grad_probs * probs, axis=-1, keepdims=True)
    grad_scores = (probs * (grad_probs - row_dot)).astype(BF)
    grad_queries = jnp.einsum("thk,kd->thd", grad_scores, keys, preferred_element_type=F32) * SCALE
    key_terms = (
        jnp.einsum("thk,thd->kd", grad_scores, query_low, preferred_element_type=F32) * SCALE
    )
    value_terms = jnp.einsum("thk,thd->kd", probs.astype(BF), low_mixed, preferred_element_type=F32)
    return (grad_queries, key_terms, value_terms)


def local(
    tokens,
    cotangent,
    lengths,
    master,
    gains,
    gain_stats,
    owner,
    stat_left,
    stat_right,
    root_left,
    root_right,
):
    nd = lax.axis_size("dp")
    nf = lax.axis_size("fsdp")
    dp_me = lax.axis_index("dp")
    core = dp_me % 2
    micros = tokens.shape[0]
    rows = tokens.shape[2]
    count = micros * rows
    band = master.shape[0]
    capacity = stat_left.shape[1]
    first = lax.axis_index("fsdp") * rows
    pre_attn, post_attn, pre_ffw, post_ffw, query_gain, key_gain = split_gains(gains)

    per = -(-FF_BLOCKS // nd)
    width = per * BC
    start = jnp.minimum(dp_me * per, FF_BLOCKS - per)
    fresh = dp_me * per - start
    gate_at = ATTN_BLOCKS * BC

    def columns(at, size):
        return lax.dynamic_slice(master, (0, at), (band, size)).astype(BF)

    def gather_rows(part):
        return lax.all_gather(part, "fsdp", axis=0, tiled=True)

    def halves(at, size):
        half = size // 2
        mine = gather_rows(columns(at + core * half, half))
        other = swap_core(mine, nd)
        whole = jnp.zeros((D, size), BF)
        whole = lax.dynamic_update_slice(whole, mine, (0, core * half))
        return lax.dynamic_update_slice(whole, other, (0, (1 - core) * half))

    w_qkv = halves(0, QKVW)
    w_out = halves(QKVW, OUTW)
    gate_cols = columns(gate_at + start * BC, width)
    up_cols = columns(gate_at + FF + start * BC, width)
    down_cols = columns(gate_at + 2 * FF + start * BC, width)
    keep = (jnp.arange(width, dtype=jnp.int32) >= fresh * BC)[None, :]
    down_cols = jnp.where(keep, down_cols, jnp.zeros_like(down_cols))
    w_gate = gather_rows(gate_cols)
    w_up = gather_rows(up_cols)
    w_down = gather_rows(down_cols)

    flat_in = tokens.astype(F32).reshape(count, D)
    normed = rms_gain(flat_in, pre_attn).astype(BF)
    projected = dot_nn(normed, w_qkv)
    queries = projected[:, :OUTW].reshape(count, HEADS, HD)
    keys = projected[:, OUTW : OUTW + HD]
    values = projected[:, OUTW + HD :]
    slots = first + jnp.arange(rows, dtype=jnp.int32)
    _, positions = slot_layout(slots)
    cosine, sine = rope_tables(positions)
    cosine, sine = (jnp.tile(cosine, (micros, 1)), jnp.tile(sine, (micros, 1)))
    rot_queries, rot_keys = prepare_heads(queries, keys, query_gain, key_gain, cosine, sine)
    query_low = rot_queries.astype(BF).reshape(micros, rows, HEADS, HD)
    own_keys = jnp.concatenate([rot_keys.astype(BF), values.astype(BF)], axis=1)
    key_buffer, key_slots = spread_keys(own_keys.reshape(micros, rows, 2 * HD), nf)
    keys_all, values_all = (key_buffer[..., :HD], key_buffer[..., HD:])
    all_probs, all_attended = [], []
    for m in range(micros):
        visible = visibility(slots, key_slots, lengths[m, 0])
        mixed, probs = attend(query_low[m], keys_all[m], values_all[m], visible)
        all_probs.append(probs)
        all_attended.append(mixed.reshape(rows, OUTW).astype(BF))

    half = (nd // 2) * rows
    outputs, saved, gathered_in, gathered_two, hiddens, low_gates, low_ups = [], [], [], [], [], [], []
    grad_resids, gain_terms, low_ones = [], [], []
    for m in range(micros):
        part_in = flat_in[m * rows : (m + 1) * rows]
        branch_one = dot_nt(all_attended[m], w_out)
        resid = part_in + rms_gain(branch_one, post_attn)
        ffw_in = rms_gain(resid, pre_ffw).astype(BF)
        every_in = gather_dp(ffw_in, nd)
        gate = dot_nn(every_in, w_gate)
        up = dot_nn(every_in, w_up)
        hidden = (jax.nn.gelu(gate, approximate=True) * up).astype(BF)
        partial = dot_nt(hidden, w_down)
        branch_two = scatter_sum_dp(partial[:half], partial[half:], nd)
        outputs.append((resid + rms_gain(branch_two, post_ffw)).astype(BF))
        gathered_in.append(every_in)
        hiddens.append(hidden)
        saved.append((branch_one, resid, gate, up, branch_two))
    for m in range(micros):
        branch_one, resid, gate, up, branch_two = saved[m]
        upstream = cotangent[m, 0].astype(F32)
        grad_two, grad_post_ffw = jax.vjp(rms_gain, branch_two, post_ffw)[1](upstream)
        every_two = gather_dp(grad_two.astype(BF), nd)
        grad_hidden = dot_nn(every_two, w_down)
        grad_gate, grad_up = jax.vjp(
            lambda gate_in, up_in: jax.nn.gelu(gate_in, approximate=True) * up_in, gate, up
        )[1](grad_hidden)
        low_gate, low_up = (grad_gate.astype(BF), grad_up.astype(BF))
        partial = dot_nt(low_gate, w_gate) + dot_nt(low_up, w_up)
        grad_ffw_in = scatter_sum_dp(partial[:half], partial[half:], nd)
        grad_resid, grad_pre_ffw = jax.vjp(rms_gain, resid, pre_ffw)[1](grad_ffw_in)
        grad_resid = upstream + grad_resid
        grad_one, grad_post_attn = jax.vjp(rms_gain, branch_one, post_attn)[1](grad_resid)
        gathered_two.append(every_two)
        low_gates.append(low_gate)
        low_ups.append(low_up)
        grad_resids.append(grad_resid)
        low_ones.append(grad_one.astype(BF))
        gain_terms.append((grad_post_attn, grad_pre_ffw, grad_post_ffw))

    def reduce_rows(lefts, rights):
        term = dot_tn(jnp.concatenate(lefts, axis=0), jnp.concatenate(rights, axis=0))
        return lax.psum_scatter(term.astype(BF), "fsdp", scatter_dimension=0, tiled=True)

    def blocks_of(part):
        return part.reshape(band, part.shape[1] // BC, BC).transpose(1, 0, 2)

    ff_bands = [
        reduce_rows(gathered_in, low_gates),
        reduce_rows(gathered_in, low_ups),
        reduce_rows(gathered_two, hiddens),
    ]
    ff_blocks = jnp.concatenate([blocks_of(part) for part in ff_bands], axis=0)

    low_one = jnp.concatenate(low_ones, axis=0)
    attended = jnp.concatenate(all_attended, axis=0)
    low_mixed = dot_nn(low_one, w_out).astype(BF).reshape(micros, rows, HEADS, HD)
    grad_queries, key_terms = [], []
    for m in range(micros):
        for_queries, for_keys, for_values = attend_back(
            query_low[m], keys_all[m], values_all[m], all_probs[m], low_mixed[m]
        )
        grad_queries.append(for_queries)
        key_terms.append(jnp.concatenate([for_keys, for_values], axis=1))
    own_terms = return_key_grads(jnp.stack(key_terms), rows, nf).reshape(count, 2 * HD)
    grad_keys, grad_values = (own_terms[:, :HD], own_terms[:, HD:])

    def heads_only(query_in, key_in, query_scale, key_scale):
        return prepare_heads(query_in, key_in, query_scale, key_scale, cosine, sine)

    pull_heads = jax.vjp(heads_only, queries, keys, query_gain, key_gain)[1]
    grad_query_pre, grad_key_pre, grad_query_gain, grad_key_gain = pull_heads(
        (jnp.concatenate(grad_queries, axis=0), grad_keys)
    )
    low_projected = jnp.concatenate(
        [grad_query_pre.reshape(count, OUTW), grad_key_pre, grad_values], axis=1
    ).astype(BF)
    grad_normed = dot_nt(low_projected, w_qkv)
    grad_in, grad_pre_attn = jax.vjp(rms_gain, flat_in, pre_attn)[1](grad_normed)
    input_grad = (jnp.concatenate(grad_resids, axis=0) + grad_in).astype(BF)

    attn_per = -(-ATTN_BLOCKS // nd)
    attn_width = attn_per * BC
    attn_term = jnp.concatenate([dot_tn(normed, low_projected), dot_tn(low_one, attended)], axis=1)
    attn_term = jnp.pad(attn_term, ((0, 0), (0, nd * attn_width - ATTN_BLOCKS * BC)))

    def owner_columns(index):
        return lax.dynamic_slice(attn_term, (0, index * attn_width), (D, attn_width))

    owners_at = part_owners(nd)
    attn_sum = scatter_sum_dp(
        jnp.concatenate([owner_columns(e) for e in owners_at[: nd // 2]], axis=0),
        jnp.concatenate([owner_columns(e) for e in owners_at[nd // 2 :]], axis=0),
        nd,
    )
    spread = lax.all_to_all(
        attn_sum.astype(BF).reshape(nf, band, attn_width), "fsdp", split_axis=0, concat_axis=0
    )
    attn_band = jnp.sum(spread.astype(F32), axis=0).astype(BF)

    def gather_blocks(part):
        pieces = gather_parts(part, nd)
        out = jnp.zeros((nd,) + part.shape, part.dtype)
        for piece, index in zip(pieces, part_owners(nd)):
            out = lax.dynamic_update_slice(out, piece[None], (index,) + (0,) * part.ndim)
        return out

    ff_all = gather_blocks(ff_blocks)
    attn_all = gather_blocks(blocks_of(attn_band))
    pieces = [attn_all.reshape((nd * attn_per, band, BC))[:ATTN_BLOCKS]]
    for kind in range(3):
        for e in range(nd):
            begin = min(e * per, FF_BLOCKS - per)
            skip = min(e * per - begin, per)
            pieces.append(ff_all[e, kind * per + skip : (kind + 1) * per])
    blocks = jnp.concatenate(pieces, axis=0)

    owners = owner[:, 0]
    index = jnp.arange(NBLK, dtype=jnp.int32)
    before = (owners[:, None] == owners[None, :]) & (index[None, :] < index[:, None])
    ranks = jnp.sum(before.astype(jnp.int32), axis=1)
    slot = owners * capacity + ranks
    my_slots = dp_me * capacity + jnp.arange(capacity, dtype=jnp.int32)
    pick_mine = (slot[None, :] == my_slots[:, None]).astype(BF)
    slot_low = jnp.einsum("sb,brc->src", pick_mine, blocks, preferred_element_type=F32)
    slot_grads = slot_low
    low_slots = slot_low.astype(BF)
    new_left = DECAY * stat_left[0] + (1.0 - DECAY) * jnp.einsum(
        "src,stc->srt", low_slots, low_slots, preferred_element_type=F32
    )
    new_right = DECAY * stat_right[0] + (1.0 - DECAY) * jnp.einsum(
        "src,srd->scd", low_slots, low_slots, preferred_element_type=F32
    )
    every_slot = jnp.arange(nd * capacity, dtype=jnp.int32)
    pick_root = (slot[:, None] == every_slot[None, :]).astype(BF)

    def roots_by_block(root):
        every = gather_blocks(root).reshape((nd * capacity,) + root.shape[1:])
        return jnp.einsum("bs,srt->brt", pick_root, every, preferred_element_type=F32).astype(BF)

    lefts = roots_by_block(root_left[0])
    rights = roots_by_block(root_right[0])
    shaped = jnp.einsum("brt,btc->brc", lefts, blocks, preferred_element_type=F32)
    shaped = jnp.einsum("brc,bcd->brd", shaped.astype(BF), rights, preferred_element_type=F32)
    factor = lax.rsqrt(jnp.mean(shaped * shaped, axis=(1, 2), keepdims=True) + EPSILON)
    changes = -RATE * shaped * factor
    new_master = master + changes.transpose(1, 0, 2).reshape(band, NBLK * BC)
    new_weights = new_master.astype(BF)

    post_attn_sum = sum(entry[0] for entry in gain_terms)
    pre_ffw_sum = sum(entry[1] for entry in gain_terms)
    post_ffw_sum = sum(entry[2] for entry in gain_terms)
    gain_sum = jnp.concatenate(
        [grad_pre_attn, post_attn_sum, pre_ffw_sum, post_ffw_sum, grad_query_gain, grad_key_gain]
    )
    gain_grad = sum_everywhere(gain_sum, nd, nf)
    new_gain_stats = DECAY * gain_stats + (1.0 - DECAY) * gain_grad * gain_grad
    gain_change = -GAIN_RATE * gain_grad * lax.rsqrt(new_gain_stats)
    return (
        jnp.stack(outputs)[:, None],
        input_grad.reshape(micros, 1, rows, D),
        slot_grads[None],
        gain_grad,
        new_left[None],
        new_right[None],
        new_master,
        new_weights,
        new_gain_stats,
        gain_change,
    )


def solution(mesh):
    in_specs = (
        P(None, "dp", "fsdp", None),
        P(None, "dp", "fsdp", None),
        P(None, "dp", None),
        P("fsdp", None),
        P(),
        P(),
        P("fsdp", None),
        P("fsdp", "dp", None, None),
        P("fsdp", "dp", None, None),
        P("fsdp", "dp", None, None),
        P("fsdp", "dp", None, None),
    )
    out_specs = (
        P(None, "dp", "fsdp", None),
        P(None, "dp", "fsdp", None),
        P("fsdp", "dp", None, None),
        P(),
        P("fsdp", "dp", None, None),
        P("fsdp", "dp", None, None),
        P("fsdp", None),
        P("fsdp", None),
        P(),
        P(),
    )
    return jax.shard_map(local, mesh=mesh, in_specs=in_specs, out_specs=out_specs, check_vma=False)
```

```python
import jax
import jax.numpy as jnp
import numpy as np
from jax import lax
from jax.experimental import pallas as pl
from jax.experimental.pallas import tpu as pltpu
from jax.sharding import PartitionSpec as P

D = 1152
HEADS = 4
HD = 256
FF = 6912
WIN = 512
PROMPT = 1024
CONT = 8
CLEN = 128
BC = 128
GLEN = 2048
QKVW = 1536
OUTW = HEADS * HD
NBLK = 182
ATTN_BLOCKS = (QKVW + OUTW) // BC
FF_BLOCKS = FF // BC

EPSILON = 1e-06
MASKED = -1e30
RATE = 0.02
GAIN_RATE = 0.05
DECAY = 0.5
SCALE = HD ** (-0.5)
DIRECT_MAX = 8
LATE = 21
VMEM_LIMIT = 40 * 1024 * 1024
BF = jnp.bfloat16
F32 = jnp.float32


def rms_gain(values, gain):
    return values * lax.rsqrt(jnp.mean(values * values, axis=-1, keepdims=True) + EPSILON) * gain


def rope_tables(positions):
    half_width = HD // 2
    freqs = 10000.0 ** (-2.0 * jnp.arange(half_width, dtype=F32) / HD)
    angles = positions.astype(F32)[:, None] * freqs[None, :]
    return (jnp.cos(angles), jnp.sin(angles))


def rotate(values, cosine, sine):
    half_width = values.shape[-1] // 2
    first_half = values[..., :half_width]
    second_half = values[..., half_width:]
    return jnp.concatenate(
        [first_half * cosine - second_half * sine, second_half * cosine + first_half * sine],
        axis=-1,
    )


def slot_layout(slots):
    in_prompt = slots < PROMPT
    offset = slots - PROMPT
    segment = jnp.where(in_prompt, -1, offset // CLEN)
    position = jnp.where(in_prompt, slots, PROMPT + offset % CLEN)
    return (segment, position)


def visibility(query_slots, key_slots, lens):
    query_seg, query_pos = slot_layout(query_slots)
    key_seg, key_pos = slot_layout(key_slots)
    picks = key_seg[:, None] == jnp.arange(CONT, dtype=jnp.int32)[None, :]
    key_len = jnp.sum(jnp.where(picks, lens[None, :], 0), axis=1)
    key_used = (key_seg < 0) | (key_pos - PROMPT < key_len)
    distance = query_pos[:, None] - key_pos[None, :]
    same_part = (key_seg[None, :] < 0) | (key_seg[None, :] == query_seg[:, None])
    present = key_slots >= 0
    return (distance >= 0) & (distance < WIN) & same_part & (key_used & present)[None, :]


def split_gains(gains):
    return (
        gains[:D],
        gains[D : 2 * D],
        gains[2 * D : 3 * D],
        gains[3 * D : 4 * D],
        gains[4 * D : 4 * D + HD],
        gains[4 * D + HD :],
    )


def prepare_heads(queries, keys, query_gain, key_gain, cosine, sine):
    rot_queries = rotate(rms_gain(queries, query_gain), cosine[:, None, :], sine[:, None, :])
    rot_keys = rotate(rms_gain(keys, key_gain), cosine, sine)
    return (rot_queries, rot_keys)


def dot_nn(left, right):
    return jnp.dot(left, right, preferred_element_type=F32)


def dot_nt(left, right):
    return lax.dot_general(left, right, (((1,), (1,)), ((), ())), preferred_element_type=F32)


def dot_tn(left, right):
    return lax.dot_general(left, right, (((0,), (0,)), ((), ())), preferred_element_type=F32)


def swap_core(value, nd):
    return lax.ppermute(value, "dp", [(e, e ^ 1) for e in range(nd)])


def shift_x(value, nd, step):
    nx = nd // 2
    pairs = [(e, ((e // 2 + step) % nx) * 2 + e % 2) for e in range(nd)]
    return lax.ppermute(value, "dp", pairs)


def gather_parts(value, nd):
    mine = [value] + [shift_x(value, nd, k) for k in range(1, nd // 2)]
    return mine + [swap_core(part, nd) for part in mine]


def gather_dp(value, nd):
    return jnp.concatenate(gather_parts(value, nd), axis=0)


def part_owners(nd):
    nx = nd // 2
    me = lax.axis_index("dp")
    x, core = me // 2, me % 2
    out = []
    for flip in range(2):
        for k in range(nx):
            out.append(((x + nx - k) % nx) * 2 + (core if flip == 0 else 1 - core))
    return out


def scatter_sum_dp(own_half, other_half, nd):
    nx = nd // 2
    received = swap_core(other_half.astype(BF), nd)
    total = own_half + received.astype(F32)
    rows = total.shape[0] // nx
    result = total[:rows]
    for k in range(1, nx):
        sent = total[k * rows : (k + 1) * rows].astype(BF)
        result = result + shift_x(sent, nd, nx - k).astype(F32)
    return result


def sum_everywhere(value, nd, nf):
    for axis, count in (("dp", nd), ("fsdp", nf)):
        step = 1
        while step < count:
            value = value + lax.ppermute(value, axis, [(e, e ^ step) for e in range(count)])
            step *= 2
    return value


def after(value, *others):
    return lax.optimization_barrier((value,) + others)[0]


def swap_fsdp(value, flip, nf):
    return lax.ppermute(value, "fsdp", [(e, e ^ flip) for e in range(nf)])


def gather_rows(own, nf):
    if nf > DIRECT_MAX:
        return lax.all_gather(own, "fsdp", axis=0, tiled=True)
    me = lax.axis_index("fsdp")
    band, width = own.shape
    straight = [own] + [swap_fsdp(own, flip, nf) for flip in range(2, nf, 2)]
    crossed = [swap_fsdp(part, 1, nf) for part in straight]
    whole = jnp.zeros((nf * band, width), own.dtype)
    for k in range(nf // 2):
        whole = lax.dynamic_update_slice(whole, straight[k], ((me ^ (2 * k)) * band, 0))
        whole = lax.dynamic_update_slice(whole, crossed[k], ((me ^ (2 * k + 1)) * band, 0))
    return whole


def add_low(left, right):
    return (left.astype(F32) + right.astype(F32)).astype(BF)


def reduce_rows(terms, nf):
    if nf > DIRECT_MAX:
        return lax.psum_scatter(terms, "fsdp", scatter_dimension=0, tiled=True)
    me = lax.axis_index("fsdp")
    band, width = (terms.shape[0] // nf, terms.shape[1])

    def part(flip):
        return lax.dynamic_slice(terms, ((me ^ flip) * band, 0), (band, width))

    sums = []
    for k in range(nf // 2 - 1, -1, -1):
        received = swap_fsdp(part(2 * k + 1), 1, nf)
        if k:
            sums.append(swap_fsdp(add_low(part(2 * k), received), 2 * k, nf))
        else:
            sums.append(received)
    total = part(0).astype(F32)
    for piece in sums:
        total = total + piece.astype(F32)
    return total.astype(BF)


def direct_reduce(terms, nf):
    band, width = (terms.shape[0] // nf, terms.shape[1])
    if nf > DIRECT_MAX:
        spread = lax.all_to_all(
            terms.reshape(nf, band, width), "fsdp", split_axis=0, concat_axis=0
        )
        return jnp.sum(spread.astype(F32), axis=0).astype(BF)
    me = lax.axis_index("fsdp")
    total = lax.dynamic_slice(terms, (me * band, 0), (band, width)).astype(F32)
    for flip in range(1, nf):
        sent = lax.dynamic_slice(terms, ((me ^ flip) * band, 0), (band, width))
        total = total + lax.ppermute(sent, "fsdp", [(e, e ^ flip) for e in range(nf)]).astype(F32)
    return total.astype(BF)


def dot_on(left, right, left_dim, right_dim):
    return lax.dot_general(
        left, right, (((left_dim,), (right_dim,)), ((), ())), preferred_element_type=F32
    )


def pick_grad(sources, flags, at):
    if len(sources) == 1:
        return sources[0][...]
    return jnp.where(flags[at] > 0, sources[1][...], sources[0][...])


def update_body(group, count, flags, refs):
    grads = refs[: group * count]
    lefts = refs[group * count : group * (count + 1)]
    rights = refs[group * (count + 1) : group * (count + 2)]
    master_ref, new_ref, low_ref = (refs[group * (count + 2)], refs[-2], refs[-1])
    for j in range(group):
        grad = pick_grad(grads[j * count : (j + 1) * count], flags, pl.program_id(0) * group + j)
        shaped = dot_on(lefts[j][...], grad, 1, 0)
        shaped = dot_on(shaped.astype(BF), rights[j][...], 1, 0)
        power = jnp.sum(jnp.sum(shaped * shaped, axis=1, keepdims=True), axis=0, keepdims=True)
        factor = -RATE * lax.rsqrt(power * (1.0 / (shaped.shape[0] * shaped.shape[1])) + EPSILON)
        at = pl.ds(j * BC, BC)
        fresh = master_ref[:, at] + shaped * factor
        new_ref[:, at] = fresh
        low_ref[:, at] = fresh.astype(BF)


def grad_specs(sources, group, skip, band):
    def spec(j, is_second):
        def index(i, part, kind, column, flags, *more):
            at = (i + skip) * group + j
            own = jnp.where(flags[at] > 0, 1, 0) if len(sources) > 1 else 0
            fits = own if is_second else 1 - own
            return (part[at] * fits, kind[at] * fits, 0, column[at] * fits)

        return pl.BlockSpec((None, None, band, BC), index)

    return [spec(j, n > 0) for j in range(group) for n in range(len(sources))]


def update_blocks(sources, places, roots, left_roots, right_roots, master, start, count, group, into):
    band = master.shape[0]
    skip = start // group

    def root_spec(shape, j):
        def index(i, part, kind, column, flags, root):
            return (root[i * group + j], 0, 0)

        return pl.BlockSpec((None,) + shape, index)

    wide = pl.BlockSpec((band, group * BC), lambda i, *tables: (0, i + skip))
    in_specs = grad_specs(sources, group, 0, band)
    in_specs += [root_spec(left_roots.shape[1:], j) for j in range(group)]
    in_specs += [root_spec(right_roots.shape[1:], j) for j in range(group)]
    in_specs += [wide]
    operands = list(sources) * group + [left_roots] * group + [right_roots] * group + [master]
    tables = list(places) + [roots]
    aliases = {}
    if into is not None:
        aliases = {len(tables) + len(operands) + n: n for n in range(2)}
        in_specs += [pl.BlockSpec(memory_space=pl.ANY)] * 2
        operands += list(into)
    return pl.pallas_call(
        lambda *refs: update_body(group, len(sources), refs[3], refs[5:]),
        grid_spec=pltpu.PrefetchScalarGridSpec(
            num_scalar_prefetch=5,
            grid=(count // group,),
            in_specs=in_specs,
            out_specs=[wide, wide],
        ),
        out_shape=[
            jax.ShapeDtypeStruct(master.shape, F32),
            jax.ShapeDtypeStruct(master.shape, BF),
        ],
        input_output_aliases=aliases,
        compiler_params=pltpu.CompilerParams(vmem_limit_bytes=VMEM_LIMIT),
        name="update_blocks",
    )(*tables, *operands)


def stats_body(group, count, skip, flags, used, refs):
    grads, (left_ref, right_ref) = (refs[: group * count], refs[group * count : group * count + 2])
    grad_out, left_out, right_out = refs[-3:]
    for j in range(group):
        at = (pl.program_id(0) + skip) * group + j
        grad = pick_grad(grads[j * count : (j + 1) * count], flags, at)
        grad = jnp.where(used[at] > 0, grad, jnp.zeros_like(grad))
        grad_out[j] = grad.astype(F32)
        left_out[j] = DECAY * left_ref[j] + (1.0 - DECAY) * dot_on(grad, grad, 1, 1)
        right_out[j] = DECAY * right_ref[j] + (1.0 - DECAY) * dot_on(grad, grad, 0, 0)


def owner_stats(sources, places, used, stat_left, stat_right, start, count, group, into):
    slots, band = (stat_left.shape[0], sources[0].shape[2])
    skip = start // group

    def slab(shape):
        return pl.BlockSpec((group,) + shape, lambda i, *tables: (i + skip, 0, 0))

    shapes = [(band, BC), stat_left.shape[1:], stat_right.shape[1:]]
    in_specs = grad_specs(sources, group, skip, band) + [slab(shapes[1]), slab(shapes[2])]
    operands = list(sources) * group + [stat_left, stat_right]
    tables = list(places) + [used]
    aliases = {}
    if into is not None:
        aliases = {len(tables) + len(operands) + n: n for n in range(3)}
        in_specs += [pl.BlockSpec(memory_space=pl.ANY)] * 3
        operands += list(into)
    return pl.pallas_call(
        lambda *refs: stats_body(group, len(sources), skip, refs[3], refs[4], refs[5:]),
        grid_spec=pltpu.PrefetchScalarGridSpec(
            num_scalar_prefetch=5,
            grid=(count // group,),
            in_specs=in_specs,
            out_specs=[slab(shape) for shape in shapes],
        ),
        out_shape=[jax.ShapeDtypeStruct((slots,) + shape, F32) for shape in shapes],
        input_output_aliases=aliases,
        compiler_params=pltpu.CompilerParams(vmem_limit_bytes=VMEM_LIMIT),
        name="owner_stats",
    )(*tables, *operands)


KEY_SHARDS = 8
TO_SECOND = [(0, 2), (1, 3), (2, 4), (3, 5)]
TO_NEXT = [(0, 1), (1, 2), (2, 3)]
ONWARDS = [(4, 6), (5, 7)]
ACROSS = [(4, 5), (5, 4), (6, 7), (7, 6)]
FIRST_SOURCE = [-1, -1, 0, 1, 2, 3, 2, 3]
SECOND_SOURCE = [-1, 0, 1, 2, 3, 2, 3, 2]


def backwards(pairs):
    return [(dst, src) for src, dst in pairs]


def pick_static(table, index):
    values = jnp.asarray(table, jnp.int32)
    hit = jnp.arange(len(table), dtype=jnp.int32) == index
    return jnp.sum(jnp.where(hit, values, 0))


def key_slots_of(rows, nf):
    me = lax.axis_index("fsdp")
    step = jnp.arange(rows, dtype=jnp.int32)
    if nf != KEY_SHARDS:
        return jnp.arange(rows * nf, dtype=jnp.int32)
    ids = [me * rows + step]
    for table in (FIRST_SOURCE, SECOND_SOURCE):
        source = pick_static(table, me)
        ids.append(jnp.where(source >= 0, source * rows + step, -1))
    return jnp.concatenate(ids)


def spread_keys(own, nf):
    if nf != KEY_SHARDS:
        return lax.all_gather(own, "fsdp", axis=0, tiled=True)
    second = lax.ppermute(own, "fsdp", TO_SECOND)
    following = lax.ppermute(own, "fsdp", TO_NEXT)
    onward = lax.ppermute(second, "fsdp", ONWARDS)
    crossed = lax.ppermute(second, "fsdp", ACROSS[:2])
    crossed_on = lax.ppermute(onward, "fsdp", ACROSS[2:])
    return jnp.concatenate([own, second + onward, following + crossed + crossed_on], axis=0)


def return_key_grads(terms, rows, nf):
    if nf != KEY_SHARDS:
        return lax.psum_scatter(
            terms.astype(BF), "fsdp", scatter_dimension=0, tiled=True
        ).astype(F32)
    first = terms[rows : 2 * rows]
    second = terms[2 * rows :].astype(BF)
    total = terms[:rows] + lax.ppermute(second, "fsdp", backwards(TO_NEXT)).astype(F32)
    first = first + lax.ppermute(second, "fsdp", ACROSS).astype(F32)
    first = first + lax.ppermute(first.astype(BF), "fsdp", backwards(ONWARDS)).astype(F32)
    return total + lax.ppermute(first.astype(BF), "fsdp", backwards(TO_SECOND)).astype(F32)


def attend(query_low, keys, values, visible):
    scores = jnp.einsum("thd,kd->thk", query_low, keys, preferred_element_type=F32) * SCALE
    scores = jnp.where(visible[:, None, :], scores, MASKED)
    highest = jnp.max(scores, axis=-1, keepdims=True)
    expo = jnp.exp(scores - highest)
    probs = expo / jnp.sum(expo, axis=-1, keepdims=True)
    mixed = jnp.einsum("thk,kd->thd", probs.astype(BF), values, preferred_element_type=F32)
    return (mixed, probs)


def attend_back(query_low, keys, values, probs, low_mixed):
    grad_probs = jnp.einsum("thd,kd->thk", low_mixed, values, preferred_element_type=F32)
    row_dot = jnp.sum(grad_probs * probs, axis=-1, keepdims=True)
    grad_scores = (probs * (grad_probs - row_dot)).astype(BF)
    grad_queries = jnp.einsum("thk,kd->thd", grad_scores, keys, preferred_element_type=F32) * SCALE
    key_terms = (
        jnp.einsum("thk,thd->kd", grad_scores, query_low, preferred_element_type=F32) * SCALE
    )
    value_terms = jnp.einsum("thk,thd->kd", probs.astype(BF), low_mixed, preferred_element_type=F32)
    return (grad_queries, key_terms, value_terms)


def local(
    tokens,
    cotangent,
    lengths,
    master,
    gains,
    gain_stats,
    owner,
    stat_left,
    stat_right,
    root_left,
    root_right,
):
    nd = lax.axis_size("dp")
    nf = lax.axis_size("fsdp")
    dp_me = lax.axis_index("dp")
    core = dp_me % 2
    micros = tokens.shape[0]
    rows = tokens.shape[2]
    count = micros * rows
    band = master.shape[0]
    capacity = stat_left.shape[1]
    first = lax.axis_index("fsdp") * rows
    pre_attn, post_attn, pre_ffw, post_ffw, query_gain, key_gain = split_gains(gains)

    per = -(-FF_BLOCKS // nd)
    width = per * BC
    start = jnp.minimum(dp_me * per, FF_BLOCKS - per)
    fresh = dp_me * per - start
    gate_at = ATTN_BLOCKS * BC

    def columns(at, size):
        return lax.dynamic_slice(master, (0, at), (band, size)).astype(BF)

    def quarters(at, size):
        part = size // nd
        mine = gather_rows(columns(at + dp_me * part, part), nf)
        whole = jnp.zeros((D, size), BF)
        for piece, index in zip(gather_parts(mine, nd), part_owners(nd)):
            whole = lax.dynamic_update_slice(whole, piece, (0, index * part))
        return whole

    w_qkv = quarters(0, QKVW)
    w_out = quarters(QKVW, OUTW)
    gate_cols = columns(gate_at + start * BC, width)
    up_cols = columns(gate_at + FF + start * BC, width)
    down_cols = columns(gate_at + 2 * FF + start * BC, width)
    keep = (jnp.arange(width, dtype=jnp.int32) >= fresh * BC)[None, :]
    down_cols = jnp.where(keep, down_cols, jnp.zeros_like(down_cols))
    w_gate = lax.all_gather(gate_cols, "fsdp", axis=0, tiled=True)
    w_up = lax.all_gather(up_cols, "fsdp", axis=0, tiled=True)
    w_down = lax.all_gather(down_cols, "fsdp", axis=0, tiled=True)

    flat_in = tokens.astype(F32).reshape(count, D)
    normed = rms_gain(flat_in, pre_attn).astype(BF)
    projected = dot_nn(normed, w_qkv)
    queries = projected[:, :OUTW].reshape(count, HEADS, HD)
    keys = projected[:, OUTW : OUTW + HD]
    values = projected[:, OUTW + HD :]
    slots = first + jnp.arange(rows, dtype=jnp.int32)
    _, positions = slot_layout(slots)
    cosine, sine = rope_tables(positions)
    cosine, sine = (jnp.tile(cosine, (micros, 1)), jnp.tile(sine, (micros, 1)))
    rot_queries, rot_keys = prepare_heads(queries, keys, query_gain, key_gain, cosine, sine)
    query_low = rot_queries.astype(BF).reshape(micros, rows, HEADS, HD)
    own_keys = jnp.concatenate([rot_keys.astype(BF), values.astype(BF)], axis=1)
    key_buffers = [spread_keys(own_keys[m * rows : (m + 1) * rows], nf) for m in range(micros)]
    key_slots = key_slots_of(rows, nf)
    keys_all = [buffer[:, :HD] for buffer in key_buffers]
    values_all = [buffer[:, HD:] for buffer in key_buffers]
    all_probs, all_attended = [], []
    for m in range(micros):
        visible = visibility(slots, key_slots, lengths[m, 0])
        mixed, probs = attend(query_low[m], keys_all[m], values_all[m], visible)
        all_probs.append(probs)
        all_attended.append(mixed.reshape(rows, OUTW).astype(BF))

    half = (nd // 2) * rows
    outputs, saved, gathered_in, gathered_two, hiddens, low_gates, low_ups = [], [], [], [], [], [], []
    grad_resids, gain_terms, low_ones = [], [], []
    for m in range(micros):
        part_in = flat_in[m * rows : (m + 1) * rows]
        branch_one = dot_nt(all_attended[m], w_out)
        resid = part_in + rms_gain(branch_one, post_attn)
        ffw_in = rms_gain(resid, pre_ffw).astype(BF)
        every_in = gather_dp(ffw_in, nd)
        gate = dot_nn(every_in, w_gate)
        up = dot_nn(every_in, w_up)
        hidden = (jax.nn.gelu(gate, approximate=True) * up).astype(BF)
        partial = dot_nt(hidden, w_down)
        branch_two = scatter_sum_dp(partial[:half], partial[half:], nd)
        outputs.append((resid + rms_gain(branch_two, post_ffw)).astype(BF))
        gathered_in.append(every_in)
        hiddens.append(hidden)
        saved.append((branch_one, resid, gate, up, branch_two))
    for m in range(micros):
        branch_one, resid, gate, up, branch_two = saved[m]
        upstream = cotangent[m, 0].astype(F32)
        grad_two, grad_post_ffw = jax.vjp(rms_gain, branch_two, post_ffw)[1](upstream)
        every_two = gather_dp(grad_two.astype(BF), nd)
        grad_hidden = dot_nn(every_two, w_down)
        grad_gate, grad_up = jax.vjp(
            lambda gate_in, up_in: jax.nn.gelu(gate_in, approximate=True) * up_in, gate, up
        )[1](grad_hidden)
        low_gate, low_up = (grad_gate.astype(BF), grad_up.astype(BF))
        partial = dot_nt(low_gate, w_gate) + dot_nt(low_up, w_up)
        grad_ffw_in = scatter_sum_dp(partial[:half], partial[half:], nd)
        grad_resid, grad_pre_ffw = jax.vjp(rms_gain, resid, pre_ffw)[1](grad_ffw_in)
        grad_resid = upstream + grad_resid
        grad_one, grad_post_attn = jax.vjp(rms_gain, branch_one, post_attn)[1](grad_resid)
        gathered_two.append(every_two)
        low_gates.append(low_gate)
        low_ups.append(low_up)
        grad_resids.append(grad_resid)
        low_ones.append(grad_one.astype(BF))
        gain_terms.append((grad_post_attn, grad_pre_ffw, grad_post_ffw))

    def weight_term(lefts, rights):
        term = dot_tn(jnp.concatenate(lefts, axis=0), jnp.concatenate(rights, axis=0))
        return term.astype(BF)

    down_term = weight_term(gathered_two, hiddens)
    ff_bands = [
        reduce_rows(weight_term(gathered_in, low_gates), nf),
        reduce_rows(weight_term(gathered_in, low_ups), nf),
        lax.psum_scatter(down_term, "fsdp", scatter_dimension=0, tiled=True),
    ]

    def gather_relative(bands):
        parts = [gather_parts(part, nd) for part in bands]
        out = jnp.zeros((nd, len(bands)) + bands[0].shape, BF)
        for kind, pieces in enumerate(parts):
            for place, piece in enumerate(pieces):
                out = lax.dynamic_update_slice(
                    out, piece[None, None], (place, kind) + (0,) * piece.ndim
                )
        return out

    ff_all = gather_relative(ff_bands)

    low_one = jnp.concatenate(low_ones, axis=0)
    attended = jnp.concatenate(all_attended, axis=0)
    low_mixed = dot_nn(low_one, w_out).astype(BF).reshape(micros, rows, HEADS, HD)
    grad_queries, key_terms = [], []
    for m in range(micros):
        for_queries, for_keys, for_values = attend_back(
            query_low[m], keys_all[m], values_all[m], all_probs[m], low_mixed[m]
        )
        grad_queries.append(for_queries)
        terms = jnp.concatenate([for_keys, for_values], axis=1)
        key_terms.append(return_key_grads(terms, rows, nf))
    own_terms = jnp.concatenate(key_terms, axis=0)
    grad_keys, grad_values = (own_terms[:, :HD], own_terms[:, HD:])

    def heads_only(query_in, key_in, query_scale, key_scale):
        return prepare_heads(query_in, key_in, query_scale, key_scale, cosine, sine)

    pull_heads = jax.vjp(heads_only, queries, keys, query_gain, key_gain)[1]
    grad_query_pre, grad_key_pre, grad_query_gain, grad_key_gain = pull_heads(
        (jnp.concatenate(grad_queries, axis=0), grad_keys)
    )
    low_projected = jnp.concatenate(
        [grad_query_pre.reshape(count, OUTW), grad_key_pre, grad_values], axis=1
    ).astype(BF)
    grad_normed = dot_nt(low_projected, w_qkv)
    grad_in, grad_pre_attn = jax.vjp(rms_gain, flat_in, pre_attn)[1](grad_normed)
    input_grad = (jnp.concatenate(grad_resids, axis=0) + grad_in).astype(BF)

    attn_per = -(-ATTN_BLOCKS // nd)
    attn_width = attn_per * BC
    attn_term = jnp.concatenate([dot_tn(normed, low_projected), dot_tn(low_one, attended)], axis=1)
    attn_term = jnp.pad(attn_term, ((0, 0), (0, nd * attn_width - ATTN_BLOCKS * BC)))

    def owner_columns(index):
        return lax.dynamic_slice(attn_term, (0, index * attn_width), (D, attn_width))

    owners_at = part_owners(nd)
    attn_sum = scatter_sum_dp(
        jnp.concatenate([owner_columns(e) for e in owners_at[: nd // 2]], axis=0),
        jnp.concatenate([owner_columns(e) for e in owners_at[nd // 2 :]], axis=0),
        nd,
    )
    attn_band = direct_reduce(attn_sum.astype(BF), nf)
    attn_all = gather_relative([attn_band])

    def relative(index):
        nx = nd // 2
        flip = (index % 2) ^ core
        return flip * nx + (dp_me // 2 + nx - index // 2) % nx

    ff_index = np.arange(3 * FF_BLOCKS)
    ff_dp = np.minimum(ff_index % FF_BLOCKS // per, nd - 1)
    ff_column = ff_index % FF_BLOCKS - np.minimum(ff_dp * per, FF_BLOCKS - per)
    attn_index = np.arange(ATTN_BLOCKS)
    part_of = relative(
        jnp.asarray(np.concatenate([attn_index // attn_per, ff_dp]).astype(np.int32))
    )
    kind_of = jnp.asarray(
        np.concatenate([np.zeros(ATTN_BLOCKS), ff_index // FF_BLOCKS]).astype(np.int32)
    )
    column_of = jnp.asarray(np.concatenate([attn_index % attn_per, ff_column]).astype(np.int32))

    owners = owner[:, 0]
    index = jnp.arange(NBLK, dtype=jnp.int32)
    before = (owners[:, None] == owners[None, :]) & (index[None, :] < index[:, None])
    ranks = jnp.sum(before.astype(jnp.int32), axis=1)
    my_slots = jnp.arange(capacity, dtype=jnp.int32)
    mine = (owners[None, :] == dp_me) & (ranks[None, :] == my_slots[:, None])
    used = jnp.sum(mine.astype(jnp.int32), axis=1)

    def of_slot(values):
        return jnp.sum(jnp.where(mine, values[None, :], 0), axis=1)

    root_of = relative(owners) * capacity + ranks
    every_left = gather_relative([after(root_left[0], w_qkv)])
    every_left = every_left.reshape((nd * capacity,) + root_left.shape[2:])
    every_right = gather_relative([after(root_right[0], w_qkv)])
    every_right = every_right.reshape((nd * capacity,) + root_right.shape[2:])

    is_attn = (index < ATTN_BLOCKS).astype(jnp.int32)
    places = (part_of, kind_of, column_of, is_attn)
    early = tuple(table[LATE:] for table in places)
    late = tuple(table[:LATE] for table in places)
    root_args = (every_left, every_right, master)
    fresh_arrays = update_blocks(
        [ff_all], early, root_of[LATE:], *root_args, LATE, NBLK - LATE, 7, None
    )
    slot_places = tuple(of_slot(table) for table in places)
    group = 3 if (capacity - LATE) % 3 == 0 else 1
    stat_args = (slot_places, used, stat_left[0], stat_right[0])
    fresh_stats = owner_stats([ff_all], *stat_args, LATE, capacity - LATE, group, None)
    both = [ff_all, attn_all]
    new_master, new_weights = update_blocks(
        both, late, root_of[:LATE], *root_args, 0, LATE, 7, fresh_arrays
    )
    slot_grads, new_left, new_right = owner_stats(both, *stat_args, 0, LATE, group, fresh_stats)

    post_attn_sum = sum(entry[0] for entry in gain_terms)
    pre_ffw_sum = sum(entry[1] for entry in gain_terms)
    post_ffw_sum = sum(entry[2] for entry in gain_terms)
    gain_sum = jnp.concatenate(
        [grad_pre_attn, post_attn_sum, pre_ffw_sum, post_ffw_sum, grad_query_gain, grad_key_gain]
    )
    gain_grad = sum_everywhere(gain_sum, nd, nf)
    new_gain_stats = DECAY * gain_stats + (1.0 - DECAY) * gain_grad * gain_grad
    gain_change = -GAIN_RATE * gain_grad * lax.rsqrt(new_gain_stats)
    return (
        jnp.stack(outputs)[:, None],
        input_grad.reshape(micros, 1, rows, D),
        slot_grads[None],
        gain_grad,
        new_left[None],
        new_right[None],
        new_master,
        new_weights,
        new_gain_stats,
        gain_change,
    )


def solution(mesh):
    in_specs = (
        P(None, "dp", "fsdp", None),
        P(None, "dp", "fsdp", None),
        P(None, "dp", None),
        P("fsdp", None),
        P(),
        P(),
        P("fsdp", None),
        P("fsdp", "dp", None, None),
        P("fsdp", "dp", None, None),
        P("fsdp", "dp", None, None),
        P("fsdp", "dp", None, None),
    )
    out_specs = (
        P(None, "dp", "fsdp", None),
        P(None, "dp", "fsdp", None),
        P("fsdp", "dp", None, None),
        P(),
        P("fsdp", "dp", None, None),
        P("fsdp", "dp", None, None),
        P("fsdp", None),
        P("fsdp", None),
        P(),
        P(),
    )
    return jax.shard_map(local, mesh=mesh, in_specs=in_specs, out_specs=out_specs, check_vma=False)
```

```python
import jax
import jax.numpy as jnp
import numpy as np
from jax import lax
from jax.experimental import pallas as pl
from jax.experimental.pallas import tpu as pltpu
from jax.sharding import PartitionSpec as P

D = 1152
HEADS = 4
HD = 256
FF = 6912
WIN = 512
PROMPT = 1024
CONT = 8
CLEN = 128
BC = 128
GLEN = 2048
QKVW = 1536
OUTW = HEADS * HD
NBLK = 182
ATTN_BLOCKS = (QKVW + OUTW) // BC
FF_BLOCKS = FF // BC

EPSILON = 1e-06
MASKED = -1e30
RATE = 0.02
GAIN_RATE = 0.05
DECAY = 0.5
SCALE = HD ** (-0.5)
DIRECT_MAX = 8
LATE = 21
VMEM_LIMIT = 40 * 1024 * 1024
BF = jnp.bfloat16
F32 = jnp.float32


def rms_gain(values, gain):
    return values * lax.rsqrt(jnp.mean(values * values, axis=-1, keepdims=True) + EPSILON) * gain


def rope_tables(positions):
    half_width = HD // 2
    freqs = 10000.0 ** (-2.0 * jnp.arange(half_width, dtype=F32) / HD)
    angles = positions.astype(F32)[:, None] * freqs[None, :]
    return (jnp.cos(angles), jnp.sin(angles))


def rotate(values, cosine, sine):
    half_width = values.shape[-1] // 2
    first_half = values[..., :half_width]
    second_half = values[..., half_width:]
    return jnp.concatenate(
        [first_half * cosine - second_half * sine, second_half * cosine + first_half * sine],
        axis=-1,
    )


def slot_layout(slots):
    in_prompt = slots < PROMPT
    offset = slots - PROMPT
    segment = jnp.where(in_prompt, -1, offset // CLEN)
    position = jnp.where(in_prompt, slots, PROMPT + offset % CLEN)
    return (segment, position)


def visibility(query_slots, key_slots, lens):
    query_seg, query_pos = slot_layout(query_slots)
    key_seg, key_pos = slot_layout(key_slots)
    picks = key_seg[:, None] == jnp.arange(CONT, dtype=jnp.int32)[None, :]
    key_len = jnp.sum(jnp.where(picks, lens[None, :], 0), axis=1)
    key_used = (key_seg < 0) | (key_pos - PROMPT < key_len)
    distance = query_pos[:, None] - key_pos[None, :]
    same_part = (key_seg[None, :] < 0) | (key_seg[None, :] == query_seg[:, None])
    present = key_slots >= 0
    return (distance >= 0) & (distance < WIN) & same_part & (key_used & present)[None, :]


def split_gains(gains):
    return (
        gains[:D],
        gains[D : 2 * D],
        gains[2 * D : 3 * D],
        gains[3 * D : 4 * D],
        gains[4 * D : 4 * D + HD],
        gains[4 * D + HD :],
    )


def prepare_heads(queries, keys, query_gain, key_gain, cosine, sine):
    rot_queries = rotate(rms_gain(queries, query_gain), cosine[:, None, :], sine[:, None, :])
    rot_keys = rotate(rms_gain(keys, key_gain), cosine, sine)
    return (rot_queries, rot_keys)


def dot_nn(left, right):
    return jnp.dot(left, right, preferred_element_type=F32)


def dot_nt(left, right):
    return lax.dot_general(left, right, (((1,), (1,)), ((), ())), preferred_element_type=F32)


def dot_tn(left, right):
    return lax.dot_general(left, right, (((0,), (0,)), ((), ())), preferred_element_type=F32)


def swap_core(value, nd):
    return lax.ppermute(value, "dp", [(e, e ^ 1) for e in range(nd)])


def shift_x(value, nd, step):
    nx = nd // 2
    pairs = [(e, ((e // 2 + step) % nx) * 2 + e % 2) for e in range(nd)]
    return lax.ppermute(value, "dp", pairs)


def gather_parts(value, nd):
    mine = [value] + [shift_x(value, nd, k) for k in range(1, nd // 2)]
    return mine + [swap_core(part, nd) for part in mine]


def gather_dp(value, nd):
    return jnp.concatenate(gather_parts(value, nd), axis=0)


def part_owners(nd):
    nx = nd // 2
    me = lax.axis_index("dp")
    x, core = me // 2, me % 2
    out = []
    for flip in range(2):
        for k in range(nx):
            out.append(((x + nx - k) % nx) * 2 + (core if flip == 0 else 1 - core))
    return out


def scatter_sum_dp(own_half, other_half, nd):
    nx = nd // 2
    received = swap_core(other_half.astype(BF), nd)
    total = own_half + received.astype(F32)
    rows = total.shape[0] // nx
    result = total[:rows]
    for k in range(1, nx):
        sent = total[k * rows : (k + 1) * rows].astype(BF)
        result = result + shift_x(sent, nd, nx - k).astype(F32)
    return result


def sum_everywhere(value, nd, nf):
    for axis, count in (("dp", nd), ("fsdp", nf)):
        step = 1
        while step < count:
            value = value + lax.ppermute(value, axis, [(e, e ^ step) for e in range(count)])
            step *= 2
    return value


def after(value, *others):
    return lax.optimization_barrier((value,) + others)[0]


def swap_fsdp(value, flip, nf):
    return lax.ppermute(value, "fsdp", [(e, e ^ flip) for e in range(nf)])


def gather_rows(own, nf, ties=()):
    if nf > DIRECT_MAX:
        return lax.all_gather(own, "fsdp", axis=0, tiled=True)
    me = lax.axis_index("fsdp")
    band, width = own.shape
    straight = [own] + [swap_fsdp(own, flip, nf) for flip in range(2, nf, 2)]
    passed = [own] + [after(part, *ties) if ties else part for part in straight[1:]]
    crossed = [swap_fsdp(part, 1, nf) for part in passed]
    whole = jnp.zeros((nf * band, width), own.dtype)
    for k in range(nf // 2):
        whole = lax.dynamic_update_slice(whole, straight[k], ((me ^ (2 * k)) * band, 0))
        whole = lax.dynamic_update_slice(whole, crossed[k], ((me ^ (2 * k + 1)) * band, 0))
    return whole


def direct_reduce(terms, nf):
    band, width = (terms.shape[0] // nf, terms.shape[1])
    spread = lax.all_to_all(terms.reshape(nf, band, width), "fsdp", split_axis=0, concat_axis=0)
    return jnp.sum(spread.astype(F32), axis=0).astype(BF)


def dot_on(left, right, left_dim, right_dim):
    return lax.dot_general(
        left, right, (((left_dim,), (right_dim,)), ((), ())), preferred_element_type=F32
    )


def pick_grad(sources, flags, at):
    if len(sources) == 1:
        return sources[0][...]
    return jnp.where(flags[at] > 0, sources[1][...], sources[0][...])


def update_body(group, count, pieces, flags, refs):
    grads = refs[: group * count]
    lefts = refs[group * count : group * (count + pieces)]
    rights = refs[group * (count + pieces) : group * (count + pieces + 1)]
    master_ref, new_ref, low_ref = (refs[group * (count + pieces + 1)], refs[-2], refs[-1])
    base = pl.program_id(0) * group
    shaped = []
    for j in range(group):
        grad = pick_grad(grads[j * count : (j + 1) * count], flags, base + j)
        product = dot_on(lefts[j][...], grad[: lefts[j].shape[1]], 1, 0)
        if pieces > 1:
            product = product + dot_on(lefts[group + j][...], grad[lefts[j].shape[1] :], 0, 0)
        shaped.append(product.astype(BF))
    shaped = [dot_on(shaped[j], rights[j][...], 1, 0) for j in range(group)]
    scale = 1.0 / (shaped[0].shape[0] * shaped[0].shape[1])
    powers = [jnp.sum(jnp.sum(s * s, axis=0, keepdims=True), axis=1, keepdims=True) for s in shaped]
    factors = [-RATE * lax.rsqrt(power * scale + EPSILON) for power in powers]
    for j in range(group):
        at = pl.ds(j * BC, BC)
        fresh = master_ref[:, at] + shaped[j] * factors[j]
        new_ref[:, at] = fresh
        low_ref[:, at] = fresh.astype(BF)


def grad_specs(sources, group, skip, band):
    def spec(j, is_second):
        def index(i, part, kind, column, flags, *more):
            at = (i + skip) * group + j
            own = jnp.where(flags[at] > 0, 1, 0) if len(sources) > 1 else 0
            fits = own if is_second else 1 - own
            return (part[at] * fits, kind[at] * fits, 0, column[at] * fits)

        return pl.BlockSpec((None, None, band, BC), index)

    return [spec(j, n > 0) for j in range(group) for n in range(len(sources))]


def update_blocks(sources, places, roots, left_roots, right_roots, master, start, count, group, into):
    band = master.shape[0]
    skip = start // group

    def root_spec(shape, j):
        def index(i, part, kind, column, flags, root):
            return (root[i * group + j], 0, 0)

        return pl.BlockSpec((None,) + shape, index)

    wide = pl.BlockSpec((band, group * BC), lambda i, *tables: (0, i + skip))
    in_specs = grad_specs(sources, group, 0, band)
    in_specs += [root_spec(left.shape[1:], j) for left in left_roots for j in range(group)]
    in_specs += [root_spec(right_roots.shape[1:], j) for j in range(group)]
    in_specs += [wide]
    operands = list(sources) * group + [left for left in left_roots for _ in range(group)]
    operands += [right_roots] * group + [master]
    tables = list(places) + [roots]
    aliases = {}
    if into is not None:
        aliases = {len(tables) + len(operands) + n: n for n in range(2)}
        in_specs += [pl.BlockSpec(memory_space=pl.ANY)] * 2
        operands += list(into)
    return pl.pallas_call(
        lambda *refs: update_body(group, len(sources), len(left_roots), refs[3], refs[5:]),
        grid_spec=pltpu.PrefetchScalarGridSpec(
            num_scalar_prefetch=5,
            grid=(count // group,),
            in_specs=in_specs,
            out_specs=[wide, wide],
        ),
        out_shape=[
            jax.ShapeDtypeStruct(master.shape, F32),
            jax.ShapeDtypeStruct(master.shape, BF),
        ],
        input_output_aliases=aliases,
        compiler_params=pltpu.CompilerParams(vmem_limit_bytes=VMEM_LIMIT),
        name="update_blocks",
    )(*tables, *operands)


def stats_body(group, count, skip, flags, used, refs):
    grads, (left_ref, right_ref) = (refs[: group * count], refs[group * count : group * count + 2])
    grad_out, left_out, right_out = refs[-3:]
    for j in range(group):
        at = (pl.program_id(0) + skip) * group + j
        grad = pick_grad(grads[j * count : (j + 1) * count], flags, at)
        grad = jnp.where(used[at] > 0, grad, jnp.zeros_like(grad))
        grad_out[j] = grad.astype(F32)
        left_out[j] = DECAY * left_ref[j] + (1.0 - DECAY) * dot_on(grad, grad, 1, 1)
        right_out[j] = DECAY * right_ref[j] + (1.0 - DECAY) * dot_on(grad, grad, 0, 0)


def owner_stats(sources, places, used, stat_left, stat_right, start, count, group, into):
    slots, band = (stat_left.shape[0], sources[0].shape[2])
    skip = start // group

    def slab(shape):
        return pl.BlockSpec((group,) + shape, lambda i, *tables: (i + skip, 0, 0))

    shapes = [(band, BC), stat_left.shape[1:], stat_right.shape[1:]]
    in_specs = grad_specs(sources, group, skip, band) + [slab(shapes[1]), slab(shapes[2])]
    operands = list(sources) * group + [stat_left, stat_right]
    tables = list(places) + [used]
    aliases = {}
    if into is not None:
        aliases = {len(tables) + len(operands) + n: n for n in range(3)}
        in_specs += [pl.BlockSpec(memory_space=pl.ANY)] * 3
        operands += list(into)
    return pl.pallas_call(
        lambda *refs: stats_body(group, len(sources), skip, refs[3], refs[4], refs[5:]),
        grid_spec=pltpu.PrefetchScalarGridSpec(
            num_scalar_prefetch=5,
            grid=(count // group,),
            in_specs=in_specs,
            out_specs=[slab(shape) for shape in shapes],
        ),
        out_shape=[jax.ShapeDtypeStruct((slots,) + shape, F32) for shape in shapes],
        input_output_aliases=aliases,
        compiler_params=pltpu.CompilerParams(vmem_limit_bytes=VMEM_LIMIT),
        name="owner_stats",
    )(*tables, *operands)


KEY_SHARDS = 8
TO_SECOND = [(0, 2), (1, 3), (2, 4), (3, 5)]
TO_NEXT = [(0, 1), (1, 2), (2, 3)]
ONWARDS = [(4, 6), (5, 7)]
ACROSS = [(4, 5), (5, 4), (6, 7), (7, 6)]
FIRST_SOURCE = [-1, -1, 0, 1, 2, 3, 2, 3]
SECOND_SOURCE = [-1, 0, 1, 2, 3, 2, 3, 2]


def backwards(pairs):
    return [(dst, src) for src, dst in pairs]


def pick_static(table, index):
    values = jnp.asarray(table, jnp.int32)
    hit = jnp.arange(len(table), dtype=jnp.int32) == index
    return jnp.sum(jnp.where(hit, values, 0))


def key_slots_of(rows, nf):
    me = lax.axis_index("fsdp")
    step = jnp.arange(rows, dtype=jnp.int32)
    if nf != KEY_SHARDS:
        return jnp.arange(rows * nf, dtype=jnp.int32)
    ids = [me * rows + step]
    for table in (FIRST_SOURCE, SECOND_SOURCE):
        source = pick_static(table, me)
        ids.append(jnp.where(source >= 0, source * rows + step, -1))
    return jnp.concatenate(ids)


def spread_keys(own, nf):
    if nf != KEY_SHARDS:
        return lax.all_gather(own, "fsdp", axis=0, tiled=True)
    second = lax.ppermute(own, "fsdp", TO_SECOND)
    following = lax.ppermute(own, "fsdp", TO_NEXT)
    onward = lax.ppermute(second, "fsdp", ONWARDS)
    crossed = lax.ppermute(second, "fsdp", ACROSS[:2])
    crossed_on = lax.ppermute(onward, "fsdp", ACROSS[2:])
    return jnp.concatenate([own, second + onward, following + crossed + crossed_on], axis=0)


def return_key_grads(terms, rows, nf):
    if nf != KEY_SHARDS:
        return lax.psum_scatter(
            terms.astype(BF), "fsdp", scatter_dimension=0, tiled=True
        ).astype(F32)
    first = terms[rows : 2 * rows]
    second = terms[2 * rows :].astype(BF)
    total = terms[:rows] + lax.ppermute(second, "fsdp", backwards(TO_NEXT)).astype(F32)
    first = first + lax.ppermute(second, "fsdp", ACROSS).astype(F32)
    first = first + lax.ppermute(first.astype(BF), "fsdp", backwards(ONWARDS)).astype(F32)
    return total + lax.ppermute(first.astype(BF), "fsdp", backwards(TO_SECOND)).astype(F32)


def attend(query_low, keys, values, visible):
    scores = jnp.einsum("thd,kd->thk", query_low, keys, preferred_element_type=F32) * SCALE
    scores = jnp.where(visible[:, None, :], scores, MASKED)
    highest = jnp.max(scores, axis=-1, keepdims=True)
    expo = jnp.exp(scores - highest)
    probs = expo / jnp.sum(expo, axis=-1, keepdims=True)
    mixed = jnp.einsum("thk,kd->thd", probs.astype(BF), values, preferred_element_type=F32)
    return (mixed, probs)


def attend_back(query_low, keys, values, probs, low_mixed):
    grad_probs = jnp.einsum("thd,kd->thk", low_mixed, values, preferred_element_type=F32)
    row_dot = jnp.sum(grad_probs * probs, axis=-1, keepdims=True)
    grad_scores = (probs * (grad_probs - row_dot)).astype(BF)
    grad_queries = jnp.einsum("thk,kd->thd", grad_scores, keys, preferred_element_type=F32) * SCALE
    key_terms = (
        jnp.einsum("thk,thd->kd", grad_scores, query_low, preferred_element_type=F32) * SCALE
    )
    value_terms = jnp.einsum("thk,thd->kd", probs.astype(BF), low_mixed, preferred_element_type=F32)
    return (grad_queries, key_terms, value_terms)


def local(
    tokens,
    cotangent,
    lengths,
    master,
    gains,
    gain_stats,
    owner,
    stat_left,
    stat_right,
    root_left,
    root_right,
):
    nd = lax.axis_size("dp")
    nf = lax.axis_size("fsdp")
    dp_me = lax.axis_index("dp")
    core = dp_me % 2
    micros = tokens.shape[0]
    rows = tokens.shape[2]
    count = micros * rows
    band = master.shape[0]
    capacity = stat_left.shape[1]
    first = lax.axis_index("fsdp") * rows
    pre_attn, post_attn, pre_ffw, post_ffw, query_gain, key_gain = split_gains(gains)

    per = -(-FF_BLOCKS // nd)
    width = per * BC
    start = jnp.minimum(dp_me * per, FF_BLOCKS - per)
    fresh = dp_me * per - start
    gate_at = ATTN_BLOCKS * BC

    def columns(at, size):
        return lax.dynamic_slice(master, (0, at), (band, size)).astype(BF)

    def gather_relative(bands, *ties):
        parts = [gather_parts(part, nd) for part in bands]
        if ties:
            parts = [[after(piece, *ties) for piece in pieces] for pieces in parts]
        out = jnp.zeros((nd, len(bands)) + bands[0].shape, BF)
        for kind, pieces in enumerate(parts):
            for place, piece in enumerate(pieces):
                out = lax.dynamic_update_slice(
                    out, piece[None, None], (place, kind) + (0,) * piece.ndim
                )
        return out

    def gather_columns(bands):
        out = jnp.zeros((nd, 1, band, sum(part.shape[1] for part in bands)), BF)
        at = 0
        for part in bands:
            for place, piece in enumerate(gather_parts(part, nd)):
                out = lax.dynamic_update_slice(out, piece[None, None], (place, 0, 0, at))
            at += part.shape[1]
        return out

    def halves(at, size, first_ties, next_ties):
        part = size // 2
        cols = columns(at + core * part, part)
        mine = gather_rows(after(cols, *first_ties) if first_ties else cols, nf, next_ties)
        whole = jnp.zeros((D, size), BF)
        whole = lax.dynamic_update_slice(whole, mine, (0, core * part))
        return lax.dynamic_update_slice(whole, swap_core(mine, nd), (0, (1 - core) * part))

    w_qkv = halves(0, QKVW, (), ())
    gate_cols = columns(gate_at + start * BC, width)
    up_cols = columns(gate_at + FF + start * BC, width)
    down_cols = columns(gate_at + 2 * FF + start * BC, width)
    keep = (jnp.arange(width, dtype=jnp.int32) >= fresh * BC)[None, :]
    down_cols = jnp.where(keep, down_cols, jnp.zeros_like(down_cols))
    both_cols = jnp.concatenate([gate_cols, up_cols], axis=1)
    w_both = lax.all_gather(both_cols, "fsdp", axis=0, tiled=True)
    w_gate, w_up = (w_both[:, :width], w_both[:, width:])
    w_down = lax.all_gather(down_cols, "fsdp", axis=0, tiled=True)

    flat_in = tokens.astype(F32).reshape(count, D)
    normed = rms_gain(flat_in, pre_attn).astype(BF)
    projected = dot_nn(normed, w_qkv)
    queries = projected[:, :OUTW].reshape(count, HEADS, HD)
    keys = projected[:, OUTW : OUTW + HD]
    values = projected[:, OUTW + HD :]
    slots = first + jnp.arange(rows, dtype=jnp.int32)
    _, positions = slot_layout(slots)
    cosine, sine = rope_tables(positions)
    cosine, sine = (jnp.tile(cosine, (micros, 1)), jnp.tile(sine, (micros, 1)))
    rot_queries, rot_keys = prepare_heads(queries, keys, query_gain, key_gain, cosine, sine)
    query_low = rot_queries.astype(BF).reshape(micros, rows, HEADS, HD)
    own_keys = jnp.concatenate([rot_keys.astype(BF), values.astype(BF)], axis=1)
    key_buffers = [spread_keys(own_keys[m * rows : (m + 1) * rows], nf) for m in range(micros)]
    key_slots = key_slots_of(rows, nf)
    w_out = halves(QKVW, OUTW, (projected,), (key_buffers[0],))
    keys_all = [buffer[:, :HD] for buffer in key_buffers]
    values_all = [buffer[:, HD:] for buffer in key_buffers]
    all_probs, all_attended = [], []
    for m in range(micros):
        visible = visibility(slots, key_slots, lengths[m, 0])
        mixed, probs = attend(query_low[m], keys_all[m], values_all[m], visible)
        all_probs.append(probs)
        all_attended.append(mixed.reshape(rows, OUTW).astype(BF))

    half = (nd // 2) * rows
    outputs, saved, gathered_in, gathered_two, hiddens, low_gates, low_ups = [], [], [], [], [], [], []
    grad_resids, gain_terms, low_ones = [], [], []
    for m in range(micros):
        part_in = flat_in[m * rows : (m + 1) * rows]
        branch_one = dot_nt(all_attended[m], w_out)
        resid = part_in + rms_gain(branch_one, post_attn)
        ffw_in = rms_gain(resid, pre_ffw).astype(BF)
        gathered_in.append(gather_dp(ffw_in, nd))
        saved.append([branch_one, resid])
    partials = []
    for m in range(micros):
        every_in = gathered_in[m]
        if m:
            every_in = after(every_in, hiddens[-1])
        gate = dot_nn(every_in, w_gate)
        up = dot_nn(every_in, w_up)
        hidden = (jax.nn.gelu(gate, approximate=True) * up).astype(BF)
        hiddens.append(hidden)
        saved[m] += [gate, up]
    for m in range(micros):
        hidden = after(hiddens[m], partials[-1] if m else hiddens[-1])
        partials.append(dot_nt(hidden, w_down))
    last = partials[-1]
    for m in range(micros):
        branch_one, resid, gate, up = saved[m]
        branch_two = scatter_sum_dp(partials[m][:half], partials[m][half:], nd)
        outputs.append((resid + rms_gain(branch_two, post_ffw)).astype(BF))
        upstream = cotangent[m, 0].astype(F32)
        grad_two, grad_post_ffw = jax.vjp(rms_gain, branch_two, post_ffw)[1](upstream)
        gathered_two.append(gather_dp(grad_two.astype(BF), nd))
        saved[m] += [upstream, grad_post_ffw]
    for m in range(micros):
        branch_one, resid, gate, up, upstream, grad_post_ffw = saved[m]
        grad_hidden = dot_nn(after(gathered_two[m], last), w_down)
        grad_gate, grad_up = jax.vjp(
            lambda gate_in, up_in: jax.nn.gelu(gate_in, approximate=True) * up_in, gate, up
        )[1](grad_hidden)
        low_gates.append(grad_gate.astype(BF))
        low_ups.append(grad_up.astype(BF))
        last = low_ups[-1]

    def weight_term(lefts, rights, follow):
        left = jnp.concatenate(lefts, axis=0)
        term = dot_tn(after(left, *follow), jnp.concatenate(rights, axis=0))
        return term.astype(BF)

    def from_x(root, *ties):
        root = after(root, *ties)
        return [root] + [shift_x(root, nd, k) for k in range(1, nd // 2)]

    right_mine = from_x(root_right[0], *gathered_two)
    down_term = weight_term(gathered_two, hiddens, (last,))
    def sum_rows(term):
        return lax.psum_scatter(term, "fsdp", scatter_dimension=0, tiled=True)

    down_band = sum_rows(down_term)
    last = down_term
    for m in range(micros):
        branch_one, resid, gate, up, upstream, grad_post_ffw = saved[m]
        ties = [last] if m else [last] + right_mine[1:]
        partial = dot_nt(after(low_gates[m], *ties), w_gate) + dot_nt(low_ups[m], w_up)
        last = partial
        grad_ffw_in = scatter_sum_dp(partial[:half], partial[half:], nd)
        grad_resid, grad_pre_ffw = jax.vjp(rms_gain, resid, pre_ffw)[1](grad_ffw_in)
        grad_resid = upstream + grad_resid
        grad_one, grad_post_attn = jax.vjp(rms_gain, branch_one, post_attn)[1](grad_resid)
        grad_resids.append(grad_resid)
        low_ones.append(grad_one.astype(BF))
        gain_terms.append((grad_post_attn, grad_pre_ffw, grad_post_ffw))
    gate_term = weight_term(gathered_in, low_gates, (last,))
    up_term = weight_term(gathered_in, low_ups, (gate_term,))
    both_band = sum_rows(jnp.concatenate([gate_term, up_term], axis=1))

    low_one = jnp.concatenate(low_ones, axis=0)
    attended = jnp.concatenate(all_attended, axis=0)
    left_mine = [from_x(root_left[0, :, :, :BC], low_one)]
    if band > BC:
        left_mine.append(from_x(root_left[0, :, :, BC:].transpose(0, 2, 1), left_mine[0][-1]))
    low_mixed = dot_nn(after(low_one, up_term), w_out).astype(BF).reshape(micros, rows, HEADS, HD)
    grad_queries, key_terms = [], []
    for m in range(micros):
        for_queries, for_keys, for_values = attend_back(
            query_low[m], keys_all[m], values_all[m], all_probs[m], low_mixed[m]
        )
        grad_queries.append(for_queries)
        terms = jnp.concatenate([for_keys, for_values], axis=1)
        key_terms.append(return_key_grads(terms, rows, nf))
        last = terms
    own_terms = jnp.concatenate(key_terms, axis=0)
    out_term = dot_tn(after(low_one, last), attended)
    grad_keys, grad_values = (own_terms[:, :HD], own_terms[:, HD:])

    def heads_only(query_in, key_in, query_scale, key_scale):
        return prepare_heads(query_in, key_in, query_scale, key_scale, cosine, sine)

    pull_heads = jax.vjp(heads_only, queries, keys, query_gain, key_gain)[1]
    grad_query_pre, grad_key_pre, grad_query_gain, grad_key_gain = pull_heads(
        (jnp.concatenate(grad_queries, axis=0), grad_keys)
    )
    low_projected = jnp.concatenate(
        [grad_query_pre.reshape(count, OUTW), grad_key_pre, grad_values], axis=1
    ).astype(BF)
    grad_normed = dot_nt(low_projected, w_qkv)
    grad_in, grad_pre_attn = jax.vjp(rms_gain, flat_in, pre_attn)[1](grad_normed)
    input_grad = (jnp.concatenate(grad_resids, axis=0) + grad_in).astype(BF)

    attn_per = -(-ATTN_BLOCKS // nd)
    attn_width = attn_per * BC
    attn_term = jnp.concatenate([dot_tn(normed, low_projected), out_term], axis=1)
    attn_term = jnp.pad(attn_term, ((0, 0), (0, nd * attn_width - ATTN_BLOCKS * BC)))

    def owner_columns(index):
        return lax.dynamic_slice(attn_term, (0, index * attn_width), (D, attn_width))

    attn_term = after(attn_term, *left_mine[-1])
    owners_at = part_owners(nd)
    attn_sum = scatter_sum_dp(
        jnp.concatenate([owner_columns(e) for e in owners_at[: nd // 2]], axis=0),
        jnp.concatenate([owner_columns(e) for e in owners_at[nd // 2 :]], axis=0),
        nd,
    )
    ff_all = gather_columns([both_band, down_band])
    attn_band = direct_reduce(after(attn_sum, both_band).astype(BF), nf)
    attn_all = gather_relative([attn_band])

    def all_parts(mine):
        parts = [after(piece, attn_sum) for piece in mine + [swap_core(piece, nd) for piece in mine]]
        out = jnp.zeros((nd,) + parts[0].shape, BF)
        for place, piece in enumerate(parts):
            out = lax.dynamic_update_slice(out, piece[None], (place,) + (0,) * piece.ndim)
        return out.reshape((nd * capacity,) + out.shape[2:])

    left_roots = [all_parts(mine) for mine in left_mine]
    right_roots = all_parts(right_mine)

    def relative(index):
        nx = nd // 2
        flip = (index % 2) ^ core
        return flip * nx + (dp_me // 2 + nx - index // 2) % nx

    ff_index = np.arange(3 * FF_BLOCKS)
    ff_dp = np.minimum(ff_index % FF_BLOCKS // per, nd - 1)
    ff_column = ff_index % FF_BLOCKS - np.minimum(ff_dp * per, FF_BLOCKS - per)
    ff_column = ff_column + ff_index // FF_BLOCKS * per
    attn_index = np.arange(ATTN_BLOCKS)
    part_of = relative(
        jnp.asarray(np.concatenate([attn_index // attn_per, ff_dp]).astype(np.int32))
    )
    kind_of = jnp.asarray(
        np.zeros(NBLK).astype(np.int32)
    )
    column_of = jnp.asarray(np.concatenate([attn_index % attn_per, ff_column]).astype(np.int32))

    owners = owner[:, 0]
    index = jnp.arange(NBLK, dtype=jnp.int32)
    before = (owners[:, None] == owners[None, :]) & (index[None, :] < index[:, None])
    ranks = jnp.sum(before.astype(jnp.int32), axis=1)
    my_slots = jnp.arange(capacity, dtype=jnp.int32)
    mine = (owners[None, :] == dp_me) & (ranks[None, :] == my_slots[:, None])
    used = jnp.sum(mine.astype(jnp.int32), axis=1)

    def of_slot(values):
        return jnp.sum(jnp.where(mine, values[None, :], 0), axis=1)

    is_attn = (index < ATTN_BLOCKS).astype(jnp.int32)
    places = (part_of, kind_of, column_of, is_attn)
    early = tuple(table[LATE:] for table in places)
    late = tuple(table[:LATE] for table in places)
    root_of = relative(owners) * capacity + ranks
    root_args = (left_roots, right_roots, master)
    fresh_arrays = update_blocks(
        [ff_all], early, root_of[LATE:], *root_args, LATE, NBLK - LATE, 7, None
    )
    slot_places = tuple(of_slot(table) for table in places)
    group = 3 if (capacity - LATE) % 3 == 0 else 1
    stat_args = (slot_places, used, stat_left[0], stat_right[0])
    fresh_stats = owner_stats([ff_all], *stat_args, LATE, capacity - LATE, group, None)
    both = [ff_all, attn_all]
    new_master, new_weights = update_blocks(
        both, late, root_of[:LATE], *root_args, 0, LATE, 7, fresh_arrays
    )
    slot_grads, new_left, new_right = owner_stats(both, *stat_args, 0, LATE, group, fresh_stats)

    post_attn_sum = sum(entry[0] for entry in gain_terms)
    pre_ffw_sum = sum(entry[1] for entry in gain_terms)
    post_ffw_sum = sum(entry[2] for entry in gain_terms)
    gain_sum = jnp.concatenate(
        [grad_pre_attn, post_attn_sum, pre_ffw_sum, post_ffw_sum, grad_query_gain, grad_key_gain]
    )
    gain_grad = sum_everywhere(after(gain_sum, attn_band), nd, nf)
    new_gain_stats = DECAY * gain_stats + (1.0 - DECAY) * gain_grad * gain_grad
    gain_change = -GAIN_RATE * gain_grad * lax.rsqrt(new_gain_stats)
    return (
        jnp.stack(outputs)[:, None],
        input_grad.reshape(micros, 1, rows, D),
        slot_grads[None],
        gain_grad,
        new_left[None],
        new_right[None],
        new_master,
        new_weights,
        new_gain_stats,
        gain_change,
    )


def solution(mesh):
    in_specs = (
        P(None, "dp", "fsdp", None),
        P(None, "dp", "fsdp", None),
        P(None, "dp", None),
        P("fsdp", None),
        P(),
        P(),
        P("fsdp", None),
        P("fsdp", "dp", None, None),
        P("fsdp", "dp", None, None),
        P("fsdp", "dp", None, None),
        P("fsdp", "dp", None, None),
    )
    out_specs = (
        P(None, "dp", "fsdp", None),
        P(None, "dp", "fsdp", None),
        P("fsdp", "dp", None, None),
        P(),
        P("fsdp", "dp", None, None),
        P("fsdp", "dp", None, None),
        P("fsdp", None),
        P("fsdp", None),
        P(),
        P(),
    )
    return jax.shard_map(local, mesh=mesh, in_specs=in_specs, out_specs=out_specs, check_vma=False)
```

```python
import jax
import jax.numpy as jnp
import numpy as np
from jax import lax
from jax.experimental import pallas as pl
from jax.experimental.pallas import tpu as pltpu
from jax.sharding import PartitionSpec as P

D = 1152
HEADS = 4
HD = 256
FF = 6912
WIN = 512
PROMPT = 1024
CONT = 8
CLEN = 128
BC = 128
GLEN = 2048
QKVW = 1536
OUTW = HEADS * HD
NBLK = 182
ATTN_BLOCKS = (QKVW + OUTW) // BC
FF_BLOCKS = FF // BC

EPSILON = 1e-06
MASKED = -1e30
RATE = 0.02
GAIN_RATE = 0.05
DECAY = 0.5
SCALE = HD ** (-0.5)
DIRECT_MAX = 8
LATE = 21
VMEM_LIMIT = 40 * 1024 * 1024
BF = jnp.bfloat16
F32 = jnp.float32


def rms_gain(values, gain):
    return values * lax.rsqrt(jnp.mean(values * values, axis=-1, keepdims=True) + EPSILON) * gain


def rope_tables(positions):
    half_width = HD // 2
    freqs = 10000.0 ** (-2.0 * jnp.arange(half_width, dtype=F32) / HD)
    angles = positions.astype(F32)[:, None] * freqs[None, :]
    return (jnp.cos(angles), jnp.sin(angles))


def rotate(values, cosine, sine):
    half_width = values.shape[-1] // 2
    first_half = values[..., :half_width]
    second_half = values[..., half_width:]
    return jnp.concatenate(
        [first_half * cosine - second_half * sine, second_half * cosine + first_half * sine],
        axis=-1,
    )


def slot_layout(slots):
    in_prompt = slots < PROMPT
    offset = slots - PROMPT
    segment = jnp.where(in_prompt, -1, offset // CLEN)
    position = jnp.where(in_prompt, slots, PROMPT + offset % CLEN)
    return (segment, position)


def visibility(query_slots, key_slots, lens):
    query_seg, query_pos = slot_layout(query_slots)
    key_seg, key_pos = slot_layout(key_slots)
    picks = key_seg[:, None] == jnp.arange(CONT, dtype=jnp.int32)[None, :]
    key_len = jnp.sum(jnp.where(picks, lens[None, :], 0), axis=1)
    key_used = (key_seg < 0) | (key_pos - PROMPT < key_len)
    distance = query_pos[:, None] - key_pos[None, :]
    same_part = (key_seg[None, :] < 0) | (key_seg[None, :] == query_seg[:, None])
    present = key_slots >= 0
    return (distance >= 0) & (distance < WIN) & same_part & (key_used & present)[None, :]


def split_gains(gains):
    return (
        gains[:D],
        gains[D : 2 * D],
        gains[2 * D : 3 * D],
        gains[3 * D : 4 * D],
        gains[4 * D : 4 * D + HD],
        gains[4 * D + HD :],
    )


def prepare_heads(queries, keys, query_gain, key_gain, cosine, sine):
    rot_queries = rotate(rms_gain(queries, query_gain), cosine[:, None, :], sine[:, None, :])
    rot_keys = rotate(rms_gain(keys, key_gain), cosine, sine)
    return (rot_queries, rot_keys)


def dot_nn(left, right):
    return jnp.dot(left, right, preferred_element_type=F32)


def dot_nt(left, right):
    return lax.dot_general(left, right, (((1,), (1,)), ((), ())), preferred_element_type=F32)


def dot_tn(left, right):
    return lax.dot_general(left, right, (((0,), (0,)), ((), ())), preferred_element_type=F32)


def swap_core(value, nd):
    return lax.ppermute(value, "dp", [(e, e ^ 1) for e in range(nd)])


def shift_x(value, nd, step):
    nx = nd // 2
    pairs = [(e, ((e // 2 + step) % nx) * 2 + e % 2) for e in range(nd)]
    return lax.ppermute(value, "dp", pairs)


def gather_parts(value, nd):
    mine = [value] + [shift_x(value, nd, k) for k in range(1, nd // 2)]
    return mine + [swap_core(part, nd) for part in mine]


def gather_dp(value, nd):
    return jnp.concatenate(gather_parts(value, nd), axis=0)


def part_owners(nd):
    nx = nd // 2
    me = lax.axis_index("dp")
    x, core = me // 2, me % 2
    out = []
    for flip in range(2):
        for k in range(nx):
            out.append(((x + nx - k) % nx) * 2 + (core if flip == 0 else 1 - core))
    return out


def scatter_sum_dp(own_half, other_half, nd):
    nx = nd // 2
    received = swap_core(other_half.astype(BF), nd)
    total = own_half + received.astype(F32)
    rows = total.shape[0] // nx
    result = total[:rows]
    for k in range(1, nx):
        sent = total[k * rows : (k + 1) * rows].astype(BF)
        result = result + shift_x(sent, nd, nx - k).astype(F32)
    return result


def sum_everywhere(value, nd, nf):
    for axis, count in (("dp", nd), ("fsdp", nf)):
        step = 1
        while step < count:
            value = value + lax.ppermute(value, axis, [(e, e ^ step) for e in range(count)])
            step *= 2
    return value


def after(value, *others):
    return lax.optimization_barrier((value,) + others)[0]


def swap_fsdp(value, flip, nf):
    return lax.ppermute(value, "fsdp", [(e, e ^ flip) for e in range(nf)])


def gather_rows(own, nf, ties=()):
    if nf > DIRECT_MAX:
        return lax.all_gather(own, "fsdp", axis=0, tiled=True)
    me = lax.axis_index("fsdp")
    band, width = own.shape
    straight = [own] + [swap_fsdp(own, flip, nf) for flip in range(2, nf, 2)]
    passed = [own] + [after(part, *ties) if ties else part for part in straight[1:]]
    crossed = [swap_fsdp(part, 1, nf) for part in passed]
    whole = jnp.zeros((nf * band, width), own.dtype)
    for k in range(nf // 2):
        whole = lax.dynamic_update_slice(whole, straight[k], ((me ^ (2 * k)) * band, 0))
        whole = lax.dynamic_update_slice(whole, crossed[k], ((me ^ (2 * k + 1)) * band, 0))
    return whole


def direct_reduce(terms, nf):
    band, width = (terms.shape[0] // nf, terms.shape[1])
    spread = lax.all_to_all(terms.reshape(nf, band, width), "fsdp", split_axis=0, concat_axis=0)
    return jnp.sum(spread.astype(F32), axis=0).astype(BF)


def dot_on(left, right, left_dim, right_dim):
    return lax.dot_general(
        left, right, (((left_dim,), (right_dim,)), ((), ())), preferred_element_type=F32
    )


def pick_grad(sources, flags, at):
    if len(sources) == 1:
        return sources[0][...]
    return jnp.where(flags[at] > 0, sources[1][...], sources[0][...])


def update_body(group, count, pieces, flags, refs):
    grads = refs[: group * count]
    lefts = refs[group * count : group * (count + pieces)]
    rights = refs[group * (count + pieces) : group * (count + pieces + 1)]
    master_ref, new_ref, low_ref = (refs[group * (count + pieces + 1)], refs[-2], refs[-1])
    base = pl.program_id(0) * group
    shaped = []
    for j in range(group):
        grad = pick_grad(grads[j * count : (j + 1) * count], flags, base + j)
        product = dot_on(lefts[j][...], grad[: lefts[j].shape[1]], 1, 0)
        if pieces > 1:
            product = product + dot_on(lefts[group + j][...], grad[lefts[j].shape[1] :], 0, 0)
        shaped.append(product.astype(BF))
    shaped = [dot_on(shaped[j], rights[j][...], 1, 0) for j in range(group)]
    scale = 1.0 / (shaped[0].shape[0] * shaped[0].shape[1])
    powers = [jnp.sum(jnp.sum(s * s, axis=0, keepdims=True), axis=1, keepdims=True) for s in shaped]
    factors = [-RATE * lax.rsqrt(power * scale + EPSILON) for power in powers]
    for j in range(group):
        at = pl.ds(j * BC, BC)
        fresh = master_ref[:, at] + shaped[j] * factors[j]
        new_ref[:, at] = fresh
        low_ref[:, at] = fresh.astype(BF)


def pack_roots(roots):
    slots, rows = roots.shape[:2]
    group = 3 if slots % 3 == 0 else 1
    rest = rows - BC

    def body(root_ref, first_ref, rest_ref):
        for j in range(group):
            first_ref[j] = root_ref[j, :, :BC]
            rest_ref[j] = root_ref[j, :, BC:].astype(F32).T.astype(BF)

    def slab(shape):
        return pl.BlockSpec((group,) + shape, lambda i: (i, 0, 0))

    return pl.pallas_call(
        body,
        grid=(slots // group,),
        in_specs=[slab((rows, rows))],
        out_specs=[slab((rows, BC)), slab((rest, rows))],
        out_shape=[
            jax.ShapeDtypeStruct((slots, rows, BC), BF),
            jax.ShapeDtypeStruct((slots, rest, rows), BF),
        ],
        compiler_params=pltpu.CompilerParams(vmem_limit_bytes=VMEM_LIMIT),
        name="pack_roots",
    )(roots)


def grad_specs(sources, group, skip, band):
    def spec(j, is_second):
        def index(i, part, kind, column, flags, *more):
            at = (i + skip) * group + j
            own = jnp.where(flags[at] > 0, 1, 0) if len(sources) > 1 else 0
            fits = own if is_second else 1 - own
            return (part[at] * fits, kind[at] * fits, 0, column[at] * fits)

        return pl.BlockSpec((None, None, band, BC), index)

    return [spec(j, n > 0) for j in range(group) for n in range(len(sources))]


def update_blocks(sources, places, roots, left_roots, right_roots, master, start, count, group, into):
    band = master.shape[0]
    skip = start // group

    def root_spec(shape, j):
        def index(i, part, kind, column, flags, root):
            return (root[i * group + j], 0, 0)

        return pl.BlockSpec((None,) + shape, index)

    wide = pl.BlockSpec((band, group * BC), lambda i, *tables: (0, i + skip))
    in_specs = grad_specs(sources, group, 0, band)
    in_specs += [root_spec(left.shape[1:], j) for left in left_roots for j in range(group)]
    in_specs += [root_spec(right_roots.shape[1:], j) for j in range(group)]
    in_specs += [wide]
    operands = list(sources) * group + [left for left in left_roots for _ in range(group)]
    operands += [right_roots] * group + [master]
    tables = list(places) + [roots]
    aliases = {}
    if into is not None:
        aliases = {len(tables) + len(operands) + n: n for n in range(2)}
        in_specs += [pl.BlockSpec(memory_space=pl.ANY)] * 2
        operands += list(into)
    return pl.pallas_call(
        lambda *refs: update_body(group, len(sources), len(left_roots), refs[3], refs[5:]),
        grid_spec=pltpu.PrefetchScalarGridSpec(
            num_scalar_prefetch=5,
            grid=(count // group,),
            in_specs=in_specs,
            out_specs=[wide, wide],
        ),
        out_shape=[
            jax.ShapeDtypeStruct(master.shape, F32),
            jax.ShapeDtypeStruct(master.shape, BF),
        ],
        input_output_aliases=aliases,
        compiler_params=pltpu.CompilerParams(vmem_limit_bytes=VMEM_LIMIT),
        name="update_blocks",
    )(*tables, *operands)


def stats_body(group, count, skip, flags, used, refs):
    grads, (left_ref, right_ref) = (refs[: group * count], refs[group * count : group * count + 2])
    grad_out, left_out, right_out = refs[-3:]
    for j in range(group):
        at = (pl.program_id(0) + skip) * group + j
        grad = pick_grad(grads[j * count : (j + 1) * count], flags, at)
        grad = jnp.where(used[at] > 0, grad, jnp.zeros_like(grad))
        grad_out[j] = grad.astype(F32)
        left_out[j] = DECAY * left_ref[j] + (1.0 - DECAY) * dot_on(grad, grad, 1, 1)
        right_out[j] = DECAY * right_ref[j] + (1.0 - DECAY) * dot_on(grad, grad, 0, 0)


def owner_stats(sources, places, used, stat_left, stat_right, start, count, group, into):
    slots, band = (stat_left.shape[0], sources[0].shape[2])
    skip = start // group

    def slab(shape):
        return pl.BlockSpec((group,) + shape, lambda i, *tables: (i + skip, 0, 0))

    shapes = [(band, BC), stat_left.shape[1:], stat_right.shape[1:]]
    in_specs = grad_specs(sources, group, skip, band) + [slab(shapes[1]), slab(shapes[2])]
    operands = list(sources) * group + [stat_left, stat_right]
    tables = list(places) + [used]
    aliases = {}
    if into is not None:
        aliases = {len(tables) + len(operands) + n: n for n in range(3)}
        in_specs += [pl.BlockSpec(memory_space=pl.ANY)] * 3
        operands += list(into)
    return pl.pallas_call(
        lambda *refs: stats_body(group, len(sources), skip, refs[3], refs[4], refs[5:]),
        grid_spec=pltpu.PrefetchScalarGridSpec(
            num_scalar_prefetch=5,
            grid=(count // group,),
            in_specs=in_specs,
            out_specs=[slab(shape) for shape in shapes],
        ),
        out_shape=[jax.ShapeDtypeStruct((slots,) + shape, F32) for shape in shapes],
        input_output_aliases=aliases,
        compiler_params=pltpu.CompilerParams(vmem_limit_bytes=VMEM_LIMIT),
        name="owner_stats",
    )(*tables, *operands)


KEY_SHARDS = 8
TO_SECOND = [(0, 2), (1, 3), (2, 4), (3, 5)]
TO_NEXT = [(0, 1), (1, 2), (2, 3)]
ONWARDS = [(4, 6), (5, 7)]
ACROSS = [(4, 5), (5, 4), (6, 7), (7, 6)]
FIRST_SOURCE = [-1, -1, 0, 1, 2, 3, 2, 3]
SECOND_SOURCE = [-1, 0, 1, 2, 3, 2, 3, 2]


def backwards(pairs):
    return [(dst, src) for src, dst in pairs]


def pick_static(table, index):
    values = jnp.asarray(table, jnp.int32)
    hit = jnp.arange(len(table), dtype=jnp.int32) == index
    return jnp.sum(jnp.where(hit, values, 0))


def key_slots_of(rows, nf):
    me = lax.axis_index("fsdp")
    step = jnp.arange(rows, dtype=jnp.int32)
    if nf != KEY_SHARDS:
        return jnp.arange(rows * nf, dtype=jnp.int32)
    ids = [me * rows + step]
    for table in (FIRST_SOURCE, SECOND_SOURCE):
        source = pick_static(table, me)
        ids.append(jnp.where(source >= 0, source * rows + step, -1))
    return jnp.concatenate(ids)


def spread_keys(own, nf):
    if nf != KEY_SHARDS:
        return lax.all_gather(own, "fsdp", axis=0, tiled=True)
    second = lax.ppermute(own, "fsdp", TO_SECOND)
    following = lax.ppermute(own, "fsdp", TO_NEXT)
    onward = lax.ppermute(second, "fsdp", ONWARDS)
    crossed = lax.ppermute(second, "fsdp", ACROSS[:2])
    crossed_on = lax.ppermute(onward, "fsdp", ACROSS[2:])
    return jnp.concatenate([own, second + onward, following + crossed + crossed_on], axis=0)


def return_key_grads(terms, rows, nf):
    if nf != KEY_SHARDS:
        return lax.psum_scatter(
            terms.astype(BF), "fsdp", scatter_dimension=0, tiled=True
        ).astype(F32)
    first = terms[rows : 2 * rows]
    second = terms[2 * rows :].astype(BF)
    total = terms[:rows] + lax.ppermute(second, "fsdp", backwards(TO_NEXT)).astype(F32)
    first = first + lax.ppermute(second, "fsdp", ACROSS).astype(F32)
    first = first + lax.ppermute(first.astype(BF), "fsdp", backwards(ONWARDS)).astype(F32)
    return total + lax.ppermute(first.astype(BF), "fsdp", backwards(TO_SECOND)).astype(F32)


def attend(query_low, keys, values, visible):
    scores = jnp.einsum("thd,kd->thk", query_low, keys, preferred_element_type=F32) * SCALE
    scores = jnp.where(visible[:, None, :], scores, MASKED)
    highest = jnp.max(scores, axis=-1, keepdims=True)
    expo = jnp.exp(scores - highest)
    probs = expo / jnp.sum(expo, axis=-1, keepdims=True)
    mixed = jnp.einsum("thk,kd->thd", probs.astype(BF), values, preferred_element_type=F32)
    return (mixed, probs)


def attend_back(query_low, keys, values, probs, low_mixed):
    grad_probs = jnp.einsum("thd,kd->thk", low_mixed, values, preferred_element_type=F32)
    row_dot = jnp.sum(grad_probs * probs, axis=-1, keepdims=True)
    grad_scores = (probs * (grad_probs - row_dot)).astype(BF)
    grad_queries = jnp.einsum("thk,kd->thd", grad_scores, keys, preferred_element_type=F32) * SCALE
    key_terms = (
        jnp.einsum("thk,thd->kd", grad_scores, query_low, preferred_element_type=F32) * SCALE
    )
    value_terms = jnp.einsum("thk,thd->kd", probs.astype(BF), low_mixed, preferred_element_type=F32)
    return (grad_queries, key_terms, value_terms)


def local(
    tokens,
    cotangent,
    lengths,
    master,
    gains,
    gain_stats,
    owner,
    stat_left,
    stat_right,
    root_left,
    root_right,
):
    nd = lax.axis_size("dp")
    nf = lax.axis_size("fsdp")
    dp_me = lax.axis_index("dp")
    core = dp_me % 2
    micros = tokens.shape[0]
    rows = tokens.shape[2]
    count = micros * rows
    band = master.shape[0]
    capacity = stat_left.shape[1]
    first = lax.axis_index("fsdp") * rows
    pre_attn, post_attn, pre_ffw, post_ffw, query_gain, key_gain = split_gains(gains)

    per = -(-FF_BLOCKS // nd)
    width = per * BC
    start = jnp.minimum(dp_me * per, FF_BLOCKS - per)
    fresh = dp_me * per - start
    gate_at = ATTN_BLOCKS * BC

    def columns(at, size):
        return lax.dynamic_slice(master, (0, at), (band, size)).astype(BF)

    def gather_relative(bands, *ties):
        parts = [gather_parts(part, nd) for part in bands]
        if ties:
            parts = [[after(piece, *ties) for piece in pieces] for pieces in parts]
        out = jnp.zeros((nd, len(bands)) + bands[0].shape, BF)
        for kind, pieces in enumerate(parts):
            for place, piece in enumerate(pieces):
                out = lax.dynamic_update_slice(
                    out, piece[None, None], (place, kind) + (0,) * piece.ndim
                )
        return out

    def gather_columns(bands):
        out = jnp.zeros((nd, 1, band, sum(part.shape[1] for part in bands)), BF)
        at = 0
        for part in bands:
            for place, piece in enumerate(gather_parts(part, nd)):
                out = lax.dynamic_update_slice(out, piece[None, None], (place, 0, 0, at))
            at += part.shape[1]
        return out

    def halves(at, size, first_ties, next_ties):
        part = size // 2
        cols = columns(at + core * part, part)
        mine = gather_rows(after(cols, *first_ties) if first_ties else cols, nf, next_ties)
        whole = jnp.zeros((D, size), BF)
        whole = lax.dynamic_update_slice(whole, mine, (0, core * part))
        return lax.dynamic_update_slice(whole, swap_core(mine, nd), (0, (1 - core) * part))

    w_qkv = halves(0, QKVW, (), ())
    gate_cols = columns(gate_at + start * BC, width)
    up_cols = columns(gate_at + FF + start * BC, width)
    down_cols = columns(gate_at + 2 * FF + start * BC, width)
    keep = (jnp.arange(width, dtype=jnp.int32) >= fresh * BC)[None, :]
    down_cols = jnp.where(keep, down_cols, jnp.zeros_like(down_cols))
    both_cols = jnp.concatenate([gate_cols, up_cols], axis=1)
    w_both = lax.all_gather(both_cols, "fsdp", axis=0, tiled=True)
    w_gate, w_up = (w_both[:, :width], w_both[:, width:])
    w_down = lax.all_gather(down_cols, "fsdp", axis=0, tiled=True)

    flat_in = tokens.astype(F32).reshape(count, D)
    normed = rms_gain(flat_in, pre_attn).astype(BF)
    projected = dot_nn(normed, w_qkv)
    queries = projected[:, :OUTW].reshape(count, HEADS, HD)
    keys = projected[:, OUTW : OUTW + HD]
    values = projected[:, OUTW + HD :]
    slots = first + jnp.arange(rows, dtype=jnp.int32)
    _, positions = slot_layout(slots)
    cosine, sine = rope_tables(positions)
    cosine, sine = (jnp.tile(cosine, (micros, 1)), jnp.tile(sine, (micros, 1)))
    rot_queries, rot_keys = prepare_heads(queries, keys, query_gain, key_gain, cosine, sine)
    query_low = rot_queries.astype(BF).reshape(micros, rows, HEADS, HD)
    own_keys = jnp.concatenate([rot_keys.astype(BF), values.astype(BF)], axis=1)
    key_buffers = [spread_keys(own_keys[m * rows : (m + 1) * rows], nf) for m in range(micros)]
    key_slots = key_slots_of(rows, nf)
    w_out = halves(QKVW, OUTW, (projected,), (key_buffers[0],))
    keys_all = [buffer[:, :HD] for buffer in key_buffers]
    values_all = [buffer[:, HD:] for buffer in key_buffers]
    all_probs, all_attended = [], []
    for m in range(micros):
        visible = visibility(slots, key_slots, lengths[m, 0])
        mixed, probs = attend(query_low[m], keys_all[m], values_all[m], visible)
        all_probs.append(probs)
        all_attended.append(mixed.reshape(rows, OUTW).astype(BF))

    half = (nd // 2) * rows
    outputs, saved, gathered_in, gathered_two, hiddens, low_gates, low_ups = [], [], [], [], [], [], []
    grad_resids, gain_terms, low_ones = [], [], []
    for m in range(micros):
        part_in = flat_in[m * rows : (m + 1) * rows]
        branch_one = dot_nt(all_attended[m], w_out)
        resid = part_in + rms_gain(branch_one, post_attn)
        ffw_in = rms_gain(resid, pre_ffw).astype(BF)
        gathered_in.append(gather_dp(ffw_in, nd))
        saved.append([branch_one, resid])
    partials = []
    for m in range(micros):
        every_in = gathered_in[m]
        if m:
            every_in = after(every_in, hiddens[-1])
        gate = dot_nn(every_in, w_gate)
        up = dot_nn(every_in, w_up)
        hidden = (jax.nn.gelu(gate, approximate=True) * up).astype(BF)
        hiddens.append(hidden)
        saved[m] += [gate, up]
    for m in range(micros):
        hidden = after(hiddens[m], *(partials[-1] if m else hiddens[-1:]))
        away = dot_nt(hidden[half:], w_down).astype(BF)
        partials.append((away, dot_nt(after(hidden[:half], away), w_down)))
    last = partials[-1][1]
    for m in range(micros):
        branch_one, resid, gate, up = saved[m]
        branch_two = scatter_sum_dp(partials[m][1], partials[m][0], nd)
        outputs.append((resid + rms_gain(branch_two, post_ffw)).astype(BF))
        upstream = cotangent[m, 0].astype(F32)
        grad_two, grad_post_ffw = jax.vjp(rms_gain, branch_two, post_ffw)[1](upstream)
        gathered_two.append(gather_dp(grad_two.astype(BF), nd))
        saved[m] += [upstream, grad_post_ffw]
    def weight_term(lefts, rights, follow):
        left = jnp.concatenate(lefts, axis=0)
        term = dot_tn(after(left, *follow), jnp.concatenate(rights, axis=0))
        return term.astype(BF)

    def sum_rows(term):
        return lax.psum_scatter(term, "fsdp", scatter_dimension=0, tiled=True)

    for m in range(micros):
        gate, up = saved[m][2:4]
        if m == micros - 1:
            last = down_term = weight_term(gathered_two, hiddens, (last,))
        grad_hidden = dot_nn(after(gathered_two[m], last), w_down)
        grad_gate, grad_up = jax.vjp(
            lambda gate_in, up_in: jax.nn.gelu(gate_in, approximate=True) * up_in, gate, up
        )[1](grad_hidden)
        low_gates.append(grad_gate.astype(BF))
        low_ups.append(grad_up.astype(BF))
        last = low_ups[-1]

    def from_x(root, *ties):
        root = after(root, *ties) if ties else root
        return [root] + [shift_x(root, nd, k) for k in range(1, nd // 2)]

    right_mine = from_x(root_right[0], *gathered_two)
    down_band = sum_rows(down_term)
    gate_term = weight_term(gathered_in, low_gates, (last,))
    up_term = weight_term(gathered_in, low_ups, (gate_term,))
    both_term = jnp.concatenate([gate_term, up_term], axis=1)
    both_band = sum_rows(both_term)
    last = both_term
    for m in range(micros):
        branch_one, resid, _, _, upstream, grad_post_ffw = saved[m]
        gate_in, up_in = (after(low_gates[m], last, *right_mine[1:]), low_ups[m])
        away = dot_nt(gate_in[half:], w_gate) + dot_nt(up_in[half:], w_up)
        gate_in = after(gate_in, away)
        last = dot_nt(gate_in[:half], w_gate) + dot_nt(up_in[:half], w_up)
        grad_ffw_in = scatter_sum_dp(last, away, nd)
        grad_resid, grad_pre_ffw = jax.vjp(rms_gain, resid, pre_ffw)[1](grad_ffw_in)
        grad_resid = upstream + grad_resid
        grad_one, grad_post_attn = jax.vjp(rms_gain, branch_one, post_attn)[1](grad_resid)
        grad_resids.append(grad_resid)
        low_ones.append(grad_one.astype(BF))
        gain_terms.append((grad_post_attn, grad_pre_ffw, grad_post_ffw))

    low_one = jnp.concatenate(low_ones, axis=0)
    attended = jnp.concatenate(all_attended, axis=0)
    owners_at = part_owners(nd)
    qkv_per, out_per = (-(-QKVW // (BC * nd)), -(-OUTW // (BC * nd)))

    def term_over_dp(left, right, per_index):
        size = per_index * BC
        right = jnp.pad(right, ((0, 0), (0, nd * size - right.shape[1])))
        terms = [
            dot_tn(left, lax.dynamic_slice(right, (0, index * size), (count, size)))
            for index in owners_at
        ]
        mine, away = (terms[: nd // 2], terms[nd // 2 :])
        away = jnp.concatenate(away, axis=0).astype(BF)
        return (scatter_sum_dp(jnp.concatenate(mine, axis=0), away, nd), away)

    out_sum, _ = term_over_dp(low_one, attended, out_per)
    left_root = after(root_left[0], low_one)
    left_pieces = pack_roots(left_root) if band > BC else [left_root]
    left_mine = [from_x(left) for left in left_pieces]
    left_here = [piece for mine in left_mine for piece in mine[1:]]

    low_mixed = dot_nn(after(low_one, down_band, *left_pieces), w_out).astype(BF).reshape(micros, rows, HEADS, HD)
    grad_queries, key_terms = [], []
    for m in range(micros):
        for_queries, for_keys, for_values = attend_back(
            query_low[m], keys_all[m], values_all[m], all_probs[m], low_mixed[m]
        )
        grad_queries.append(for_queries)
        terms = jnp.concatenate([for_keys, for_values], axis=1)
        key_terms.append(return_key_grads(terms, rows, nf))
        last = terms
    own_terms = after(jnp.concatenate(key_terms, axis=0), *left_here)
    grad_keys, grad_values = (own_terms[:, :HD], own_terms[:, HD:])

    def heads_only(query_in, key_in, query_scale, key_scale):
        return prepare_heads(query_in, key_in, query_scale, key_scale, cosine, sine)

    pull_heads = jax.vjp(heads_only, queries, keys, query_gain, key_gain)[1]
    grad_query_pre, grad_key_pre, grad_query_gain, grad_key_gain = pull_heads(
        (jnp.concatenate(grad_queries, axis=0), grad_keys)
    )
    low_projected = jnp.concatenate(
        [grad_query_pre.reshape(count, OUTW), grad_key_pre, grad_values], axis=1
    ).astype(BF)
    grad_normed = dot_nt(low_projected, w_qkv)
    grad_in, grad_pre_attn = jax.vjp(rms_gain, flat_in, pre_attn)[1](grad_normed)
    input_grad = (jnp.concatenate(grad_resids, axis=0) + grad_in).astype(BF)

    qkv_sum, qkv_away = term_over_dp(after(normed, both_band), low_projected, qkv_per)
    attn_sum = jnp.concatenate([qkv_sum, out_sum], axis=1).astype(BF)
    ff_all = gather_columns([both_band, down_band])
    attn_band = direct_reduce(after(attn_sum, both_band), nf)
    attn_all = gather_relative([attn_band])

    def all_parts(mine, *ties):
        parts = mine + [swap_core(piece, nd) for piece in mine]
        parts = [after(piece, *ties) for piece in parts]
        out = jnp.zeros((nd,) + parts[0].shape, BF)
        for place, piece in enumerate(parts):
            out = lax.dynamic_update_slice(out, piece[None], (place,) + (0,) * piece.ndim)
        return out.reshape((nd * capacity,) + out.shape[2:])

    right_roots = all_parts(right_mine, qkv_away)
    left_roots = [all_parts(mine, qkv_away) for mine in left_mine]

    def relative(index):
        nx = nd // 2
        flip = (index % 2) ^ core
        return flip * nx + (dp_me // 2 + nx - index // 2) % nx

    ff_index = np.arange(3 * FF_BLOCKS)
    ff_dp = np.minimum(ff_index % FF_BLOCKS // per, nd - 1)
    ff_column = ff_index % FF_BLOCKS - np.minimum(ff_dp * per, FF_BLOCKS - per)
    ff_column = ff_column + ff_index // FF_BLOCKS * per
    qkv_index, out_index = (np.arange(QKVW // BC), np.arange(OUTW // BC))
    attn_dp = np.concatenate([qkv_index // qkv_per, out_index // out_per])
    attn_column = np.concatenate([qkv_index % qkv_per, qkv_per + out_index % out_per])
    part_of = relative(
        jnp.asarray(np.concatenate([attn_dp, ff_dp]).astype(np.int32))
    )
    kind_of = jnp.asarray(
        np.zeros(NBLK).astype(np.int32)
    )
    column_of = jnp.asarray(np.concatenate([attn_column, ff_column]).astype(np.int32))

    owners = owner[:, 0]
    index = jnp.arange(NBLK, dtype=jnp.int32)
    before = (owners[:, None] == owners[None, :]) & (index[None, :] < index[:, None])
    ranks = jnp.sum(before.astype(jnp.int32), axis=1)
    my_slots = jnp.arange(capacity, dtype=jnp.int32)
    mine = (owners[None, :] == dp_me) & (ranks[None, :] == my_slots[:, None])
    used = jnp.sum(mine.astype(jnp.int32), axis=1)

    def of_slot(values):
        return jnp.sum(jnp.where(mine, values[None, :], 0), axis=1)

    is_attn = (index < ATTN_BLOCKS).astype(jnp.int32)
    places = (part_of, kind_of, column_of, is_attn)
    early = tuple(table[LATE:] for table in places)
    late = tuple(table[:LATE] for table in places)
    root_of = relative(owners) * capacity + ranks
    root_args = (left_roots, right_roots, master)
    fresh_arrays = update_blocks(
        [ff_all], early, root_of[LATE:], *root_args, LATE, NBLK - LATE, 7, None
    )
    slot_places = tuple(of_slot(table) for table in places)
    group = 3 if (capacity - LATE) % 3 == 0 else 1
    stat_args = (slot_places, used, stat_left[0], stat_right[0])
    fresh_stats = owner_stats([ff_all], *stat_args, LATE, capacity - LATE, group, None)
    both = [ff_all, attn_all]
    new_master, new_weights = update_blocks(
        both, late, root_of[:LATE], *root_args, 0, LATE, 7, fresh_arrays
    )
    slot_grads, new_left, new_right = owner_stats(both, *stat_args, 0, LATE, group, fresh_stats)

    post_attn_sum = sum(entry[0] for entry in gain_terms)
    pre_ffw_sum = sum(entry[1] for entry in gain_terms)
    post_ffw_sum = sum(entry[2] for entry in gain_terms)
    gain_sum = jnp.concatenate(
        [grad_pre_attn, post_attn_sum, pre_ffw_sum, post_ffw_sum, grad_query_gain, grad_key_gain]
    )
    gain_grad = sum_everywhere(after(gain_sum, attn_band), nd, nf)
    new_gain_stats = DECAY * gain_stats + (1.0 - DECAY) * gain_grad * gain_grad
    gain_change = -GAIN_RATE * gain_grad * lax.rsqrt(new_gain_stats)
    return (
        jnp.stack(outputs)[:, None],
        input_grad.reshape(micros, 1, rows, D),
        slot_grads[None],
        gain_grad,
        new_left[None],
        new_right[None],
        new_master,
        new_weights,
        new_gain_stats,
        gain_change,
    )


def solution(mesh):
    in_specs = (
        P(None, "dp", "fsdp", None),
        P(None, "dp", "fsdp", None),
        P(None, "dp", None),
        P("fsdp", None),
        P(),
        P(),
        P("fsdp", None),
        P("fsdp", "dp", None, None),
        P("fsdp", "dp", None, None),
        P("fsdp", "dp", None, None),
        P("fsdp", "dp", None, None),
    )
    out_specs = (
        P(None, "dp", "fsdp", None),
        P(None, "dp", "fsdp", None),
        P("fsdp", "dp", None, None),
        P(),
        P("fsdp", "dp", None, None),
        P("fsdp", "dp", None, None),
        P("fsdp", None),
        P("fsdp", None),
        P(),
        P(),
    )
    return jax.shard_map(local, mesh=mesh, in_specs=in_specs, out_specs=out_specs, check_vma=False)
```

```python
import jax
import jax.numpy as jnp
import numpy as np
from jax import lax
from jax.experimental import pallas as pl
from jax.experimental.pallas import tpu as pltpu
from jax.sharding import PartitionSpec as P

D = 1152
HEADS = 4
HD = 256
FF = 6912
WIN = 512
PROMPT = 1024
CONT = 8
CLEN = 128
BC = 128
GLEN = 2048
QKVW = 1536
OUTW = HEADS * HD
NBLK = 182
ATTN_BLOCKS = (QKVW + OUTW) // BC
FF_BLOCKS = FF // BC

EPSILON = 1e-06
MASKED = -1e30
RATE = 0.02
GAIN_RATE = 0.05
DECAY = 0.5
SCALE = HD ** (-0.5)
DIRECT_MAX = 8
LATE = 21
VMEM_LIMIT = 40 * 1024 * 1024
BF = jnp.bfloat16
F32 = jnp.float32


def rms_gain(values, gain):
    return values * lax.rsqrt(jnp.mean(values * values, axis=-1, keepdims=True) + EPSILON) * gain


def rope_tables(positions):
    half_width = HD // 2
    freqs = 10000.0 ** (-2.0 * jnp.arange(half_width, dtype=F32) / HD)
    angles = positions.astype(F32)[:, None] * freqs[None, :]
    return (jnp.cos(angles), jnp.sin(angles))


def rotate(values, cosine, sine):
    half_width = values.shape[-1] // 2
    first_half = values[..., :half_width]
    second_half = values[..., half_width:]
    return jnp.concatenate(
        [first_half * cosine - second_half * sine, second_half * cosine + first_half * sine],
        axis=-1,
    )


def slot_layout(slots):
    in_prompt = slots < PROMPT
    offset = slots - PROMPT
    segment = jnp.where(in_prompt, -1, offset // CLEN)
    position = jnp.where(in_prompt, slots, PROMPT + offset % CLEN)
    return (segment, position)


def visibility(query_slots, key_slots, lens):
    query_seg, query_pos = slot_layout(query_slots)
    key_seg, key_pos = slot_layout(key_slots)
    picks = key_seg[:, None] == jnp.arange(CONT, dtype=jnp.int32)[None, :]
    key_len = jnp.sum(jnp.where(picks, lens[None, :], 0), axis=1)
    key_used = (key_seg < 0) | (key_pos - PROMPT < key_len)
    distance = query_pos[:, None] - key_pos[None, :]
    same_part = (key_seg[None, :] < 0) | (key_seg[None, :] == query_seg[:, None])
    present = key_slots >= 0
    return (distance >= 0) & (distance < WIN) & same_part & (key_used & present)[None, :]


def split_gains(gains):
    return (
        gains[:D],
        gains[D : 2 * D],
        gains[2 * D : 3 * D],
        gains[3 * D : 4 * D],
        gains[4 * D : 4 * D + HD],
        gains[4 * D + HD :],
    )


def prepare_heads(queries, keys, query_gain, key_gain, cosine, sine):
    rot_queries = rotate(rms_gain(queries, query_gain), cosine[:, None, :], sine[:, None, :])
    rot_keys = rotate(rms_gain(keys, key_gain), cosine, sine)
    return (rot_queries, rot_keys)


def dot_nn(left, right):
    return jnp.dot(left, right, preferred_element_type=F32)


def dot_nt(left, right):
    return lax.dot_general(left, right, (((1,), (1,)), ((), ())), preferred_element_type=F32)


def dot_tn(left, right):
    return lax.dot_general(left, right, (((0,), (0,)), ((), ())), preferred_element_type=F32)


def swap_core(value, nd):
    return lax.ppermute(value, "dp", [(e, e ^ 1) for e in range(nd)])


def shift_x(value, nd, step):
    nx = nd // 2
    pairs = [(e, ((e // 2 + step) % nx) * 2 + e % 2) for e in range(nd)]
    return lax.ppermute(value, "dp", pairs)


def gather_parts(value, nd):
    mine = [value] + [shift_x(value, nd, k) for k in range(1, nd // 2)]
    return mine + [swap_core(part, nd) for part in mine]


def gather_dp(value, nd):
    return jnp.concatenate(gather_parts(value, nd), axis=0)


def part_owners(nd):
    nx = nd // 2
    me = lax.axis_index("dp")
    x, core = me // 2, me % 2
    out = []
    for flip in range(2):
        for k in range(nx):
            out.append(((x + nx - k) % nx) * 2 + (core if flip == 0 else 1 - core))
    return out


def scatter_sum_dp(own_half, other_half, nd):
    nx = nd // 2
    received = swap_core(other_half.astype(BF), nd)
    total = own_half + received.astype(F32)
    rows = total.shape[0] // nx
    result = total[:rows]
    for k in range(1, nx):
        sent = total[k * rows : (k + 1) * rows].astype(BF)
        result = result + shift_x(sent, nd, nx - k).astype(F32)
    return result


def sum_everywhere(value, nd, nf):
    for axis, count in (("dp", nd), ("fsdp", nf)):
        step = 1
        while step < count:
            value = value + lax.ppermute(value, axis, [(e, e ^ step) for e in range(count)])
            step *= 2
    return value


def after(value, *others):
    return lax.optimization_barrier((value,) + others)[0]


def swap_fsdp(value, flip, nf):
    return lax.ppermute(value, "fsdp", [(e, e ^ flip) for e in range(nf)])


def gather_rows(own, nf, ties=()):
    if nf > DIRECT_MAX:
        return lax.all_gather(own, "fsdp", axis=0, tiled=True)
    me = lax.axis_index("fsdp")
    band, width = own.shape
    straight = [own] + [swap_fsdp(own, flip, nf) for flip in range(2, nf, 2)]
    passed = [own] + [after(part, *ties) if ties else part for part in straight[1:]]
    crossed = [swap_fsdp(part, 1, nf) for part in passed]
    whole = jnp.zeros((nf * band, width), own.dtype)
    for k in range(nf // 2):
        whole = lax.dynamic_update_slice(whole, straight[k], ((me ^ (2 * k)) * band, 0))
        whole = lax.dynamic_update_slice(whole, crossed[k], ((me ^ (2 * k + 1)) * band, 0))
    return whole


def direct_reduce(terms, nf, meanwhile):
    band, width = (terms.shape[0] // nf, terms.shape[1])
    spread = lax.all_to_all(terms.reshape(nf, band, width), "fsdp", split_axis=0, concat_axis=0)
    spread = after(spread, meanwhile)
    return jnp.sum(spread.astype(F32), axis=0).astype(BF)


def dot_on(left, right, left_dim, right_dim):
    return lax.dot_general(
        left, right, (((left_dim,), (right_dim,)), ((), ())), preferred_element_type=F32
    )


def pick_grad(sources, flags, at):
    if len(sources) == 1:
        return sources[0][...]
    return jnp.where(flags[at] > 0, sources[1][...], sources[0][...])


def update_body(group, count, pieces, flags, refs):
    grads = refs[: group * count]
    lefts = refs[group * count : group * (count + pieces)]
    rights = refs[group * (count + pieces) : group * (count + pieces + 1)]
    master_ref, new_ref, low_ref = (refs[group * (count + pieces + 1)], refs[-2], refs[-1])
    base = pl.program_id(0) * group
    shaped = []
    for j in range(group):
        grad = pick_grad(grads[j * count : (j + 1) * count], flags, base + j)
        product = dot_on(lefts[j][...], grad[: lefts[j].shape[1]], 1, 0)
        if pieces > 1:
            product = product + dot_on(lefts[group + j][...], grad[lefts[j].shape[1] :], 0, 0)
        shaped.append(product.astype(BF))
    shaped = [dot_on(shaped[j], rights[j][...], 1, 0) for j in range(group)]
    scale = 1.0 / (shaped[0].shape[0] * shaped[0].shape[1])
    powers = [jnp.sum(jnp.sum(s * s, axis=0, keepdims=True), axis=1, keepdims=True) for s in shaped]
    factors = [-RATE * lax.rsqrt(power * scale + EPSILON) for power in powers]
    for j in range(group):
        at = pl.ds(j * BC, BC)
        fresh = master_ref[:, at] + shaped[j] * factors[j]
        new_ref[:, at] = fresh
        low_ref[:, at] = fresh.astype(BF)


def pack_roots(roots):
    slots, rows = roots.shape[:2]
    group = 3 if slots % 3 == 0 else 1
    rest = rows - BC

    def body(root_ref, first_ref, rest_ref):
        for j in range(group):
            first_ref[j] = root_ref[j, :, :BC]
            rest_ref[j] = root_ref[j, :, BC:].astype(F32).T.astype(BF)

    def slab(shape):
        return pl.BlockSpec((group,) + shape, lambda i: (i, 0, 0))

    return pl.pallas_call(
        body,
        grid=(slots // group,),
        in_specs=[slab((rows, rows))],
        out_specs=[slab((rows, BC)), slab((rest, rows))],
        out_shape=[
            jax.ShapeDtypeStruct((slots, rows, BC), BF),
            jax.ShapeDtypeStruct((slots, rest, rows), BF),
        ],
        compiler_params=pltpu.CompilerParams(vmem_limit_bytes=VMEM_LIMIT),
        name="pack_roots",
    )(roots)


def grad_specs(sources, group, skip, band):
    def spec(j, is_second):
        def index(i, part, kind, column, flags, *more):
            at = (i + skip) * group + j
            own = jnp.where(flags[at] > 0, 1, 0) if len(sources) > 1 else 0
            fits = own if is_second else 1 - own
            return (part[at] * fits, kind[at] * fits, 0, column[at] * fits)

        return pl.BlockSpec((None, None, band, BC), index)

    return [spec(j, n > 0) for j in range(group) for n in range(len(sources))]


def update_blocks(sources, places, roots, left_roots, right_roots, master, start, count, group, into):
    band = master.shape[0]
    skip = start // group

    def root_spec(shape, j):
        def index(i, part, kind, column, flags, root):
            return (root[i * group + j], 0, 0)

        return pl.BlockSpec((None,) + shape, index)

    wide = pl.BlockSpec((band, group * BC), lambda i, *tables: (0, i + skip))
    in_specs = grad_specs(sources, group, 0, band)
    in_specs += [root_spec(left.shape[1:], j) for left in left_roots for j in range(group)]
    in_specs += [root_spec(right_roots.shape[1:], j) for j in range(group)]
    in_specs += [wide]
    operands = list(sources) * group + [left for left in left_roots for _ in range(group)]
    operands += [right_roots] * group + [master]
    tables = list(places) + [roots]
    aliases = {}
    if into is not None:
        aliases = {len(tables) + len(operands) + n: n for n in range(2)}
        in_specs += [pl.BlockSpec(memory_space=pl.ANY)] * 2
        operands += list(into)
    return pl.pallas_call(
        lambda *refs: update_body(group, len(sources), len(left_roots), refs[3], refs[5:]),
        grid_spec=pltpu.PrefetchScalarGridSpec(
            num_scalar_prefetch=5,
            grid=(count // group,),
            in_specs=in_specs,
            out_specs=[wide, wide],
        ),
        out_shape=[
            jax.ShapeDtypeStruct(master.shape, F32),
            jax.ShapeDtypeStruct(master.shape, BF),
        ],
        input_output_aliases=aliases,
        compiler_params=pltpu.CompilerParams(vmem_limit_bytes=VMEM_LIMIT),
        name="update_blocks",
    )(*tables, *operands)


def stats_body(group, count, skip, flags, used, refs):
    grads, (left_ref, right_ref) = (refs[: group * count], refs[group * count : group * count + 2])
    grad_out, left_out, right_out = refs[-3:]
    for j in range(group):
        at = (pl.program_id(0) + skip) * group + j
        grad = pick_grad(grads[j * count : (j + 1) * count], flags, at)
        grad = jnp.where(used[at] > 0, grad, jnp.zeros_like(grad))
        grad_out[j] = grad.astype(F32)
        left_out[j] = DECAY * left_ref[j] + (1.0 - DECAY) * dot_on(grad, grad, 1, 1)
        right_out[j] = DECAY * right_ref[j] + (1.0 - DECAY) * dot_on(grad, grad, 0, 0)


def owner_stats(sources, places, used, stat_left, stat_right, start, count, group, into):
    slots, band = (stat_left.shape[0], sources[0].shape[2])
    skip = start // group

    def slab(shape):
        return pl.BlockSpec((group,) + shape, lambda i, *tables: (i + skip, 0, 0))

    shapes = [(band, BC), stat_left.shape[1:], stat_right.shape[1:]]
    in_specs = grad_specs(sources, group, skip, band) + [slab(shapes[1]), slab(shapes[2])]
    operands = list(sources) * group + [stat_left, stat_right]
    tables = list(places) + [used]
    aliases = {}
    if into is not None:
        aliases = {len(tables) + len(operands) + n: n for n in range(3)}
        in_specs += [pl.BlockSpec(memory_space=pl.ANY)] * 3
        operands += list(into)
    return pl.pallas_call(
        lambda *refs: stats_body(group, len(sources), skip, refs[3], refs[4], refs[5:]),
        grid_spec=pltpu.PrefetchScalarGridSpec(
            num_scalar_prefetch=5,
            grid=(count // group,),
            in_specs=in_specs,
            out_specs=[slab(shape) for shape in shapes],
        ),
        out_shape=[jax.ShapeDtypeStruct((slots,) + shape, F32) for shape in shapes],
        input_output_aliases=aliases,
        compiler_params=pltpu.CompilerParams(vmem_limit_bytes=VMEM_LIMIT),
        name="owner_stats",
    )(*tables, *operands)


KEY_SHARDS = 8
TO_SECOND = [(0, 2), (1, 3), (2, 4), (3, 5)]
TO_NEXT = [(0, 1), (1, 2), (2, 3)]
ONWARDS = [(4, 6), (5, 7)]
ACROSS = [(4, 5), (5, 4), (6, 7), (7, 6)]
FIRST_SOURCE = [-1, -1, 0, 1, 2, 3, 2, 3]
SECOND_SOURCE = [-1, 0, 1, 2, 3, 2, 3, 2]


def backwards(pairs):
    return [(dst, src) for src, dst in pairs]


def pick_static(table, index):
    values = jnp.asarray(table, jnp.int32)
    hit = jnp.arange(len(table), dtype=jnp.int32) == index
    return jnp.sum(jnp.where(hit, values, 0))


def key_slots_of(rows, nf):
    me = lax.axis_index("fsdp")
    step = jnp.arange(rows, dtype=jnp.int32)
    if nf != KEY_SHARDS:
        return jnp.arange(rows * nf, dtype=jnp.int32)
    ids = [me * rows + step]
    for table in (FIRST_SOURCE, SECOND_SOURCE):
        source = pick_static(table, me)
        ids.append(jnp.where(source >= 0, source * rows + step, -1))
    return jnp.concatenate(ids)


def spread_keys(own, nf):
    if nf != KEY_SHARDS:
        return lax.all_gather(own, "fsdp", axis=0, tiled=True)
    second = lax.ppermute(own, "fsdp", TO_SECOND)
    following = lax.ppermute(own, "fsdp", TO_NEXT)
    onward = lax.ppermute(second, "fsdp", ONWARDS)
    crossed = lax.ppermute(second, "fsdp", ACROSS[:2])
    crossed_on = lax.ppermute(onward, "fsdp", ACROSS[2:])
    return jnp.concatenate([own, second + onward, following + crossed + crossed_on], axis=0)


def return_key_grads(terms, rows, nf):
    if nf != KEY_SHARDS:
        return lax.psum_scatter(
            terms.astype(BF), "fsdp", scatter_dimension=0, tiled=True
        ).astype(F32)
    first = terms[rows : 2 * rows]
    second = terms[2 * rows :].astype(BF)
    total = terms[:rows] + lax.ppermute(second, "fsdp", backwards(TO_NEXT)).astype(F32)
    first = first + lax.ppermute(second, "fsdp", ACROSS).astype(F32)
    first = first + lax.ppermute(first.astype(BF), "fsdp", backwards(ONWARDS)).astype(F32)
    return total + lax.ppermute(first.astype(BF), "fsdp", backwards(TO_SECOND)).astype(F32)


def attend(query_low, keys, values, visible):
    scores = jnp.einsum("thd,kd->thk", query_low, keys, preferred_element_type=F32) * SCALE
    scores = jnp.where(visible[:, None, :], scores, MASKED)
    highest = jnp.max(scores, axis=-1, keepdims=True)
    expo = jnp.exp(scores - highest)
    probs = expo / jnp.sum(expo, axis=-1, keepdims=True)
    mixed = jnp.einsum("thk,kd->thd", probs.astype(BF), values, preferred_element_type=F32)
    return (mixed, probs)


def attend_back(query_low, keys, values, probs, low_mixed):
    grad_probs = jnp.einsum("thd,kd->thk", low_mixed, values, preferred_element_type=F32)
    row_dot = jnp.sum(grad_probs * probs, axis=-1, keepdims=True)
    grad_scores = (probs * (grad_probs - row_dot)).astype(BF)
    grad_queries = jnp.einsum("thk,kd->thd", grad_scores, keys, preferred_element_type=F32) * SCALE
    key_terms = (
        jnp.einsum("thk,thd->kd", grad_scores, query_low, preferred_element_type=F32) * SCALE
    )
    value_terms = jnp.einsum("thk,thd->kd", probs.astype(BF), low_mixed, preferred_element_type=F32)
    return (grad_queries, key_terms, value_terms)


def local(
    tokens,
    cotangent,
    lengths,
    master,
    gains,
    gain_stats,
    owner,
    stat_left,
    stat_right,
    root_left,
    root_right,
):
    nd = lax.axis_size("dp")
    nf = lax.axis_size("fsdp")
    dp_me = lax.axis_index("dp")
    core = dp_me % 2
    micros = tokens.shape[0]
    rows = tokens.shape[2]
    count = micros * rows
    band = master.shape[0]
    capacity = stat_left.shape[1]
    first = lax.axis_index("fsdp") * rows
    pre_attn, post_attn, pre_ffw, post_ffw, query_gain, key_gain = split_gains(gains)

    per = -(-FF_BLOCKS // nd)
    width = per * BC
    start = jnp.minimum(dp_me * per, FF_BLOCKS - per)
    fresh = dp_me * per - start
    gate_at = ATTN_BLOCKS * BC

    def columns(at, size):
        return lax.dynamic_slice(master, (0, at), (band, size)).astype(BF)

    def gather_relative(bands, *ties):
        parts = [gather_parts(part, nd) for part in bands]
        if ties:
            parts = [[after(piece, *ties) for piece in pieces] for pieces in parts]
        out = jnp.zeros((nd, len(bands)) + bands[0].shape, BF)
        for kind, pieces in enumerate(parts):
            for place, piece in enumerate(pieces):
                out = lax.dynamic_update_slice(
                    out, piece[None, None], (place, kind) + (0,) * piece.ndim
                )
        return out

    def gather_columns(bands):
        out = jnp.zeros((nd, 1, band, sum(part.shape[1] for part in bands)), BF)
        at = 0
        for part in bands:
            for place, piece in enumerate(gather_parts(part, nd)):
                out = lax.dynamic_update_slice(out, piece[None, None], (place, 0, 0, at))
            at += part.shape[1]
        return out

    def halves(at, size, first_ties, next_ties):
        part = size // 2
        cols = columns(at + core * part, part)
        mine = gather_rows(after(cols, *first_ties) if first_ties else cols, nf, next_ties)
        whole = jnp.zeros((D, size), BF)
        whole = lax.dynamic_update_slice(whole, mine, (0, core * part))
        return lax.dynamic_update_slice(whole, swap_core(mine, nd), (0, (1 - core) * part))

    w_qkv = halves(0, QKVW, (), ())
    gate_cols = columns(gate_at + start * BC, width)
    up_cols = columns(gate_at + FF + start * BC, width)
    down_cols = columns(gate_at + 2 * FF + start * BC, width)
    keep = (jnp.arange(width, dtype=jnp.int32) >= fresh * BC)[None, :]
    down_cols = jnp.where(keep, down_cols, jnp.zeros_like(down_cols))
    both_cols = jnp.concatenate([gate_cols, up_cols], axis=1)
    w_both = lax.all_gather(both_cols, "fsdp", axis=0, tiled=True)
    w_gate, w_up = (w_both[:, :width], w_both[:, width:])
    w_down = lax.all_gather(down_cols, "fsdp", axis=0, tiled=True)

    flat_in = tokens.astype(F32).reshape(count, D)
    normed = rms_gain(flat_in, pre_attn).astype(BF)
    projected = dot_nn(normed, w_qkv)
    queries = projected[:, :OUTW].reshape(count, HEADS, HD)
    keys = projected[:, OUTW : OUTW + HD]
    values = projected[:, OUTW + HD :]
    slots = first + jnp.arange(rows, dtype=jnp.int32)
    _, positions = slot_layout(slots)
    cosine, sine = rope_tables(positions)
    cosine, sine = (jnp.tile(cosine, (micros, 1)), jnp.tile(sine, (micros, 1)))
    rot_queries, rot_keys = prepare_heads(queries, keys, query_gain, key_gain, cosine, sine)
    query_low = rot_queries.astype(BF).reshape(micros, rows, HEADS, HD)
    own_keys = jnp.concatenate([rot_keys.astype(BF), values.astype(BF)], axis=1)
    key_buffers = [spread_keys(own_keys[m * rows : (m + 1) * rows], nf) for m in range(micros)]
    key_slots = key_slots_of(rows, nf)
    w_out = halves(QKVW, OUTW, (projected,), (key_buffers[0],))
    keys_all = [buffer[:, :HD] for buffer in key_buffers]
    values_all = [buffer[:, HD:] for buffer in key_buffers]
    all_probs, all_attended = [], []
    for m in range(micros):
        visible = visibility(slots, key_slots, lengths[m, 0])
        mixed, probs = attend(query_low[m], keys_all[m], values_all[m], visible)
        all_probs.append(probs)
        all_attended.append(mixed.reshape(rows, OUTW).astype(BF))

    half = (nd // 2) * rows
    outputs, saved, gathered_in, gathered_two, hiddens, low_gates, low_ups = [], [], [], [], [], [], []
    grad_resids, gain_terms, low_ones = [], [], []
    for m in range(micros):
        part_in = flat_in[m * rows : (m + 1) * rows]
        branch_one = dot_nt(all_attended[m], w_out)
        resid = part_in + rms_gain(branch_one, post_attn)
        ffw_in = rms_gain(resid, pre_ffw).astype(BF)
        gathered_in.append(gather_dp(ffw_in, nd))
        saved.append([branch_one, resid])
    partials = []
    for m in range(micros):
        every_in = gathered_in[m]
        if m:
            every_in = after(every_in, hiddens[-1])
        gate = dot_nn(every_in, w_gate)
        up = dot_nn(every_in, w_up)
        hidden = (jax.nn.gelu(gate, approximate=True) * up).astype(BF)
        hiddens.append(hidden)
        saved[m] += [gate, up]
    for m in range(micros):
        hidden = after(hiddens[m], *(partials[-1] if m else hiddens[-1:]))
        away = dot_nt(hidden[half:], w_down).astype(BF)
        partials.append((away, dot_nt(after(hidden[:half], away), w_down)))
    last = partials[-1][1]
    for m in range(micros):
        branch_one, resid, gate, up = saved[m]
        branch_two = scatter_sum_dp(partials[m][1], partials[m][0], nd)
        outputs.append((resid + rms_gain(branch_two, post_ffw)).astype(BF))
        upstream = cotangent[m, 0].astype(F32)
        grad_two, grad_post_ffw = jax.vjp(rms_gain, branch_two, post_ffw)[1](upstream)
        gathered_two.append(gather_dp(grad_two.astype(BF), nd))
        saved[m] += [upstream, grad_post_ffw]
    def weight_term(lefts, rights, follow):
        left = jnp.concatenate(lefts, axis=0)
        term = dot_tn(after(left, *follow), jnp.concatenate(rights, axis=0))
        return term.astype(BF)

    def sum_rows(term):
        return lax.psum_scatter(term, "fsdp", scatter_dimension=0, tiled=True)

    for m in range(micros):
        gate, up = saved[m][2:4]
        if m == micros - 1:
            last = down_term = weight_term(gathered_two, hiddens, (last,))
        grad_hidden = dot_nn(after(gathered_two[m], last), w_down)
        grad_gate, grad_up = jax.vjp(
            lambda gate_in, up_in: jax.nn.gelu(gate_in, approximate=True) * up_in, gate, up
        )[1](grad_hidden)
        low_gates.append(grad_gate.astype(BF))
        low_ups.append(grad_up.astype(BF))
        last = low_ups[-1]

    def from_x(root, *ties):
        root = after(root, *ties) if ties else root
        return [root] + [shift_x(root, nd, k) for k in range(1, nd // 2)]

    right_mine = from_x(root_right[0], *gathered_two)
    down_band = sum_rows(down_term)
    gate_term = weight_term(gathered_in, low_gates, (last,))
    up_term = weight_term(gathered_in, low_ups, (gate_term,))
    both_term = jnp.concatenate([gate_term, up_term], axis=1)
    both_band = sum_rows(both_term)
    last = both_term
    for m in range(micros):
        branch_one, resid, _, _, upstream, grad_post_ffw = saved[m]
        gate_in, up_in = (after(low_gates[m], last, *right_mine[1:]), low_ups[m])
        away = dot_nt(gate_in[half:], w_gate) + dot_nt(up_in[half:], w_up)
        gate_in = after(gate_in, away)
        last = dot_nt(gate_in[:half], w_gate) + dot_nt(up_in[:half], w_up)
        grad_ffw_in = scatter_sum_dp(last, away, nd)
        grad_resid, grad_pre_ffw = jax.vjp(rms_gain, resid, pre_ffw)[1](grad_ffw_in)
        grad_resid = upstream + grad_resid
        grad_one, grad_post_attn = jax.vjp(rms_gain, branch_one, post_attn)[1](grad_resid)
        grad_resids.append(grad_resid)
        low_ones.append(grad_one.astype(BF))
        gain_terms.append((grad_post_attn, grad_pre_ffw, grad_post_ffw))

    low_one = jnp.concatenate(low_ones, axis=0)
    attended = jnp.concatenate(all_attended, axis=0)
    owners_at = part_owners(nd)
    qkv_per, out_per = (-(-QKVW // (BC * nd)), -(-OUTW // (BC * nd)))

    def term_over_dp(left, right, per_index):
        size = per_index * BC
        right = jnp.pad(right, ((0, 0), (0, nd * size - right.shape[1])))
        terms = [
            dot_tn(left, lax.dynamic_slice(right, (0, index * size), (count, size)))
            for index in owners_at
        ]
        mine, away = (terms[: nd // 2], terms[nd // 2 :])
        away = jnp.concatenate(away, axis=0).astype(BF)
        return (scatter_sum_dp(jnp.concatenate(mine, axis=0), away, nd), away)

    out_sum, _ = term_over_dp(low_one, attended, out_per)
    left_root = after(root_left[0], low_one)
    left_pieces = pack_roots(left_root) if band > BC else [left_root]
    left_mine = [from_x(left) for left in left_pieces]
    left_here = [piece for mine in left_mine for piece in mine[1:]]

    low_mixed = dot_nn(after(low_one, down_band, *left_pieces), w_out).astype(BF).reshape(micros, rows, HEADS, HD)
    grad_queries, key_terms = [], []
    for m in range(micros):
        for_queries, for_keys, for_values = attend_back(
            query_low[m], keys_all[m], values_all[m], all_probs[m], low_mixed[m]
        )
        grad_queries.append(for_queries)
        terms = jnp.concatenate([for_keys, for_values], axis=1)
        key_terms.append(return_key_grads(terms, rows, nf))
        last = terms
    own_terms = after(jnp.concatenate(key_terms, axis=0), *left_here)
    grad_keys, grad_values = (own_terms[:, :HD], own_terms[:, HD:])

    def heads_only(query_in, key_in, query_scale, key_scale):
        return prepare_heads(query_in, key_in, query_scale, key_scale, cosine, sine)

    pull_heads = jax.vjp(heads_only, queries, keys, query_gain, key_gain)[1]
    grad_query_pre, grad_key_pre, grad_query_gain, grad_key_gain = pull_heads(
        (jnp.concatenate(grad_queries, axis=0), grad_keys)
    )
    low_projected = jnp.concatenate(
        [grad_query_pre.reshape(count, OUTW), grad_key_pre, grad_values], axis=1
    ).astype(BF)
    grad_normed = dot_nt(low_projected, w_qkv)
    grad_in, grad_pre_attn = jax.vjp(rms_gain, flat_in, pre_attn)[1](grad_normed)
    input_grad = (jnp.concatenate(grad_resids, axis=0) + grad_in).astype(BF)

    qkv_sum, qkv_away = term_over_dp(after(normed, both_band), low_projected, qkv_per)
    attn_sum = jnp.concatenate([qkv_sum, out_sum], axis=1).astype(BF)
    ff_all = gather_columns([both_band, down_band])

    def all_parts(mine, *ties):
        parts = mine + [swap_core(piece, nd) for piece in mine]
        parts = [after(piece, *ties) for piece in parts]
        out = jnp.zeros((nd,) + parts[0].shape, BF)
        for place, piece in enumerate(parts):
            out = lax.dynamic_update_slice(out, piece[None], (place,) + (0,) * piece.ndim)
        return out.reshape((nd * capacity,) + out.shape[2:])

    right_roots = all_parts(right_mine, qkv_away)
    left_roots = [all_parts(mine, qkv_away) for mine in left_mine]

    def relative(index):
        nx = nd // 2
        flip = (index % 2) ^ core
        return flip * nx + (dp_me // 2 + nx - index // 2) % nx

    ff_index = np.arange(3 * FF_BLOCKS)
    ff_dp = np.minimum(ff_index % FF_BLOCKS // per, nd - 1)
    ff_column = ff_index % FF_BLOCKS - np.minimum(ff_dp * per, FF_BLOCKS - per)
    ff_column = ff_column + ff_index // FF_BLOCKS * per
    qkv_index, out_index = (np.arange(QKVW // BC), np.arange(OUTW // BC))
    attn_dp = np.concatenate([qkv_index // qkv_per, out_index // out_per])
    attn_column = np.concatenate([qkv_index % qkv_per, qkv_per + out_index % out_per])
    part_of = relative(
        jnp.asarray(np.concatenate([attn_dp, ff_dp]).astype(np.int32))
    )
    kind_of = jnp.asarray(
        np.zeros(NBLK).astype(np.int32)
    )
    column_of = jnp.asarray(np.concatenate([attn_column, ff_column]).astype(np.int32))

    owners = owner[:, 0]
    index = jnp.arange(NBLK, dtype=jnp.int32)
    before = (owners[:, None] == owners[None, :]) & (index[None, :] < index[:, None])
    ranks = jnp.sum(before.astype(jnp.int32), axis=1)
    my_slots = jnp.arange(capacity, dtype=jnp.int32)
    mine = (owners[None, :] == dp_me) & (ranks[None, :] == my_slots[:, None])
    used = jnp.sum(mine.astype(jnp.int32), axis=1)

    def of_slot(values):
        return jnp.sum(jnp.where(mine, values[None, :], 0), axis=1)

    is_attn = (index < ATTN_BLOCKS).astype(jnp.int32)
    places = (part_of, kind_of, column_of, is_attn)
    early = tuple(table[LATE:] for table in places)
    late = tuple(table[:LATE] for table in places)
    root_of = relative(owners) * capacity + ranks
    root_args = (left_roots, right_roots, master)
    slot_places = tuple(of_slot(table) for table in places)
    group = 3 if (capacity - LATE) % 3 == 0 else 1
    stat_args = (slot_places, used, stat_left[0], stat_right[0])
    fresh_stats = owner_stats([ff_all], *stat_args, LATE, capacity - LATE, group, None)
    attn_band = direct_reduce(after(attn_sum, both_band), nf, fresh_stats[0])
    attn_all = gather_relative([attn_band])
    fresh_arrays = update_blocks(
        [ff_all], early, root_of[LATE:], left_roots, right_roots, after(master, attn_band), LATE, NBLK - LATE, 7, None
    )
    both = [ff_all, attn_all]
    new_master, new_weights = update_blocks(
        both, late, root_of[:LATE], *root_args, 0, LATE, 7, fresh_arrays
    )
    slot_grads, new_left, new_right = owner_stats(both, *stat_args, 0, LATE, group, fresh_stats)

    post_attn_sum = sum(entry[0] for entry in gain_terms)
    pre_ffw_sum = sum(entry[1] for entry in gain_terms)
    post_ffw_sum = sum(entry[2] for entry in gain_terms)
    gain_sum = jnp.concatenate(
        [grad_pre_attn, post_attn_sum, pre_ffw_sum, post_ffw_sum, grad_query_gain, grad_key_gain]
    )
    gain_grad = sum_everywhere(after(gain_sum, attn_band), nd, nf)
    new_gain_stats = DECAY * gain_stats + (1.0 - DECAY) * gain_grad * gain_grad
    gain_change = -GAIN_RATE * gain_grad * lax.rsqrt(new_gain_stats)
    return (
        jnp.stack(outputs)[:, None],
        input_grad.reshape(micros, 1, rows, D),
        slot_grads[None],
        gain_grad,
        new_left[None],
        new_right[None],
        new_master,
        new_weights,
        new_gain_stats,
        gain_change,
    )


def solution(mesh):
    in_specs = (
        P(None, "dp", "fsdp", None),
        P(None, "dp", "fsdp", None),
        P(None, "dp", None),
        P("fsdp", None),
        P(),
        P(),
        P("fsdp", None),
        P("fsdp", "dp", None, None),
        P("fsdp", "dp", None, None),
        P("fsdp", "dp", None, None),
        P("fsdp", "dp", None, None),
    )
    out_specs = (
        P(None, "dp", "fsdp", None),
        P(None, "dp", "fsdp", None),
        P("fsdp", "dp", None, None),
        P(),
        P("fsdp", "dp", None, None),
        P("fsdp", "dp", None, None),
        P("fsdp", None),
        P("fsdp", None),
        P(),
        P(),
    )
    return jax.shard_map(local, mesh=mesh, in_specs=in_specs, out_specs=out_specs, check_vma=False)
```

```python
import jax
import jax.numpy as jnp
import numpy as np
from jax import lax
from jax.experimental import pallas as pl
from jax.experimental.pallas import tpu as pltpu
from jax.sharding import PartitionSpec as P

D = 1152
HEADS = 4
HD = 256
FF = 6912
WIN = 512
PROMPT = 1024
CONT = 8
CLEN = 128
BC = 128
GLEN = 2048
QKVW = 1536
OUTW = HEADS * HD
NBLK = 182
ATTN_BLOCKS = (QKVW + OUTW) // BC
FF_BLOCKS = FF // BC

EPSILON = 1e-06
MASKED = -1e30
RATE = 0.02
GAIN_RATE = 0.05
DECAY = 0.5
SCALE = HD ** (-0.5)
DIRECT_MAX = 8
LATE = 21
VMEM_LIMIT = 40 * 1024 * 1024
BF = jnp.bfloat16
F32 = jnp.float32


def rms_gain(values, gain):
    return values * lax.rsqrt(jnp.mean(values * values, axis=-1, keepdims=True) + EPSILON) * gain


def rope_tables(positions):
    half_width = HD // 2
    freqs = 10000.0 ** (-2.0 * jnp.arange(half_width, dtype=F32) / HD)
    angles = positions.astype(F32)[:, None] * freqs[None, :]
    return (jnp.cos(angles), jnp.sin(angles))


def rotate(values, cosine, sine):
    half_width = values.shape[-1] // 2
    first_half = values[..., :half_width]
    second_half = values[..., half_width:]
    return jnp.concatenate(
        [first_half * cosine - second_half * sine, second_half * cosine + first_half * sine],
        axis=-1,
    )


def slot_layout(slots):
    in_prompt = slots < PROMPT
    offset = slots - PROMPT
    segment = jnp.where(in_prompt, -1, offset // CLEN)
    position = jnp.where(in_prompt, slots, PROMPT + offset % CLEN)
    return (segment, position)


def visibility(query_slots, key_slots, lens):
    query_seg, query_pos = slot_layout(query_slots)
    key_seg, key_pos = slot_layout(key_slots)
    picks = key_seg[:, None] == jnp.arange(CONT, dtype=jnp.int32)[None, :]
    key_len = jnp.sum(jnp.where(picks, lens[None, :], 0), axis=1)
    key_used = (key_seg < 0) | (key_pos - PROMPT < key_len)
    distance = query_pos[:, None] - key_pos[None, :]
    same_part = (key_seg[None, :] < 0) | (key_seg[None, :] == query_seg[:, None])
    present = key_slots >= 0
    return (distance >= 0) & (distance < WIN) & same_part & (key_used & present)[None, :]


def split_gains(gains):
    return (
        gains[:D],
        gains[D : 2 * D],
        gains[2 * D : 3 * D],
        gains[3 * D : 4 * D],
        gains[4 * D : 4 * D + HD],
        gains[4 * D + HD :],
    )


def prepare_heads(queries, keys, query_gain, key_gain, cosine, sine):
    rot_queries = rotate(rms_gain(queries, query_gain), cosine[:, None, :], sine[:, None, :])
    rot_keys = rotate(rms_gain(keys, key_gain), cosine, sine)
    return (rot_queries, rot_keys)


def dot_nn(left, right):
    return jnp.dot(left, right, preferred_element_type=F32)


def dot_nt(left, right):
    return lax.dot_general(left, right, (((1,), (1,)), ((), ())), preferred_element_type=F32)


def dot_tn(left, right):
    return lax.dot_general(left, right, (((0,), (0,)), ((), ())), preferred_element_type=F32)


def swap_core(value, nd):
    return lax.ppermute(value, "dp", [(e, e ^ 1) for e in range(nd)])


def shift_x(value, nd, step):
    nx = nd // 2
    pairs = [(e, ((e // 2 + step) % nx) * 2 + e % 2) for e in range(nd)]
    return lax.ppermute(value, "dp", pairs)


def gather_parts(value, nd):
    mine = [value] + [shift_x(value, nd, k) for k in range(1, nd // 2)]
    return mine + [swap_core(part, nd) for part in mine]


def gather_dp(value, nd):
    return jnp.concatenate(gather_parts(value, nd), axis=0)


def part_owners(nd):
    nx = nd // 2
    me = lax.axis_index("dp")
    x, core = me // 2, me % 2
    out = []
    for flip in range(2):
        for k in range(nx):
            out.append(((x + nx - k) % nx) * 2 + (core if flip == 0 else 1 - core))
    return out


def scatter_sum_dp(own_half, other_half, nd):
    nx = nd // 2
    received = swap_core(other_half.astype(BF), nd)
    total = own_half + received.astype(F32)
    rows = total.shape[0] // nx
    result = total[:rows]
    for k in range(1, nx):
        sent = total[k * rows : (k + 1) * rows].astype(BF)
        result = result + shift_x(sent, nd, nx - k).astype(F32)
    return result


def sum_everywhere(value, nd, nf):
    for axis, count in (("dp", nd), ("fsdp", nf)):
        step = 1
        while step < count:
            value = value + lax.ppermute(value, axis, [(e, e ^ step) for e in range(count)])
            step *= 2
    return value


def after(value, *others):
    return lax.optimization_barrier((value,) + others)[0]


def swap_fsdp(value, flip, nf):
    return lax.ppermute(value, "fsdp", [(e, e ^ flip) for e in range(nf)])


def gather_rows(own, nf, ties=()):
    if nf > DIRECT_MAX:
        return lax.all_gather(own, "fsdp", axis=0, tiled=True)
    me = lax.axis_index("fsdp")
    band, width = own.shape
    straight = [own] + [swap_fsdp(own, flip, nf) for flip in range(2, nf, 2)]
    passed = [own] + [after(part, *ties) if ties else part for part in straight[1:]]
    crossed = [swap_fsdp(part, 1, nf) for part in passed]
    whole = jnp.zeros((nf * band, width), own.dtype)
    for k in range(nf // 2):
        whole = lax.dynamic_update_slice(whole, straight[k], ((me ^ (2 * k)) * band, 0))
        whole = lax.dynamic_update_slice(whole, crossed[k], ((me ^ (2 * k + 1)) * band, 0))
    return whole


def direct_reduce(terms, nf, meanwhile):
    band, width = (terms.shape[0] // nf, terms.shape[1])
    spread = lax.all_to_all(terms.reshape(nf, band, width), "fsdp", split_axis=0, concat_axis=0)
    spread = after(spread, meanwhile)
    return jnp.sum(spread.astype(F32), axis=0).astype(BF)


def dot_on(left, right, left_dim, right_dim):
    return lax.dot_general(
        left, right, (((left_dim,), (right_dim,)), ((), ())), preferred_element_type=F32
    )


def pick_grad(sources, flags, at):
    if len(sources) == 1:
        return sources[0][...]
    return jnp.where(flags[at] > 0, sources[1][...], sources[0][...])


def update_body(group, count, pieces, flags, refs):
    grads = refs[: group * count]
    lefts = refs[group * count : group * (count + pieces)]
    rights = refs[group * (count + pieces) : group * (count + pieces + 1)]
    master_ref, new_ref, low_ref = (refs[group * (count + pieces + 1)], refs[-2], refs[-1])
    base = pl.program_id(0) * group
    shaped = []
    for j in range(group):
        grad = pick_grad(grads[j * count : (j + 1) * count], flags, base + j)
        product = dot_on(lefts[j][...], grad[: lefts[j].shape[1]], 1, 0)
        if pieces > 1:
            product = product + dot_on(lefts[group + j][...], grad[lefts[j].shape[1] :], 0, 0)
        shaped.append(product.astype(BF))
    shaped = [dot_on(shaped[j], rights[j][...], 1, 0) for j in range(group)]
    scale = 1.0 / (shaped[0].shape[0] * shaped[0].shape[1])
    powers = [jnp.sum(jnp.sum(s * s, axis=0, keepdims=True), axis=1, keepdims=True) for s in shaped]
    factors = [-RATE * lax.rsqrt(power * scale + EPSILON) for power in powers]
    for j in range(group):
        at = pl.ds(j * BC, BC)
        fresh = master_ref[:, at] + shaped[j] * factors[j]
        new_ref[:, at] = fresh
        low_ref[:, at] = fresh.astype(BF)


def pack_roots(roots):
    slots, rows = roots.shape[:2]
    group = 3 if slots % 3 == 0 else 1
    rest = rows - BC

    def body(root_ref, first_ref, rest_ref):
        for j in range(group):
            first_ref[j] = root_ref[j, :, :BC]
            rest_ref[j] = root_ref[j, :, BC:].astype(F32).T.astype(BF)

    def slab(shape):
        return pl.BlockSpec((group,) + shape, lambda i: (i, 0, 0))

    return pl.pallas_call(
        body,
        grid=(slots // group,),
        in_specs=[slab((rows, rows))],
        out_specs=[slab((rows, BC)), slab((rest, rows))],
        out_shape=[
            jax.ShapeDtypeStruct((slots, rows, BC), BF),
            jax.ShapeDtypeStruct((slots, rest, rows), BF),
        ],
        compiler_params=pltpu.CompilerParams(vmem_limit_bytes=VMEM_LIMIT),
        name="pack_roots",
    )(roots)


def grad_specs(sources, group, skip, band):
    def spec(j, is_second):
        def index(i, part, kind, column, flags, *more):
            at = (i + skip) * group + j
            own = jnp.where(flags[at] > 0, 1, 0) if len(sources) > 1 else 0
            fits = own if is_second else 1 - own
            return (part[at] * fits, kind[at] * fits, 0, column[at] * fits)

        return pl.BlockSpec((None, None, band, BC), index)

    return [spec(j, n > 0) for j in range(group) for n in range(len(sources))]


def update_blocks(sources, places, roots, left_roots, right_roots, master, start, count, group, into):
    band = master.shape[0]
    skip = start // group

    def root_spec(shape, j):
        def index(i, part, kind, column, flags, root):
            return (root[i * group + j], 0, 0)

        return pl.BlockSpec((None,) + shape, index)

    wide = pl.BlockSpec((band, group * BC), lambda i, *tables: (0, i + skip))
    in_specs = grad_specs(sources, group, 0, band)
    in_specs += [root_spec(left.shape[1:], j) for left in left_roots for j in range(group)]
    in_specs += [root_spec(right_roots.shape[1:], j) for j in range(group)]
    in_specs += [wide]
    operands = list(sources) * group + [left for left in left_roots for _ in range(group)]
    operands += [right_roots] * group + [master]
    tables = list(places) + [roots]
    aliases = {}
    if into is not None:
        aliases = {len(tables) + len(operands) + n: n for n in range(2)}
        in_specs += [pl.BlockSpec(memory_space=pl.ANY)] * 2
        operands += list(into)
    return pl.pallas_call(
        lambda *refs: update_body(group, len(sources), len(left_roots), refs[3], refs[5:]),
        grid_spec=pltpu.PrefetchScalarGridSpec(
            num_scalar_prefetch=5,
            grid=(count // group,),
            in_specs=in_specs,
            out_specs=[wide, wide],
        ),
        out_shape=[
            jax.ShapeDtypeStruct(master.shape, F32),
            jax.ShapeDtypeStruct(master.shape, BF),
        ],
        input_output_aliases=aliases,
        compiler_params=pltpu.CompilerParams(vmem_limit_bytes=VMEM_LIMIT),
        name="update_blocks",
    )(*tables, *operands)


def stats_body(group, count, skip, flags, used, refs):
    grads, (left_ref, right_ref) = (refs[: group * count], refs[group * count : group * count + 2])
    grad_out, left_out, right_out = refs[-3:]
    for j in range(group):
        at = (pl.program_id(0) + skip) * group + j
        grad = pick_grad(grads[j * count : (j + 1) * count], flags, at)
        grad = jnp.where(used[at] > 0, grad, jnp.zeros_like(grad))
        grad_out[j] = grad.astype(F32)
        left_out[j] = DECAY * left_ref[j] + (1.0 - DECAY) * dot_on(grad, grad, 1, 1)
        right_out[j] = DECAY * right_ref[j] + (1.0 - DECAY) * dot_on(grad, grad, 0, 0)


def owner_stats(sources, places, used, stat_left, stat_right, start, count, group, into):
    slots, band = (stat_left.shape[0], sources[0].shape[2])
    skip = start // group

    def slab(shape):
        return pl.BlockSpec((group,) + shape, lambda i, *tables: (i + skip, 0, 0))

    shapes = [(band, BC), stat_left.shape[1:], stat_right.shape[1:]]
    in_specs = grad_specs(sources, group, skip, band) + [slab(shapes[1]), slab(shapes[2])]
    operands = list(sources) * group + [stat_left, stat_right]
    tables = list(places) + [used]
    aliases = {}
    if into is not None:
        aliases = {len(tables) + len(operands) + n: n for n in range(3)}
        in_specs += [pl.BlockSpec(memory_space=pl.ANY)] * 3
        operands += list(into)
    return pl.pallas_call(
        lambda *refs: stats_body(group, len(sources), skip, refs[3], refs[4], refs[5:]),
        grid_spec=pltpu.PrefetchScalarGridSpec(
            num_scalar_prefetch=5,
            grid=(count // group,),
            in_specs=in_specs,
            out_specs=[slab(shape) for shape in shapes],
        ),
        out_shape=[jax.ShapeDtypeStruct((slots,) + shape, F32) for shape in shapes],
        input_output_aliases=aliases,
        compiler_params=pltpu.CompilerParams(vmem_limit_bytes=VMEM_LIMIT),
        name="owner_stats",
    )(*tables, *operands)


KEY_SHARDS = 8
TO_SECOND = [(0, 2), (1, 3), (2, 4), (3, 5)]
TO_NEXT = [(0, 1), (1, 2), (2, 3)]
ONWARDS = [(4, 6), (5, 7)]
ACROSS = [(4, 5), (5, 4), (6, 7), (7, 6)]
FIRST_SOURCE = [-1, -1, 0, 1, 2, 3, 2, 3]
SECOND_SOURCE = [-1, 0, 1, 2, 3, 2, 3, 2]


def backwards(pairs):
    return [(dst, src) for src, dst in pairs]


def pick_static(table, index):
    values = jnp.asarray(table, jnp.int32)
    hit = jnp.arange(len(table), dtype=jnp.int32) == index
    return jnp.sum(jnp.where(hit, values, 0))


def key_slots_of(rows, nf):
    me = lax.axis_index("fsdp")
    step = jnp.arange(rows, dtype=jnp.int32)
    if nf != KEY_SHARDS:
        return jnp.arange(rows * nf, dtype=jnp.int32)
    ids = [me * rows + step]
    for table in (FIRST_SOURCE, SECOND_SOURCE):
        source = pick_static(table, me)
        ids.append(jnp.where(source >= 0, source * rows + step, -1))
    return jnp.concatenate(ids)


def spread_keys(own, nf):
    if nf != KEY_SHARDS:
        return lax.all_gather(own, "fsdp", axis=0, tiled=True)
    second = lax.ppermute(own, "fsdp", TO_SECOND)
    following = lax.ppermute(own, "fsdp", TO_NEXT)
    onward = lax.ppermute(second, "fsdp", ONWARDS)
    crossed = lax.ppermute(second, "fsdp", ACROSS[:2])
    crossed_on = lax.ppermute(onward, "fsdp", ACROSS[2:])
    return jnp.concatenate([own, second + onward, following + crossed + crossed_on], axis=0)


def return_key_grads(terms, rows, nf):
    if nf != KEY_SHARDS:
        return lax.psum_scatter(
            terms.astype(BF), "fsdp", scatter_dimension=0, tiled=True
        ).astype(F32)
    first = terms[rows : 2 * rows]
    second = terms[2 * rows :].astype(BF)
    total = terms[:rows] + lax.ppermute(second, "fsdp", backwards(TO_NEXT)).astype(F32)
    first = first + lax.ppermute(second, "fsdp", ACROSS).astype(F32)
    first = first + lax.ppermute(first.astype(BF), "fsdp", backwards(ONWARDS)).astype(F32)
    return total + lax.ppermute(first.astype(BF), "fsdp", backwards(TO_SECOND)).astype(F32)


def attend(query_low, keys, values, visible):
    scores = jnp.einsum("thd,kd->thk", query_low, keys, preferred_element_type=F32) * SCALE
    scores = jnp.where(visible[:, None, :], scores, MASKED)
    highest = jnp.max(scores, axis=-1, keepdims=True)
    expo = jnp.exp(scores - highest)
    probs = expo / jnp.sum(expo, axis=-1, keepdims=True)
    mixed = jnp.einsum("thk,kd->thd", probs.astype(BF), values, preferred_element_type=F32)
    return (mixed, probs)


def attend_back(query_low, keys, values, probs, low_mixed):
    grad_probs = jnp.einsum("thd,kd->thk", low_mixed, values, preferred_element_type=F32)
    row_dot = jnp.sum(grad_probs * probs, axis=-1, keepdims=True)
    grad_scores = (probs * (grad_probs - row_dot)).astype(BF)
    grad_queries = jnp.einsum("thk,kd->thd", grad_scores, keys, preferred_element_type=F32) * SCALE
    key_terms = (
        jnp.einsum("thk,thd->kd", grad_scores, query_low, preferred_element_type=F32) * SCALE
    )
    value_terms = jnp.einsum("thk,thd->kd", probs.astype(BF), low_mixed, preferred_element_type=F32)
    return (grad_queries, key_terms, value_terms)


def local(
    tokens,
    cotangent,
    lengths,
    master,
    gains,
    gain_stats,
    owner,
    stat_left,
    stat_right,
    root_left,
    root_right,
):
    nd = lax.axis_size("dp")
    nf = lax.axis_size("fsdp")
    dp_me = lax.axis_index("dp")
    core = dp_me % 2
    micros = tokens.shape[0]
    rows = tokens.shape[2]
    count = micros * rows
    band = master.shape[0]
    capacity = stat_left.shape[1]
    first = lax.axis_index("fsdp") * rows
    pre_attn, post_attn, pre_ffw, post_ffw, query_gain, key_gain = split_gains(gains)

    per = -(-FF_BLOCKS // nd)
    width = per * BC
    start = jnp.minimum(dp_me * per, FF_BLOCKS - per)
    fresh = dp_me * per - start
    gate_at = ATTN_BLOCKS * BC

    def columns(at, size):
        return lax.dynamic_slice(master, (0, at), (band, size)).astype(BF)

    def gather_relative(bands, *ties):
        parts = [gather_parts(part, nd) for part in bands]
        if ties:
            parts = [[after(piece, *ties) for piece in pieces] for pieces in parts]
        out = jnp.zeros((nd, len(bands)) + bands[0].shape, BF)
        for kind, pieces in enumerate(parts):
            for place, piece in enumerate(pieces):
                out = lax.dynamic_update_slice(
                    out, piece[None, None], (place, kind) + (0,) * piece.ndim
                )
        return out

    def gather_columns(bands):
        out = jnp.zeros((nd, 1, band, sum(part.shape[1] for part in bands)), BF)
        at = 0
        for part in bands:
            for place, piece in enumerate(gather_parts(part, nd)):
                out = lax.dynamic_update_slice(out, piece[None, None], (place, 0, 0, at))
            at += part.shape[1]
        return out

    def halves(at, size, first_ties, next_ties):
        part = size // 2
        cols = columns(at + core * part, part)
        mine = gather_rows(after(cols, *first_ties) if first_ties else cols, nf, next_ties)
        whole = jnp.zeros((D, size), BF)
        whole = lax.dynamic_update_slice(whole, mine, (0, core * part))
        return lax.dynamic_update_slice(whole, swap_core(mine, nd), (0, (1 - core) * part))

    w_qkv = halves(0, QKVW, (), ())
    gate_cols = columns(gate_at + start * BC, width)
    up_cols = columns(gate_at + FF + start * BC, width)
    down_cols = columns(gate_at + 2 * FF + start * BC, width)
    keep = (jnp.arange(width, dtype=jnp.int32) >= fresh * BC)[None, :]
    down_cols = jnp.where(keep, down_cols, jnp.zeros_like(down_cols))
    both_cols = jnp.concatenate([gate_cols, up_cols], axis=1)
    w_both = lax.all_gather(both_cols, "fsdp", axis=0, tiled=True)
    w_gate, w_up = (w_both[:, :width], w_both[:, width:])
    w_down = lax.all_gather(down_cols, "fsdp", axis=0, tiled=True)

    flat_in = tokens.astype(F32).reshape(count, D)
    normed = rms_gain(flat_in, pre_attn).astype(BF)
    projected = dot_nn(normed, w_qkv)
    queries = projected[:, :OUTW].reshape(count, HEADS, HD)
    keys = projected[:, OUTW : OUTW + HD]
    values = projected[:, OUTW + HD :]
    slots = first + jnp.arange(rows, dtype=jnp.int32)
    _, positions = slot_layout(slots)
    cosine, sine = rope_tables(positions)
    cosine, sine = (jnp.tile(cosine, (micros, 1)), jnp.tile(sine, (micros, 1)))
    rot_queries, rot_keys = prepare_heads(queries, keys, query_gain, key_gain, cosine, sine)
    query_low = rot_queries.astype(BF).reshape(micros, rows, HEADS, HD)
    own_keys = jnp.concatenate([rot_keys.astype(BF), values.astype(BF)], axis=1)
    key_buffers = [spread_keys(own_keys[m * rows : (m + 1) * rows], nf) for m in range(micros)]
    key_slots = key_slots_of(rows, nf)
    w_out = halves(QKVW, OUTW, (projected,), (key_buffers[0],))
    keys_all = [buffer[:, :HD] for buffer in key_buffers]
    values_all = [buffer[:, HD:] for buffer in key_buffers]
    all_probs, all_attended = [], []
    for m in range(micros):
        visible = visibility(slots, key_slots, lengths[m, 0])
        mixed, probs = attend(query_low[m], keys_all[m], values_all[m], visible)
        all_probs.append(probs)
        all_attended.append(mixed.reshape(rows, OUTW).astype(BF))

    half = (nd // 2) * rows
    outputs, saved, gathered_in, gathered_two, hiddens, low_gates, low_ups = [], [], [], [], [], [], []
    grad_resids, gain_terms, low_ones = [], [], []
    for m in range(micros):
        part_in = flat_in[m * rows : (m + 1) * rows]
        branch_one = dot_nt(all_attended[m], w_out)
        resid = part_in + rms_gain(branch_one, post_attn)
        ffw_in = rms_gain(resid, pre_ffw).astype(BF)
        gathered_in.append(gather_dp(ffw_in, nd))
        saved.append([branch_one, resid])
    partials = []
    for m in range(micros):
        every_in = gathered_in[m]
        if m:
            every_in = after(every_in, hiddens[-1])
        gate = dot_nn(every_in, w_gate)
        up = dot_nn(every_in, w_up)
        hidden = (jax.nn.gelu(gate, approximate=True) * up).astype(BF)
        hiddens.append(hidden)
        saved[m] += [gate, up]
    for m in range(micros):
        hidden = after(hiddens[m], *(partials[-1] if m else hiddens[-1:]))
        away = dot_nt(hidden[half:], w_down).astype(BF)
        partials.append((away, dot_nt(after(hidden[:half], away), w_down)))
    last = partials[-1][1]
    for m in range(micros):
        branch_one, resid, gate, up = saved[m]
        branch_two = scatter_sum_dp(partials[m][1], partials[m][0], nd)
        outputs.append((resid + rms_gain(branch_two, post_ffw)).astype(BF))
        upstream = cotangent[m, 0].astype(F32)
        grad_two, grad_post_ffw = jax.vjp(rms_gain, branch_two, post_ffw)[1](upstream)
        gathered_two.append(gather_dp(grad_two.astype(BF), nd))
        saved[m] += [upstream, grad_post_ffw]
    def weight_term(lefts, rights, follow):
        left = jnp.concatenate(lefts, axis=0)
        term = dot_tn(after(left, *follow), jnp.concatenate(rights, axis=0))
        return term.astype(BF)

    def sum_rows(term):
        return lax.psum_scatter(term, "fsdp", scatter_dimension=0, tiled=True)

    for m in range(micros):
        gate, up = saved[m][2:4]
        if m == micros - 1:
            last = down_term = weight_term(gathered_two, hiddens, (last,))
        grad_hidden = dot_nn(after(gathered_two[m], last), w_down)
        grad_gate, grad_up = jax.vjp(
            lambda gate_in, up_in: jax.nn.gelu(gate_in, approximate=True) * up_in, gate, up
        )[1](grad_hidden)
        low_gates.append(grad_gate.astype(BF))
        low_ups.append(grad_up.astype(BF))
        last = low_ups[-1]

    def from_x(root, *ties):
        root = after(root, *ties) if ties else root
        return [root] + [shift_x(root, nd, k) for k in range(1, nd // 2)]

    right_mine = from_x(root_right[0], *gathered_two)
    down_band = sum_rows(down_term)
    gate_term = weight_term(gathered_in, low_gates, (last,))
    up_term = weight_term(gathered_in, low_ups, (gate_term,))
    both_term = jnp.concatenate([gate_term, up_term], axis=1)
    both_band = sum_rows(both_term)
    last = both_term
    for m in range(micros):
        branch_one, resid, _, _, upstream, grad_post_ffw = saved[m]
        gate_in, up_in = (after(low_gates[m], last, *right_mine[1:]), low_ups[m])
        away = dot_nt(gate_in[half:], w_gate) + dot_nt(up_in[half:], w_up)
        gate_in = after(gate_in, away)
        last = dot_nt(gate_in[:half], w_gate) + dot_nt(up_in[:half], w_up)
        grad_ffw_in = scatter_sum_dp(last, away, nd)
        grad_resid, grad_pre_ffw = jax.vjp(rms_gain, resid, pre_ffw)[1](grad_ffw_in)
        grad_resid = upstream + grad_resid
        grad_one, grad_post_attn = jax.vjp(rms_gain, branch_one, post_attn)[1](grad_resid)
        grad_resids.append(grad_resid)
        low_ones.append(grad_one.astype(BF))
        gain_terms.append((grad_post_attn, grad_pre_ffw, grad_post_ffw))

    low_one = jnp.concatenate(low_ones, axis=0)
    attended = jnp.concatenate(all_attended, axis=0)
    owners_at = part_owners(nd)
    qkv_per, out_per = (-(-QKVW // (BC * nd)), -(-OUTW // (BC * nd)))

    def term_over_dp(left, right, per_index):
        size = per_index * BC
        right = jnp.pad(right, ((0, 0), (0, nd * size - right.shape[1])))
        terms = [
            dot_tn(left, lax.dynamic_slice(right, (0, index * size), (count, size)))
            for index in owners_at
        ]
        mine, away = (terms[: nd // 2], terms[nd // 2 :])
        away = jnp.concatenate(away, axis=0).astype(BF)
        return (scatter_sum_dp(jnp.concatenate(mine, axis=0), away, nd), away)

    out_sum, _ = term_over_dp(low_one, attended, out_per)
    left_root = after(root_left[0], low_one)
    left_pieces = pack_roots(left_root) if band > BC else [left_root]
    left_mine = [from_x(left) for left in left_pieces]
    left_here = [piece for mine in left_mine for piece in mine[1:]]

    low_mixed = dot_nn(after(low_one, down_band, *left_pieces), w_out).astype(BF).reshape(micros, rows, HEADS, HD)
    grad_queries, key_terms = [], []
    for m in range(micros):
        for_queries, for_keys, for_values = attend_back(
            query_low[m], keys_all[m], values_all[m], all_probs[m], low_mixed[m]
        )
        grad_queries.append(for_queries)
        terms = jnp.concatenate([for_keys, for_values], axis=1)
        key_terms.append(return_key_grads(terms, rows, nf))
        last = terms
    own_terms = after(jnp.concatenate(key_terms, axis=0), *left_here)
    grad_keys, grad_values = (own_terms[:, :HD], own_terms[:, HD:])

    def heads_only(query_in, key_in, query_scale, key_scale):
        return prepare_heads(query_in, key_in, query_scale, key_scale, cosine, sine)

    pull_heads = jax.vjp(heads_only, queries, keys, query_gain, key_gain)[1]
    grad_query_pre, grad_key_pre, grad_query_gain, grad_key_gain = pull_heads(
        (jnp.concatenate(grad_queries, axis=0), grad_keys)
    )
    low_projected = jnp.concatenate(
        [grad_query_pre.reshape(count, OUTW), grad_key_pre, grad_values], axis=1
    ).astype(BF)
    grad_normed = dot_nt(low_projected, w_qkv)
    grad_in, grad_pre_attn = jax.vjp(rms_gain, flat_in, pre_attn)[1](grad_normed)
    input_grad = (jnp.concatenate(grad_resids, axis=0) + grad_in).astype(BF)

    qkv_sum, qkv_away = term_over_dp(after(normed, both_band), low_projected, qkv_per)
    attn_sum = jnp.concatenate([qkv_sum, out_sum], axis=1).astype(BF)
    ff_all = gather_columns([after(both_band, qkv_sum), down_band])

    def all_parts(mine, *ties):
        parts = mine + [swap_core(piece, nd) for piece in mine]
        parts = [after(piece, *ties) for piece in parts]
        out = jnp.zeros((nd,) + parts[0].shape, BF)
        for place, piece in enumerate(parts):
            out = lax.dynamic_update_slice(out, piece[None], (place,) + (0,) * piece.ndim)
        return out.reshape((nd * capacity,) + out.shape[2:])

    right_roots = all_parts(right_mine, qkv_away)
    left_roots = [all_parts(mine, qkv_away) for mine in left_mine]

    def relative(index):
        nx = nd // 2
        flip = (index % 2) ^ core
        return flip * nx + (dp_me // 2 + nx - index // 2) % nx

    ff_index = np.arange(3 * FF_BLOCKS)
    ff_dp = np.minimum(ff_index % FF_BLOCKS // per, nd - 1)
    ff_column = ff_index % FF_BLOCKS - np.minimum(ff_dp * per, FF_BLOCKS - per)
    ff_column = ff_column + ff_index // FF_BLOCKS * per
    qkv_index, out_index = (np.arange(QKVW // BC), np.arange(OUTW // BC))
    attn_dp = np.concatenate([qkv_index // qkv_per, out_index // out_per])
    attn_column = np.concatenate([qkv_index % qkv_per, qkv_per + out_index % out_per])
    part_of = relative(
        jnp.asarray(np.concatenate([attn_dp, ff_dp]).astype(np.int32))
    )
    kind_of = jnp.asarray(
        np.zeros(NBLK).astype(np.int32)
    )
    column_of = jnp.asarray(np.concatenate([attn_column, ff_column]).astype(np.int32))

    owners = owner[:, 0]
    index = jnp.arange(NBLK, dtype=jnp.int32)
    before = (owners[:, None] == owners[None, :]) & (index[None, :] < index[:, None])
    ranks = jnp.sum(before.astype(jnp.int32), axis=1)
    my_slots = jnp.arange(capacity, dtype=jnp.int32)
    mine = (owners[None, :] == dp_me) & (ranks[None, :] == my_slots[:, None])
    used = jnp.sum(mine.astype(jnp.int32), axis=1)

    def of_slot(values):
        return jnp.sum(jnp.where(mine, values[None, :], 0), axis=1)

    is_attn = (index < ATTN_BLOCKS).astype(jnp.int32)
    places = (part_of, kind_of, column_of, is_attn)
    early = tuple(table[LATE:] for table in places)
    late = tuple(table[:LATE] for table in places)
    root_of = relative(owners) * capacity + ranks
    root_args = (left_roots, right_roots, master)
    slot_places = tuple(of_slot(table) for table in places)
    group = 3 if (capacity - LATE) % 3 == 0 else 1
    stat_args = (slot_places, used, stat_left[0], stat_right[0])
    fresh_stats = owner_stats([ff_all], *stat_args, LATE, capacity - LATE, group, None)
    attn_band = direct_reduce(after(attn_sum, both_band), nf, fresh_stats[0])
    attn_all = gather_relative([attn_band])
    fresh_arrays = update_blocks(
        [ff_all], early, root_of[LATE:], left_roots, right_roots, after(master, attn_band), LATE, NBLK - LATE, 7, None
    )
    both = [ff_all, attn_all]
    new_master, new_weights = update_blocks(
        both, late, root_of[:LATE], *root_args, 0, LATE, 7, fresh_arrays
    )
    slot_grads, new_left, new_right = owner_stats(both, *stat_args, 0, LATE, group, fresh_stats)

    post_attn_sum = sum(entry[0] for entry in gain_terms)
    pre_ffw_sum = sum(entry[1] for entry in gain_terms)
    post_ffw_sum = sum(entry[2] for entry in gain_terms)
    gain_sum = jnp.concatenate(
        [grad_pre_attn, post_attn_sum, pre_ffw_sum, post_ffw_sum, grad_query_gain, grad_key_gain]
    )
    gain_grad = sum_everywhere(after(gain_sum, attn_band), nd, nf)
    new_gain_stats = DECAY * gain_stats + (1.0 - DECAY) * gain_grad * gain_grad
    gain_change = -GAIN_RATE * gain_grad * lax.rsqrt(new_gain_stats)
    return (
        jnp.stack(outputs)[:, None],
        input_grad.reshape(micros, 1, rows, D),
        slot_grads[None],
        gain_grad,
        new_left[None],
        new_right[None],
        new_master,
        new_weights,
        new_gain_stats,
        gain_change,
    )


def solution(mesh):
    in_specs = (
        P(None, "dp", "fsdp", None),
        P(None, "dp", "fsdp", None),
        P(None, "dp", None),
        P("fsdp", None),
        P(),
        P(),
        P("fsdp", None),
        P("fsdp", "dp", None, None),
        P("fsdp", "dp", None, None),
        P("fsdp", "dp", None, None),
        P("fsdp", "dp", None, None),
    )
    out_specs = (
        P(None, "dp", "fsdp", None),
        P(None, "dp", "fsdp", None),
        P("fsdp", "dp", None, None),
        P(),
        P("fsdp", "dp", None, None),
        P("fsdp", "dp", None, None),
        P("fsdp", None),
        P("fsdp", None),
        P(),
        P(),
    )
    return jax.shard_map(local, mesh=mesh, in_specs=in_specs, out_specs=out_specs, check_vma=False)
```
